32 devices in a mesh: dp: 8 (over y, x, core), tensor: 4 (over z).
Axes of the slice: x: 2, y: 2, z: 4, core: 2. Of those that a mesh axis runs over, the one named last changes fastest.
Arguments:
- tokens: bfloat16 [16384, 768], P(('dp', 'tensor')), may hold values from -6 to 6
- starts: int32 [8, 8], P('dp'), may hold values from 0 to 2047, as said below
- w_qkv: bfloat16 [768, 2304], P(None, 'tensor'), may hold values from -0.21875 to 0.21875
- b_qkv: bfloat16 [2304], P('tensor'), may hold values from -3 to 3
- w_out: bfloat16 [768, 768], P('tensor'), may hold values from -2 to 2
- b_out: bfloat16 [768], replicated, may hold values from -3 to 3
- gain_one: bfloat16 [768], replicated, may hold values from 0.099609375 to 1.8984375
- shift_one: bfloat16 [768], replicated, may hold values from -3 to 3
- w_in: bfloat16 [768, 3072], P(None, 'tensor'), may hold values from -0.21875 to 0.21875
- b_in: bfloat16 [3072], P('tensor'), may hold values from -3 to 3
- w_two: bfloat16 [3072, 768], P('tensor'), may hold values from -0.21875 to 0.21875
- b_two: bfloat16 [768], replicated, may hold values from -3 to 3
- gain_two: bfloat16 [768], replicated, may hold values from 0.099609375 to 1.8984375
- shift_two: bfloat16 [768], replicated, may hold values from -3 to 3
- cotangent: bfloat16 [16384, 768], P(('dp', 'tensor')), may hold values from -6 to 6
Outputs:
- block_out: bfloat16 [16384, 768], P(('dp', 'tensor'))
- d_tokens: bfloat16 [16384, 768], P(('dp', 'tensor'))
- d_w_qkv: float32 [768, 2304], P(None, 'tensor')
- d_b_qkv: float32 [2304], P('tensor')
- d_w_out: float32 [768, 768], P('tensor')
- d_b_out: float32 [768], replicated
- d_gain_one: float32 [768], replicated
- d_shift_one: float32 [768], replicated
- d_w_in: float32 [768, 3072], P(None, 'tensor')
- d_b_in: float32 [3072], P('tensor')
- d_w_two: float32 [3072, 768], P('tensor')
- d_b_two: float32 [768], replicated
- d_gain_two: float32 [768], replicated
- d_shift_two: float32 [768], replicated
The draws below stay inside these ranges and needn't reach their ends.
Inputs may be any that keep to these rules, and one draw needn't show every extreme that they name: Each row holds exactly 8 documents: its first start is 0 and its starts rise strictly. In the first row the last document is a single token.
All inputs are finite; a program needn't handle non-finite values.
Results may differ from the reference program's by a relative error of at most 0.014.
Values may be sent and summed in bfloat16 or wider, within the bound.
No kernel may reach another device: no remote copies, remote signals or barrier semaphores. Data moves between devices by JAX's collectives and lax.ppermute only.
A program may use at most 192 MiB of HBM per device.

```python
import math
import jax
import jax.numpy as jnp
from jax import lax

D = 768
HEAD = 64
FF = 3072
GROUP = 64
ROW_LEN = 2048
DOCS = 8
ROWS = 8
TOKENS = 16384


def draw_starts(key, part):

    def one_row(subkey):
        picks = jax.random.permutation(subkey, ROW_LEN - 1)[:DOCS - 1] + 1
        return jnp.concatenate([jnp.zeros((1,), jnp.int32), jnp.sort(picks).astype(jnp.int32)])
    table = jax.vmap(one_row)(jax.random.split(jax.random.fold_in(key, 11), ROWS))
    return table.at[0, DOCS - 1].set(ROW_LEN - 1)


def levels(stream_key, shape, shards, least, largest):
    factor_of, own = 1.0, jax.random.fold_in(stream_key, 6)
    for dim, blocks in shards:
        heights = jnp.exp(jax.random.uniform(jax.random.fold_in(own, dim), (blocks,), jnp.float32, least / len(shards), largest / len(shards)))
        factor_of = factor_of * jnp.repeat(heights, shape[dim] // blocks).reshape([-1 if axis == dim else 1 for axis in range(len(shape))])
    return factor_of


def scatter_about(own_key, shape, scale, limit, cuts=(), kind=jnp.bfloat16):
    values = jax.random.normal(own_key, shape, jnp.float32) * scale
    if len(cuts) > 0:
        values = levels(own_key, shape, cuts, -0.22, 0.18) * values
    return jnp.clip(values, min=-limit, max=limit).astype(kind)


def setup_inputs(seed: int = 0) -> dict:
    splits = jax.random.split(jax.random.key(seed), 16)
    tokens = scatter_about(splits[0], (TOKENS, D), 1.0, 6.0, ((0, 32),))
    starts = draw_starts(jax.random.fold_in(splits[15], 71), 0)
    w_qkv = scatter_about(splits[2], (D, 3 * D), D ** -0.5, 0.21875, ((1, 4),))
    b_qkv = scatter_about(splits[3], (3 * D,), 0.5, 3.0, ((0, 4),))
    w_out = scatter_about(splits[4], (D, D), (max(D // 96, 1)) ** -0.5, 2.0, ((0, 4),))
    b_out = scatter_about(splits[5], (D,), 0.5, 3.0)
    gain_one = jnp.clip(1.0 + 0.18 * jax.random.normal(splits[6], (D,), jnp.float32), 0.099609375, 1.8984375).astype(jnp.bfloat16)
    shift_one = scatter_about(splits[7], (D,), 0.5, 3.0)
    w_in = scatter_about(splits[8], (D, FF), D ** -0.5, 0.21875, ((1, 4),))
    b_in = scatter_about(splits[9], (FF,), 0.5, 3.0, ((0, 4),))
    w_two = scatter_about(splits[10], (FF, D), (FF // 4) ** -0.5, 0.21875, ((0, 4),))
    b_two = scatter_about(splits[11], (D,), 0.5, 3.0)
    gain_two = jnp.clip(1.0 + 0.18 * jax.random.normal(splits[12], (D,), jnp.float32), 0.099609375, 1.8984375).astype(jnp.bfloat16)
    shift_two = scatter_about(splits[13], (D,), 0.5, 3.0)
    cotangent = scatter_about(splits[14], (TOKENS, D), 1.0, 6.0, ((0, 32),))
    return dict(tokens=tokens, starts=starts, w_qkv=w_qkv, b_qkv=b_qkv, w_out=w_out, b_out=b_out, gain_one=gain_one, shift_one=shift_one, w_in=w_in, b_in=b_in, w_two=w_two, b_two=b_two, gain_two=gain_two, shift_two=shift_two, cotangent=cotangent)


highest = lax.Precision.HIGHEST

@jax.custom_vjp
def low(v):
    return lax.optimization_barrier(v.astype(jnp.bfloat16)).astype(jnp.float32)

@jax.custom_vjp
def low_back(v):
    return v

def low_keep(v):
    return (low(v), None)

def low_pass(kept, grad):
    return (grad,)

def back_keep(v):
    return (v, None)

def back_low(kept, grad):
    return (low(grad),)
low.defvjp(low_keep, low_pass)
low_back.defvjp(back_keep, back_low)

def doc_tables(starts_row):
    places = jnp.arange(ROW_LEN, dtype=jnp.int32)
    started = (places[:, None] >= starts_row[None, :]).astype(jnp.int32)
    doc_ids = lax.optimization_barrier(jnp.sum(started, axis=1)) - 1
    onehot = (doc_ids[:, None] == jnp.arange(DOCS, dtype=jnp.int32)[None, :]).astype(jnp.int32)
    finish = jnp.concatenate([starts_row[1:], jnp.full((1,), ROW_LEN, jnp.int32)])
    own_start = lax.optimization_barrier(jnp.sum(onehot * starts_row[None, :], axis=1))
    own_len = lax.optimization_barrier(jnp.sum(onehot * (finish - starts_row)[None, :], axis=1))
    angles = 0.5 * math.pi * (places - own_start).astype(jnp.float32) / own_len.astype(jnp.float32)
    return (angles, doc_ids)

def attend(mixed, angles, doc_ids):
    length = mixed.shape[0]
    head_count = mixed.shape[1] // (3 * HEAD)
    blocks = length // GROUP
    pieces = mixed.reshape(blocks, GROUP, head_count, 3, HEAD)
    queries = jax.nn.relu(pieces[:, :, :, 0])
    key_pos = jax.nn.relu(pieces[:, :, :, 1])
    values = pieces[:, :, :, 2]
    cosine = jnp.cos(angles).reshape(blocks, GROUP, 1, 1)
    sines = jnp.sin(angles).reshape(blocks, GROUP, 1, 1)
    query_feat = jnp.concatenate([queries * cosine, queries * sines], axis=-1)
    key_feat = jnp.concatenate([key_pos * cosine, key_pos * sines], axis=-1)
    doc_blocks = doc_ids.reshape(blocks, GROUP)
    within = jnp.arange(GROUP, dtype=jnp.int32)
    inside_mask = ((doc_blocks[:, :, None] == doc_blocks[:, None, :]) & (within[None, :, None] >= within[None, None, :])).astype(jnp.float32)
    scores = jnp.einsum('bihf,bjhf->bhij', query_feat, key_feat, precision=highest) * inside_mask[:, None]
    numerator = jnp.einsum('bhij,bjhd->bihd', scores, values, precision=highest)
    denominator = jnp.transpose(lax.optimization_barrier(jnp.sum(scores, axis=-1)), (0, 2, 1))
    first_doc = doc_blocks[:, 0]
    last_doc = doc_blocks[:, -1]
    tail_mask = (doc_blocks == last_doc[:, None]).astype(jnp.float32)
    states = jnp.einsum('bjhf,bjhd,bj->bhfd', key_feat, values, tail_mask, precision=highest)
    key_sums = jnp.einsum('bjhf,bj->bhf', key_feat, tail_mask, precision=highest)
    order = jnp.arange(blocks, dtype=jnp.int32)
    link_mask = ((last_doc[None, :] == first_doc[:, None]) & (order[None, :] < order[:, None])).astype(jnp.float32)
    carried = jnp.einsum('cb,bhfd->chfd', link_mask, states, precision=highest)
    carried_sum = jnp.einsum('cb,bhf->chf', link_mask, key_sums, precision=highest)
    opening = (doc_blocks == first_doc[:, None]).astype(jnp.float32)
    numerator = numerator + jnp.einsum('bihf,bhfd,bi->bihd', query_feat, carried, opening, precision=highest)
    denominator = denominator + jnp.einsum('bihf,bhf,bi->bih', query_feat, carried_sum, opening, precision=highest)
    result = numerator / jnp.maximum(denominator, 1.0)[..., None]
    return result.reshape(length, head_count * HEAD)

def normalize(rows_in, gain, shift):
    centred = rows_in - lax.optimization_barrier(jnp.mean(rows_in, axis=-1, keepdims=True))
    spread = lax.optimization_barrier(jnp.mean(centred * centred, axis=-1, keepdims=True))
    return centred * lax.rsqrt(spread + 1e-05) * gain + shift

def forward_layer(token_row, params, angles, doc_ids):
    w_qkv, b_qkv, w_out, b_out, gain_one, shift_one, w_in, b_in, w_two, b_two, gain_two, shift_two = params
    mixed = low_back(jnp.dot(token_row, w_qkv, precision=highest) + b_qkv)
    attended = low(attend(mixed, angles, doc_ids))
    branch = low_back(jnp.dot(attended, w_out, precision=highest) + b_out)
    first_out = low(normalize(token_row + branch, gain_one, shift_one))
    hidden = low_back(jnp.dot(first_out, w_in, precision=highest) + b_in)
    active = low(jax.nn.gelu(hidden))
    second = low_back(jnp.dot(active, w_two, precision=highest) + b_two)
    return normalize(first_out + second, gain_two, shift_two)

def reference(tokens, starts, w_qkv, b_qkv, w_out, b_out, gain_one, shift_one, w_in, b_in, w_two, b_two, gain_two, shift_two, cotangent):
    params = tuple((weight.astype(jnp.float32) for weight in (w_qkv, b_qkv, w_out, b_out, gain_one, shift_one, w_in, b_in, w_two, b_two, gain_two, shift_two)))

    def one_row(running, sliced):
        token_row, back_row, starts_row = sliced
        angles, doc_ids = doc_tables(starts_row)

        def forward(row_in, weights):
            return forward_layer(row_in, weights, angles, doc_ids)
        result, pullback = jax.vjp(forward, token_row.astype(jnp.float32), params)
        d_row, d_weights = pullback(back_row.astype(jnp.float32))
        running = jax.tree.map(lambda first_val, second_val: first_val + second_val, running, d_weights)
        return (running, (result.astype(jnp.bfloat16), d_row.astype(jnp.bfloat16)))
    empty_grads = jax.tree.map(jnp.zeros_like, params)
    totals, (out_rows, grad_rows) = lax.scan(one_row, empty_grads, (tokens.reshape(ROWS, ROW_LEN, D), cotangent.reshape(ROWS, ROW_LEN, D), starts))
    return (out_rows.reshape(TOKENS, D), grad_rows.reshape(TOKENS, D), totals[0], totals[1], totals[2], totals[3], totals[4], totals[5], totals[6], totals[7], totals[8], totals[9], totals[10], totals[11])
```

```python
import functools
import math

import jax
import jax.numpy as jnp
from jax import lax
from jax.sharding import PartitionSpec as P

HEAD = 64
ROW_LEN = 2048
DOCS = 8
F32 = jnp.float32
BF16 = jnp.bfloat16


def dot(left, right, dims):
    return lax.dot_general(left, right, (dims, ((), ())), preferred_element_type=F32)


class Places:
    def __init__(self, dp, tensor):
        self.dp, self.tensor = dp, tensor
        self.row = lax.axis_index("dp")
        self.z = lax.axis_index("tensor")

    def bit(self, which):
        return (self.row >> which) & 1

    def swap(self, value, which):
        return lax.ppermute(value, "dp", [(d, d ^ (1 << which)) for d in range(self.dp)])

    def turn(self, value, step):
        size = self.tensor
        return lax.ppermute(value, "tensor", [(k, (k + step) % size) for k in range(size)])

    def onward(self, value, step):
        size = self.tensor
        pairs = [(k, k + step) for k in range(size) if 0 <= k + step < size]
        return lax.ppermute(value, "tensor", pairs)


def pair(own, other, bit):
    return jnp.where(bit == 0, jnp.stack([own, other]), jnp.stack([other, own]))


def gather_pieces(places, piece):
    parts = [piece] + [places.turn(piece, step) for step in range(1, places.tensor)]
    half = places.tensor // 2
    first, second = jnp.stack(parts[:half]), jnp.stack(parts[half:])
    first = pair(first, places.swap(first, 1), places.bit(1))
    second = pair(second, places.swap(second, 2), places.bit(2))
    first = pair(first, places.swap(first, 2), places.bit(2))
    second = pair(second, places.swap(second, 1), places.bit(1))
    first = pair(first, places.swap(first, 0), places.bit(0))
    second = pair(second, places.swap(second, 0), places.bit(0))
    second = jnp.swapaxes(second, 1, 2)
    return jnp.concatenate([first, second], axis=3)


def own_rows(places, weight):
    rows = weight.shape[0] // 8
    return lax.dynamic_slice_in_dim(weight, (places.row & 7) * rows, rows, 0)


def by_shard(pieces):
    ordered = jnp.transpose(pieces, (3, 1, 2, 0, 4, 5))
    return ordered.reshape(ordered.shape[0], -1, ordered.shape[-1])


def keep_and_send(value, bit, dim):
    kept = lax.dynamic_index_in_dim(value, bit, dim, keepdims=False)
    sent = lax.dynamic_index_in_dim(value, 1 - bit, dim, keepdims=False)
    return kept.astype(F32), sent.astype(BF16)


def reduce_pieces(places, grads, order):
    shards, rows, cols = grads.shape
    value = grads.reshape(shards, 2, 2, 2, rows // 8, cols)
    for which in (0,) + order:
        kept, sent = keep_and_send(value, places.bit(which), 1)
        value = kept + places.swap(sent, which).astype(F32)
    total = value[0]
    for step in range(1, shards):
        total = total + places.turn(value[step].astype(BF16), -step).astype(F32)
    for which in range(3, places.dp.bit_length() - 1):
        total = total + places.swap(total, which)
    low = total.astype(BF16)
    for which in order[::-1] + (0,):
        low = pair(low, places.swap(low, which), places.bit(which))
    return low.reshape(rows, cols).astype(F32)


def doc_tables(starts_row, places, count):
    spots = places.z * count + jnp.arange(count, dtype=jnp.int32)
    started = (spots[:, None] >= starts_row[None, :]).astype(jnp.int32)
    doc_ids = jnp.sum(started, axis=1) - 1
    onehot = (doc_ids[:, None] == jnp.arange(DOCS, dtype=jnp.int32)[None, :]).astype(jnp.int32)
    finish = jnp.concatenate([starts_row[1:], jnp.full((1,), ROW_LEN, jnp.int32)])
    own_start = jnp.sum(onehot * starts_row[None, :], axis=1)
    own_len = jnp.sum(onehot * (finish - starts_row)[None, :], axis=1)
    angles = 0.5 * math.pi * (spots - own_start).astype(F32) / own_len.astype(F32)
    return angles, doc_ids


def doc_at(starts_row, spot):
    return jnp.sum((spot >= starts_row).astype(jnp.int32)) - 1


def shift_shards(state, step):
    return jnp.roll(state, step, axis=0)


def norm_parts(rows_in):
    centred = rows_in - jnp.mean(rows_in, axis=-1, keepdims=True)
    spread = jnp.mean(centred * centred, axis=-1, keepdims=True)
    scale = lax.rsqrt(spread + 1e-05)
    return centred * scale, scale


def norm_back(grad, normed, scale, gain):
    e = grad * gain
    d_rows = scale * (
        e
        - jnp.mean(e, axis=-1, keepdims=True)
        - normed * jnp.mean(e * normed, axis=-1, keepdims=True)
    )
    return d_rows, jnp.sum(grad * normed, axis=0), jnp.sum(grad, axis=0)


def gelu_parts(v):
    k = math.sqrt(2 / math.pi)
    t = jnp.tanh(k * (v + 0.044715 * v * v * v))
    slope = 0.5 * (1 + t) + 0.5 * v * (1 - t * t) * k * (1 + 3 * 0.044715 * v * v)
    return 0.5 * v * (1 + t), slope


def on_device(dp, tensor, tokens, starts, w_qkv, b_qkv, w_out, b_out, gain_one, shift_one, w_in, b_in,
              w_two, b_two, gain_two, shift_two, cotangent):
    places = Places(dp, tensor)
    count = tokens.shape[0]
    width = tokens.shape[1]
    heads = w_qkv.shape[1] // (3 * HEAD)
    f = lambda a: a.astype(F32)
    qkv_all = by_shard(gather_pieces(places, own_rows(places, w_qkv)))
    rest = jnp.concatenate([own_rows(places, w_out), own_rows(places, w_in), own_rows(places, w_two)])
    rest_all = gather_pieces(places, rest)
    n_out, n_in = w_out.shape[0] // 8, w_in.shape[0] // 8
    out_all = by_shard(rest_all[..., :n_out, :])
    in_all = by_shard(rest_all[..., n_out:n_out + n_in, :])
    two_all = by_shard(rest_all[..., n_out + n_in:, :])
    biases = jnp.concatenate([b_qkv, b_in]).reshape(1, -1)
    bias_all = jnp.concatenate([biases] + [places.turn(biases, s) for s in range(1, tensor)])
    bias_qkv, bias_in = f(bias_all[:, :b_qkv.shape[0]]), f(bias_all[:, b_qkv.shape[0]:])

    row = starts[0]
    angles, docs = doc_tables(row, places, count)
    base = places.z * count
    first_doc, last_doc = doc_at(row, base), doc_at(row, base + count - 1)
    opening = (docs == first_doc).astype(F32)
    tail = (docs == last_doc).astype(F32)
    spot = jnp.arange(count)
    mask = jnp.where((docs[:, None] == docs[None, :]) & (spot[:, None] >= spot[None, :]),
                     jnp.cos(angles[:, None] - angles[None, :]), 0.0)
    cosine, sines = jnp.cos(angles)[:, None], jnp.sin(angles)[:, None]

    mixed = jnp.einsum("td,jdc->jtc", tokens, qkv_all, preferred_element_type=F32) + bias_qkv[:, None]
    parts = mixed.reshape(tensor, count, heads, 3, HEAD)
    query, key, value = (jnp.transpose(parts[:, :, :, i], (0, 2, 1, 3)) for i in range(3))
    query, key, value = jax.nn.relu(query).astype(BF16), jax.nn.relu(key).astype(BF16), value.astype(BF16)
    ones = jnp.ones(value.shape[:-1] + (1,), BF16)
    value_one = jnp.concatenate([value, ones], axis=-1)

    def feats(a, weight):
        return jnp.concatenate([f(a) * (cosine * weight), f(a) * (sines * weight)], axis=-1).astype(BF16)

    fq_open = feats(query, opening[:, None])
    fk_tail = feats(key, tail[:, None])
    state = jnp.einsum("jhtf,jhtv->jhfv", fk_tail, value_one, preferred_element_type=F32).astype(BF16)
    carried = jnp.zeros(state.shape, F32)
    for step in range(1, tensor):
        link = (doc_at(row, base - (step - 1) * count - 1) == first_doc).astype(F32)
        carried = carried + link * f(shift_shards(places.onward(state, step), step))
    carried = carried.astype(BF16)
    scores = jnp.einsum("jhtf,jhsf->jhts", query, key, preferred_element_type=F32) * mask
    scores = scores.astype(BF16)
    sums = jnp.einsum("jhts,jhsv->jhtv", scores, value_one, preferred_element_type=F32) + jnp.einsum(
        "jhtf,jhfv->jhtv", fq_open, carried, preferred_element_type=F32)
    den_raw = sums[..., HEAD:]
    den = jnp.maximum(den_raw, 1.0)
    o = sums[..., :HEAD] / den
    attended = jnp.transpose(o, (2, 0, 1, 3)).reshape(count, width).astype(BF16)
    w_out_full = out_all.reshape(width, width)
    r1 = f(tokens) + dot(attended, w_out_full, ((1,), (0,))) + f(b_out)
    n1, s1 = norm_parts(r1)
    first = (n1 * f(gain_one) + f(shift_one)).astype(BF16)
    hidden = jnp.einsum("td,jdc->jtc", first, in_all, preferred_element_type=F32) + bias_in[:, None]
    act, slope = gelu_parts(hidden)
    act = act.astype(BF16)
    second = jnp.einsum("jtc,jcd->td", act, two_all, preferred_element_type=F32) + f(b_two)
    n2, s2 = norm_parts(f(first) + second)
    block_out = (n2 * f(gain_two) + f(shift_two)).astype(BF16)

    d_r2, d_gain_two, d_shift_two = norm_back(f(cotangent), n2, s2, f(gain_two))
    d_second = d_r2.astype(BF16)
    d_b_two = jnp.sum(f(d_second), axis=0)
    g_two = jnp.einsum("td,jtc->jdc", d_second, act, preferred_element_type=F32)
    d_w_two = reduce_pieces(places, g_two, (1, 2)).T
    d_hidden = (jnp.einsum("td,jcd->jtc", d_second, two_all, preferred_element_type=F32) * slope).astype(BF16)
    d_b_in = jnp.sum(f(d_hidden), axis=1)
    g_in = jnp.einsum("td,jtc->jdc", first, d_hidden, preferred_element_type=F32)
    d_w_in = reduce_pieces(places, g_in, (2, 1))
    d_first = jnp.einsum("jtc,jdc->td", d_hidden, in_all, preferred_element_type=F32) + d_r2
    d_r1, d_gain_one, d_shift_one = norm_back(d_first, n1, s1, f(gain_one))
    d_branch = d_r1.astype(BF16)
    d_b_out = jnp.sum(f(d_branch), axis=0)
    g_out = dot(attended, d_branch, ((0,), (0,))).reshape(tensor, -1, width)
    d_w_out = reduce_pieces(places, g_out, (1, 2))
    g = dot(d_branch, w_out_full, ((1,), (1,))).reshape(count, tensor, heads, HEAD)
    g = jnp.transpose(g, (1, 2, 0, 3))
    d_num = g / den
    d_den = jnp.where(den_raw > 1.0, -jnp.sum(g * o, axis=-1, keepdims=True) / den, 0.0)
    d_sums = jnp.concatenate([d_num, d_den], axis=-1).astype(BF16)
    d_carried = jnp.einsum("jhtf,jhtv->jhfv", fq_open, d_sums, preferred_element_type=F32).astype(BF16)
    d_state = jnp.zeros(state.shape, F32)
    for step in range(1, tensor):
        link = (doc_at(row, base + step * count) == last_doc).astype(F32)
        d_state = d_state + link * f(shift_shards(places.onward(d_carried, -step), -step))
    d_state = d_state.astype(BF16)
    d_scores = (jnp.einsum("jhtv,jhsv->jhts", d_sums, value_one, preferred_element_type=F32) * mask).astype(BF16)
    d_fq = jnp.einsum("jhtv,jhfv->jhtf", d_sums, carried, preferred_element_type=F32) * opening[:, None]
    d_query = jnp.einsum("jhts,jhsf->jhtf", d_scores, key, preferred_element_type=F32) + (
        d_fq[..., :HEAD] * cosine + d_fq[..., HEAD:] * sines)
    d_fk = jnp.einsum("jhtv,jhfv->jhtf", value_one, d_state, preferred_element_type=F32) * tail[:, None]
    d_key = jnp.einsum("jhts,jhtf->jhsf", d_scores, query, preferred_element_type=F32) + (
        d_fk[..., :HEAD] * cosine + d_fk[..., HEAD:] * sines)
    d_value = jnp.einsum("jhts,jhtv->jhsv", scores, d_sums[..., :HEAD], preferred_element_type=F32) + jnp.einsum(
        "jhtf,jhfv->jhtv", fk_tail, d_state[..., :HEAD], preferred_element_type=F32)
    d_query = jnp.where(query > 0, d_query, 0.0)
    d_key = jnp.where(key > 0, d_key, 0.0)
    d_mixed = jnp.stack([d_query, d_key, d_value], axis=3).astype(BF16)
    d_mixed = jnp.transpose(d_mixed, (0, 2, 1, 3, 4)).reshape(tensor, count, -1)
    d_b_qkv = jnp.sum(f(d_mixed), axis=1)
    g_qkv = jnp.einsum("td,jtc->jdc", tokens, d_mixed, preferred_element_type=F32)
    d_w_qkv = reduce_pieces(places, g_qkv, (2, 1))
    d_tokens = (jnp.einsum("jtc,jdc->td", d_mixed, qkv_all, preferred_element_type=F32) + d_r1).astype(BF16)

    shared = jnp.concatenate([d_b_out, d_gain_one, d_shift_one, d_b_two, d_gain_two, d_shift_two])
    split = jnp.concatenate([d_b_qkv, d_b_in], axis=1)
    turned = jnp.concatenate([split[::-1], split[::-1]])
    split = lax.dynamic_slice_in_dim(turned, tensor - 1 - places.z, tensor, 0)
    summed = lax.psum(jnp.concatenate([shared, split.reshape(-1)]), ("dp", "tensor"))
    d_b_out, d_gain_one, d_shift_one, d_b_two, d_gain_two, d_shift_two = jnp.split(summed[:6 * width], 6)
    split = lax.dynamic_index_in_dim(summed[6 * width:].reshape(tensor, -1), places.z, 0, keepdims=False)
    d_b_qkv, d_b_in = split[:b_qkv.shape[0]], split[b_qkv.shape[0]:]
    return (block_out, d_tokens, d_w_qkv, d_b_qkv, d_w_out, d_b_out, d_gain_one, d_shift_one, d_w_in, d_b_in,
            d_w_two, d_b_two, d_gain_two, d_shift_two)


def solution(mesh):
    sizes = dict(mesh.shape)
    rows = P(("dp", "tensor"), None)
    wide, tall, cut, whole = P(None, "tensor"), P("tensor", None), P("tensor"), P()
    in_specs = (rows, P("dp", None), wide, cut, tall, whole, whole, whole, wide, cut, tall, whole, whole, whole, rows)
    out_specs = (rows, rows, wide, cut, tall, whole, whole, whole, wide, cut, tall, whole, whole, whole)
    return jax.shard_map(
        functools.partial(on_device, sizes["dp"], sizes["tensor"]),
        mesh=mesh, in_specs=in_specs, out_specs=out_specs, check_vma=False,
    )
```

```python
import functools
import math

import jax
import jax.numpy as jnp
from jax import lax
from jax.experimental import pallas as pl
from jax.experimental.pallas import tpu as pltpu
from jax.sharding import PartitionSpec as P

HEAD = 64
ROW_LEN = 2048
DOCS = 8
F32 = jnp.float32
BF16 = jnp.bfloat16
NN = ((1,), (0,))
NT = ((1,), (1,))
TN = ((0,), (0,))
STATE = 80
COST = 0.2 * 1.15e9
VMEM = pl.BlockSpec(memory_space=pltpu.VMEM)
SMEM = pl.BlockSpec(memory_space=pltpu.SMEM)
ANY = pl.BlockSpec(memory_space=pl.ANY)


def dot(left, right, dims=NN):
    return lax.dot_general(left, right, (dims, ((), ())), preferred_element_type=F32)


def call(body, outs, specs, scratch=(), limit=48, after=(), cost=0):
    n = len(specs)

    def waiting_body(*refs):
        body(*refs[:n], *refs[n + len(after):])

    return lambda *operands: pl.pallas_call(
        waiting_body,
        out_shape=outs,
        in_specs=list(specs) + [ANY] * len(after),
        out_specs=jax.tree.map(lambda _: VMEM, outs),
        scratch_shapes=scratch,
        cost_estimate=pl.CostEstimate(flops=1 + int(cost * COST), bytes_accessed=1, transcendentals=0),
        compiler_params=pltpu.CompilerParams(vmem_limit_bytes=limit << 20),
    )(*operands, *after)


def shaped(shape, dtype):
    return jax.ShapeDtypeStruct(shape, dtype)


class Places:
    def __init__(self, dp, tensor):
        self.dp, self.tensor = dp, tensor
        self.row = lax.axis_index("dp")
        self.z = lax.axis_index("tensor")
        self.piece = self.row & 7

    def swap(self, value, mask):
        return lax.ppermute(value, "dp", [(d, d ^ mask) for d in range(self.dp)])

    def turn(self, value, step):
        size = self.tensor
        return lax.ppermute(value, "tensor", [(k, (k + step) % size) for k in range(size)])

    def onward(self, value, step):
        size = self.tensor
        pairs = [(k, k + step) for k in range(size) if 0 <= k + step < size]
        return lax.ppermute(value, "tensor", pairs)


CORE, X, Y = 1, 2, 4
BUFFERS = ((0, (0, 2)), (0, (4, 6)), (0, (1, 3)), (0, (5, 7)), (2, (0, 4)), (2, (2, 6)), (2, (1, 5)), (2, (3, 7)))


def stacked(*groups, after=()):
    sizes = [len(group) for group in groups]

    def body(*refs):
        sources, targets = list(refs[:sum(sizes)]), refs[sum(sizes):]
        for size, target in zip(sizes, targets, strict=True):
            for k in range(size):
                target[k] = sources.pop(0)[...]

    outs = tuple(shaped((len(group),) + group[0].shape, group[0].dtype) for group in groups)
    flat = [value for group in groups for value in group]
    return call(body, outs, [VMEM] * len(flat), after=after)(*flat)


def mix_pieces_kernel(first, second, third, fourth, a, b, bias_qkv, bias_in):
    rows, wide = a.shape[1], bias_qkv.shape[2]
    for j, part in enumerate((first, second, third, fourth)):
        (a, b)[j // 2][j % 2] = part[0:rows]
        extra = part[rows:].astype(F32)
        bias_qkv[j] = extra[0:1, :wide]
        bias_in[j] = extra[1:2]


def swap_halves(places, a, b):
    return places.swap(a, X), places.swap(b, Y)


def gather_rest(places, a, b, a2, b2):
    near, far = stacked((a, b)), stacked((a2, b2))
    return a, a2, b, b2, places.swap(near[0], CORE), places.swap(far[0], CORE)


def start_placing(piece, buffers, targets, sems):
    copies = []
    a, a2, b, b2, near, far = buffers
    buffers = (a, a2, near.at[0], far.at[0], b, b2, near.at[1], far.at[1])
    for buffer, (shard, pieces) in zip(buffers, BUFFERS, strict=True):
        for k, other in enumerate(pieces):
            for at, target, first_row, rows in targets:
                spot = pl.multiple_of(first_row + (piece ^ other) * rows, 8)
                copies.append(pltpu.make_async_copy(
                    buffer.at[k, :, at:at + rows, :],
                    target.at[shard:shard + 2, pl.ds(spot, rows), :],
                    sems.at[len(copies)],
                ))
    for copy in copies:
        copy.start()
    half = len(copies) // 2
    return copies[:half], copies[half:]


def wait_all(copies):
    for copy in copies:
        copy.wait()


def doubled(part):
    return jnp.concatenate([part, part], axis=1)


def with_one(value):
    lanes = lax.broadcasted_iota(jnp.int32, (value.shape[0], 2 * HEAD), 1)
    return jnp.where(lanes < HEAD, doubled(value.astype(F32)), (lanes == HEAD).astype(F32)).astype(BF16)


def head_parts(mixed_ref, shard, head):
    at = head * 3 * HEAD
    return tuple(mixed_ref[shard, :, at + t * HEAD:at + (t + 1) * HEAD] for t in range(3))


def causal_blocks(count):
    half = count // 2
    return ((0, half, 0, half), (half, count, 0, count))


def mix_kernel(info, tokens, bias, key_table, *refs):
    buffers, (mixed_out, state_out, weight), sems = refs[:6], refs[6:9], refs[9]
    wide = mixed_out.shape[2]
    tall = weight.shape[1] - wide
    halves = start_placing(
        info[0], buffers, ((0, weight, 0, wide // 8), (wide // 8, weight, wide, tall // 8)), sems)

    def shard_step(j, carry):
        mixed = dot(tokens[...], weight[j, 0:wide], NT) + bias[j]
        lanes = lax.broadcasted_iota(jnp.int32, mixed.shape, 1)
        mixed_out[j] = jnp.where(lanes % 192 >= 128, mixed, jnp.maximum(mixed, 0.0)).astype(BF16)
        for h in range(3):
            _, key, value = head_parts(mixed_out, j, h)
            feats = (doubled(key).astype(F32) * key_table[...]).astype(BF16)
            state_out[j, h] = dot(with_one(value), feats, TN)[:STATE].astype(BF16)
        return carry

    for k, half in enumerate(halves):
        wait_all(half)
        lax.fori_loop(2 * k, 2 * k + 2, shard_step, 0)


def local_kernel(mixed, mask, sums_out):
    def shard_step(j, carry):
        for h in range(3):
            query, key, value = head_parts(mixed, j, h)
            value = with_one(value)
            for r0, r1, c0, c1 in causal_blocks(mask.shape[0]):
                scores = (dot(query[r0:r1], key[c0:c1], NT) * mask[r0:r1, c0:c1]).astype(BF16)
                sums_out[j, h, r0:r1] = dot(scores, value[c0:c1])
        return carry

    lax.fori_loop(0, mixed.shape[0], shard_step, 0)


def norm_parts(rows_in):
    centred = rows_in - jnp.mean(rows_in, axis=-1, keepdims=True)
    spread = jnp.mean(centred * centred, axis=-1, keepdims=True)
    scale = lax.rsqrt(spread + 1e-05)
    return centred * scale, scale


def norm_back(grad, normed, scale, gain):
    e = grad * gain
    d_rows = scale * (
        e
        - jnp.mean(e, axis=-1, keepdims=True)
        - normed * jnp.mean(e * normed, axis=-1, keepdims=True)
    )
    return d_rows, jnp.sum(grad * normed, axis=0, keepdims=True), jnp.sum(grad, axis=0, keepdims=True)


def join_kernel(info, sums, arrived1, arrived2, arrived3, mixed, query_table, tokens, weight, b_out, gain, shift,
                attended, carried, dens, first, normed_out, scale_out):
    shards = mixed.shape[0]
    for j in range(shards):
        total = None
        for step, arrived in enumerate((arrived1, arrived2, arrived3), 1):
            linked = info[step].astype(F32) * arrived[(j - step) % shards].astype(F32)
            total = linked if total is None else total + linked
        carried[j] = total.astype(BF16)

    def shard_step(j, branch):
        lanes = lax.broadcasted_iota(jnp.int32, (tokens.shape[0], 128), 1)
        kept = jnp.zeros((tokens.shape[0], 128), F32)
        for h in range(3):
            query = head_parts(mixed, j, h)[0]
            feats = (doubled(query).astype(F32) * query_table[...]).astype(BF16)
            total = sums[j, h][:, :STATE] + dot(feats, carried[j, h], NT)
            den = total[:, HEAD:HEAD + 1]
            inverse = 1.0 / jnp.maximum(den, 1.0)
            attended[j, :, h * HEAD:(h + 1) * HEAD] = (total[:, :HEAD] * inverse).astype(BF16)
            kept = jnp.where(lanes == h, inverse, kept)
            kept = jnp.where(lanes == 8 + h, jnp.where(den > 1.0, inverse, 0.0), kept)
        dens[j] = kept
        return branch + dot(attended[j], weight[j, weight.shape[1] - 192:])

    branch = lax.fori_loop(0, shards, shard_step, jnp.zeros(tokens.shape, F32))
    normed, scale = norm_parts(tokens[...].astype(F32) + branch + b_out[...])
    normed_out[...] = normed
    scale_out[...] = jnp.broadcast_to(scale, scale_out.shape)
    first[...] = (normed * gain[...] + shift[...]).astype(BF16)


def gelu_parts(v):
    k = math.sqrt(2 / math.pi)
    square = v * v
    t = jnp.tanh(v * (k + k * 0.044715 * square))
    half = 0.5 * v
    bent = half * t
    slope = (0.5 + 0.5 * t) + (half - bent * t) * (k + 3 * k * 0.044715 * square)
    return half + bent, slope


def rows_ordered(turned, piece, order):
    rows = turned.shape[0] // 8
    return jnp.concatenate(
        [turned[pl.ds(pl.multiple_of((piece ^ other) * rows, rows), rows), :] for other in order], axis=0)


ROUTES = ((0, 4, 2, 6), (0, 2, 4, 6))


def weight_grad(turned, piece, route, sends, right):
    order = tuple(other + sends for other in ROUTES[route])
    return dot(rows_ordered(turned, piece, order), right).astype(BF16)


def feed_kernel(info, first, bias, b_two, gain, shift, cotangent, *refs):
    buffers = refs[:6]
    active, slope, block_out, d_second_out, d_r2_out, vectors, *grads = refs[6:14]
    w_in, w_two, turned, total, sems = refs[14:]
    shards, width = w_in.shape[0], w_in.shape[2]
    rows = width // 8
    halves = start_placing(info[0], buffers, ((0, w_in, 0, rows), (rows, w_two, 0, rows)), sems)
    total[...] = jnp.broadcast_to(b_two[...], total.shape)

    def forward_step(j, carry):
        act, bend = gelu_parts(dot(first[...], w_in[j]) + bias[j])
        active[j] = act.astype(BF16)
        slope[j] = bend.astype(BF16)
        total[...] += dot(active[j], w_two[j])
        return carry

    for k, half in enumerate(halves):
        wait_all(half)
        lax.fori_loop(2 * k, 2 * k + 2, forward_step, 0)
    normed, scale = norm_parts(first[...].astype(F32) + total[...])
    block_out[...] = (normed * gain[...] + shift[...]).astype(BF16)
    d_r2, d_gain, d_shift = norm_back(cotangent[...].astype(F32), normed, scale, gain[...])
    d_r2_out[...] = d_r2
    d_second = d_r2.astype(BF16)
    d_second_out[...] = d_second
    turned[...] = d_second.T
    vectors[0:1] = d_gain
    vectors[1:2] = d_shift
    vectors[2:3] = jnp.sum(d_second.astype(F32), axis=0, keepdims=True)
    vectors[3:] = jnp.zeros((5, vectors.shape[1]), F32)
    for j in range(shards):
        for sends in (1, 0):
            grads[sends][:, j * width:(j + 1) * width] = weight_grad(turned, info[0], j // 2, sends, active[j])


def feed_back_kernel(info, first, d_second, slope, *refs):
    buffers = refs[:6]
    d_hidden, d_bias, *grads = refs[6:10]
    w_two, turned, sems = refs[10:]
    shards, width = w_two.shape[0], w_two.shape[2]
    rows = width // 8
    halves = start_placing(info[0], buffers, ((rows, w_two, 0, rows),), sems)
    turned[...] = first[...].T
    for j in range(shards):
        if j % 2 == 0:
            wait_all(halves[j // 2])
        d_active = dot(d_second[...], w_two[j], NT)
        d_h = (d_active * slope[j].astype(F32)).astype(BF16)
        d_hidden[j] = d_h
        d_bias[j] = jnp.broadcast_to(jnp.sum(d_h.astype(F32), axis=0, keepdims=True), d_bias.shape[1:])
        for sends in (1, 0):
            grads[sends][:, j * width:(j + 1) * width] = weight_grad(turned, info[0], j // 2, sends, d_hidden[j])


def first_back_kernel(info, d_hidden, d_r2, normed, scale, gain, *refs):
    buffers = refs[:6]
    d_r1_out, d_branch_out, vectors = refs[6:9]
    w_in, total, sems = refs[9:]
    rows = w_in.shape[1] // 8
    halves = start_placing(info[0], buffers, ((0, w_in, 0, rows),), sems)
    total[...] = d_r2[...]

    def first_step(j, carry):
        total[...] += dot(d_hidden[j], w_in[j], NT)
        return carry

    for k, half in enumerate(halves):
        wait_all(half)
        lax.fori_loop(2 * k, 2 * k + 2, first_step, 0)
    d_r1, d_gain, d_shift = norm_back(total[...], normed[...], scale[:, 0:1], gain[...])
    d_r1_out[...] = d_r1
    d_branch = d_r1.astype(BF16)
    d_branch_out[...] = d_branch
    vectors[0:1] = d_gain
    vectors[1:2] = d_shift
    vectors[2:3] = jnp.sum(d_branch.astype(F32), axis=0, keepdims=True)
    vectors[3:] = jnp.zeros((5, vectors.shape[1]), F32)


def heads_back_kernel(d_branch, weight, attended, dens, mixed, query_table, d_sums, d_carried):
    def shard_step(j, carry):
        g_all = dot(d_branch[...], weight[j, weight.shape[1] - 192:], NT)
        lanes = lax.broadcasted_iota(jnp.int32, (d_branch.shape[0], 128), 1)
        for h in range(3):
            g = g_all[:, h * HEAD:(h + 1) * HEAD]
            o = attended[j, :, h * HEAD:(h + 1) * HEAD].astype(F32)
            inverse, inverse_if = dens[j, :, h:h + 1], dens[j, :, 8 + h:9 + h]
            d_den = -jnp.sum(g * o, axis=-1, keepdims=True) * inverse_if
            d_num = doubled(g * inverse)
            both = jnp.where(lanes < HEAD, d_num, jnp.where(lanes == HEAD, d_den, 0.0)).astype(BF16)
            d_sums[j, h] = both
            query = head_parts(mixed, j, h)[0]
            feats = (doubled(query).astype(F32) * query_table[...]).astype(BF16)
            d_carried[j, h] = dot(both, feats, TN)[:STATE].astype(BF16)
        return carry

    lax.fori_loop(0, mixed.shape[0], shard_step, 0)


def local_back_kernel(mixed, d_sums, mask, mask_t, d_mixed):
    def shard_step(j, carry):
        for h in range(3):
            query, key, value = head_parts(mixed, j, h)
            value = with_one(value)
            grad = d_sums[j, h]
            at = h * 3 * HEAD
            for r0, r1, c0, c1 in causal_blocks(mask.shape[0]):
                d_scores = (dot(grad[r0:r1], value[c0:c1], NT) * mask[r0:r1, c0:c1]).astype(BF16)
                d_mixed[j, r0:r1, at:at + HEAD] = dot(d_scores, key[c0:c1])
            half = mask.shape[0] // 2
            for c0, c1, r0 in ((0, half, 0), (half, 2 * half, half)):
                turned = mask_t[c0:c1, r0:]
                d_scores = (dot(value[c0:c1], grad[r0:], NT) * turned).astype(BF16)
                d_mixed[j, c0:c1, at + HEAD:at + 2 * HEAD] = dot(d_scores, query[r0:])
                scores = (dot(key[c0:c1], query[r0:], NT) * turned).astype(BF16)
                d_mixed[j, c0:c1, at + 2 * HEAD:at + 3 * HEAD] = dot(scores, grad[r0:])[:, :HEAD]
        return carry

    lax.fori_loop(0, mixed.shape[0], shard_step, 0)


def mix_back_kernel(base, info, mixed, local, d_sums, carried, arrived1, arrived2, arrived3, query_table, key_table,
                    tokens, attended, d_branch, *refs):
    last = base > 0
    sources, refs = (refs[:4], refs[4:]) if last else ((), refs)
    d_mixed, d_bias, *grads = refs[:4]
    turned, turned_branch, state, held, middles = refs[-5:]
    shards, wide = mixed.shape[0], mixed.shape[2]
    width = d_mixed.shape[2]
    turned[...] = tokens[...].T
    turned_branch[...] = d_branch[...].T
    for k in range(2):
        total = None
        for step, arrived in enumerate((arrived1, arrived2, arrived3), 1):
            linked = info[3 + step].astype(F32) * arrived[(base + k + step) % shards].astype(F32)
            total = linked if total is None else total + linked
        state[k] = total.astype(BF16)

    def folded(both):
        return both[:, :HEAD] + both[:, HEAD:]

    def shard_step(k, carry):
        j = base + k
        parts = []
        for h in range(3):
            query, key, value = head_parts(mixed, j, h)
            at = h * 3 * HEAD
            spans = [slice(at + t * HEAD, at + (t + 1) * HEAD) for t in range(3)]
            d_query = folded(dot(d_sums[j, h][:, :STATE], carried[j, h]) * query_table[...])
            d_query = jnp.where(query.astype(F32) > 0, local[j, :, spans[0]] + d_query, 0.0)
            d_key = folded(dot(with_one(value)[:, :STATE], state[k, h]) * key_table[...])
            d_key = jnp.where(key.astype(F32) > 0, local[j, :, spans[1]] + d_key, 0.0)
            feats = (doubled(key).astype(F32) * key_table[...]).astype(BF16)
            d_value = local[j, :, spans[2]] + dot(feats, state[k, h], NT)[:, :HEAD]
            parts += [d_query, d_key, d_value]
        whole = jnp.concatenate(parts + [attended[j].astype(F32)], axis=1).astype(BF16)
        d_mixed[k] = whole
        middles[k] = jnp.concatenate([parts[-1], attended[j][:, :HEAD].astype(F32)], axis=1)
        d_bias[k] = jnp.broadcast_to(jnp.sum(d_mixed[k].astype(F32), axis=0, keepdims=True), d_bias.shape[1:])
        return carry

    lax.fori_loop(0, 2, shard_step, 0)
    rows = grads[0].shape[0]
    low = wide // 128 * 128
    for k in range(2):
        lanes = lax.broadcasted_iota(jnp.int32, (d_mixed.shape[1], 128), 1)
        middle = middles[k]
        left_side = jnp.where(lanes < HEAD, middle, 0.0).astype(BF16)
        right_side = jnp.where(lanes < HEAD, 0.0, middle).astype(BF16)
        left_side = jnp.concatenate([d_mixed[k][:, :low], left_side], axis=1)
        right_side = jnp.concatenate([right_side, d_mixed[k][:, low + 128:]], axis=1)
        for sends in (1, 0):
            out, at = grads[sends], k * width
            order = tuple(other + sends for other in ROUTES[k])
            left = dot(rows_ordered(turned, info[0], order), left_side)
            right = dot(rows_ordered(turned_branch, info[0], order), right_side)
            out[0:rows, at:at + low] = left[:, :low].astype(BF16)
            out[0:rows, at + low:at + low + 128] = (left[:, low:] + right[:, :128]).astype(BF16)
            out[0:rows, at + low + 128:at + width] = right[:, 128:].astype(BF16)
    if last:
        one, two, bias_in, bias_first = sources
        vectors = refs[4]
        held[0:3] = one[0:3]
        held[3:6] = two[0:3]
        for j in range(shards):
            held[6 + 2 * j:7 + 2 * j] = bias_first[j, 0:1] if j < 2 else d_bias[j - 2, 0:1]
            held[7 + 2 * j:8 + 2 * j] = bias_in[j, 0:1]
        held[14:16] = jnp.zeros((2, width), F32)
        low_rows = held[...].astype(BF16)
        vectors[...] = low_rows
        grads[1][rows:, 0:width] = low_rows[0:8]
        grads[1][rows:, width:] = low_rows[8:16]


def tokens_back_kernel(d_mixed_a, d_mixed_b, weight, d_r1, d_tokens):
    wide = weight.shape[1] - 192
    total = d_r1[...]
    for j in range(weight.shape[0]):
        d_mixed = (d_mixed_a, d_mixed_b)[j // 2]
        total = total + dot(d_mixed[j % 2][:, :wide], weight[j, 0:wide])
    d_tokens[...] = total.astype(BF16)


def later(values, others):
    return lax.optimization_barrier((values, others))[0]


def halves_like(rows, width, extra=0):
    keep, send = shaped((rows, width), F32), shaped((rows, width), BF16)
    return keep, send, keep, shaped((rows + extra, width), BF16)


def first_halves_kernel(keep, got, *outs):
    half, width = outs[0].shape
    for k in range(2):
        cols = slice(k * width, (k + 1) * width)
        outs[2 * k][...] = keep[0:half, cols].astype(F32) + got[0:half, cols].astype(F32)
        send = keep[half:2 * half, cols].astype(F32) + got[half:2 * half, cols].astype(F32)
        outs[2 * k + 1][0:half] = send.astype(BF16)


def first_halves_rows_kernel(keep, got, mine, *outs):
    first_halves_kernel(keep, got, *outs[:4])
    half, width = outs[0].shape
    for k in range(2):
        spots = slice(8 * k, 8 * k + 8)
        rows = mine[spots].astype(F32) + got[4 * half // 2:, k * width:(k + 1) * width].astype(F32)
        outs[4][spots] = rows.astype(BF16)
        outs[3][half + 8 * k:half + 8 * k + 8] = rows.astype(BF16)


def next_halves_kernel(keep0, keep1, got0, got1, *outs):
    half = outs[0].shape[0]
    for k, (keep, got) in enumerate(((keep0, got0), (keep1, got1))):
        outs[2 * k][...] = keep[0:half] + got[0:half].astype(F32)
        outs[2 * k + 1][...] = (keep[half:] + got[half:].astype(F32)).astype(BF16)


def ends_kernel(keep0, keep1, got0, got1, end0, end1):
    end0[...] = (keep0[...] + got0[...].astype(F32)).astype(BF16)
    end1[...] = (keep1[...] + got1[...].astype(F32)).astype(BF16)


def feed_last_kernel(keep0, keep1, got0, got1, two0, two1, *outs):
    rows, width = outs[0].shape[0] // 2, outs[0].shape[1]
    for j, out in enumerate(outs):
        keep, got, two = (keep0, got0, two0) if j < 2 else (keep1, got1, two1)
        cols = slice(j % 2 * width, (j % 2 + 1) * width)
        out[0:rows] = (keep[:, cols] + got[:, cols].astype(F32)).astype(BF16)
        out[rows:] = two[:, cols]


def mix_next_kernel(a0, send_a0, a1, send_a1, b0, b1, got0, got1, mine, keep0, send0, keep1, send1, rows_out):
    half = a0.shape[0]
    for a, send_a, b, got, keep, send in ((a0, send_a0, b0, got0, keep0, send0), (a1, send_a1, b1, got1, keep1, send1)):
        keep[0:half] = a[...]
        keep[half:] = b[0:half] + got[0:half].astype(F32)
        send[0:half] = send_a[...]
        send[half:2 * half] = (b[half:] + got[half:2 * half].astype(F32)).astype(BF16)
    rows = (mine[...].astype(F32) + got1[2 * half:].astype(F32)).astype(BF16)
    rows_out[...] = rows
    send1[2 * half:] = rows


def mix_last_kernel(keep0, keep1, got0, got1, mine, *outs):
    half = keep0.shape[0] // 2
    rows = (mine[...].astype(F32) + got1[2 * half:].astype(F32)).astype(BF16)
    for j, out in enumerate(outs):
        keep, got = (keep0, got0) if j % 2 == 0 else (keep1, got1)
        spots = slice(j // 2 * half, (j // 2 + 1) * half)
        out[0:half] = (keep[spots] + got[spots].astype(F32)).astype(BF16)
        out[half:half + 6] = rows[0:6]
        out[half + 6:half + 8] = rows[6 + 2 * j:8 + 2 * j]


def swap_all(places, values, masks):
    return [places.swap(value, mask) for value, mask in zip(values, masks, strict=True)]


def turn_back(places, parts):
    return [parts[0]] + [places.turn(parts[s], -s) for s in range(1, places.tensor)]


def pair_sum(mine, other):
    return (mine.astype(F32) + other.astype(F32)).astype(BF16)


def over_groups(places, total):
    mask = 8
    while mask < places.dp:
        total = total + places.swap(total, mask)
        mask *= 2
    return total


def added(places, values, rows, after=()):
    kind = BF16 if places.dp == 8 else F32

    def body(*refs):
        total = refs[0][0:rows].astype(F32)
        for other in refs[1:-1]:
            total = total + other[0:rows].astype(F32)
        refs[-1][...] = total.astype(kind)

    total = call(body, shaped((rows, values[0].shape[1]), kind), [VMEM] * len(values), after=after)(*values)
    return over_groups(places, total).astype(BF16)


def spread_chips(places, own):
    return [own, places.swap(own, X), places.swap(own, Y), places.swap(own, X + Y)]


def spread_cores(places, four):
    return list(four) + [places.swap(stacked(four)[0], CORE)]


def place_rows(piece, pieces, targets):
    for k in range(8):
        source = pieces[k // 2] if k % 2 == 0 else pieces[4].at[k // 2]
        for t, target in enumerate(targets):
            rows = target.shape[0] // 8
            spot = pl.multiple_of((piece ^ k) * rows, rows)
            target[pl.ds(spot, rows), :] = source[t * rows:(t + 1) * rows].astype(F32)


def finish_feed_kernel(info, own, x, y, xy, core, d_in, d_two, held):
    place_rows(info[0], (own, x, y, xy, core), (d_in, held))
    d_two[...] = held[...].T


def finish_mix_kernel(info, own, x, y, xy, core, d_qkv, d_out, held):
    place_rows(info[0], (own, x, y, xy, core), (held,))
    turned = held[...].T
    d_qkv[...] = turned[0:d_qkv.shape[0]]
    d_out[...] = turned[d_qkv.shape[0]:]


def doc_tables(starts_row, base, count):
    spots = base + jnp.arange(count, dtype=jnp.int32)
    started = (spots[:, None] >= starts_row[None, :]).astype(jnp.int32)
    doc_ids = jnp.sum(started, axis=1) - 1
    onehot = (doc_ids[:, None] == jnp.arange(DOCS, dtype=jnp.int32)[None, :]).astype(jnp.int32)
    finish = jnp.concatenate([starts_row[1:], jnp.full((1,), ROW_LEN, jnp.int32)])
    own_start = jnp.sum(onehot * starts_row[None, :], axis=1)
    own_len = jnp.sum(onehot * (finish - starts_row)[None, :], axis=1)
    angles = 0.5 * math.pi * (spots - own_start).astype(F32) / own_len.astype(F32)
    return angles, doc_ids


def doc_at(starts_row, spot):
    return jnp.sum((spot >= starts_row).astype(jnp.int32)) - 1


def on_device(dp, tensor, tokens, starts, w_qkv, b_qkv, w_out, b_out, gain_one, shift_one, w_in, b_in,
              w_two, b_two, gain_two, shift_two, cotangent):
    places = Places(dp, tensor)
    count, width = tokens.shape
    piece = places.piece
    line = lambda a: a.astype(F32).reshape(1, -1)

    def own_rows(weight):
        rows = weight.shape[0] // 8
        return lax.dynamic_slice_in_dim(weight, piece * rows, rows, 0)

    rows = width // 8
    wide = w_qkv.shape[1]
    bias_rows = jnp.concatenate([b_qkv, jnp.zeros((width - wide,), BF16), b_in]).reshape(2, width)
    mix_piece = jnp.concatenate([own_rows(w_qkv.T), own_rows(w_out), bias_rows, jnp.zeros((6, width), BF16)])
    feed_piece = jnp.concatenate([own_rows(w_in), own_rows(w_two)])
    mix_parts = [mix_piece] + [places.turn(mix_piece, s) for s in range(1, tensor)]
    feed_parts = [feed_piece] + [places.turn(feed_piece, s) for s in range(1, tensor - 1)]
    feed_parts.append(places.turn(later(feed_piece, mix_parts), tensor - 1))
    pair = shaped((2, rows, width), BF16)
    mix_a, mix_b, bias_qkv, bias_in = call(
        mix_pieces_kernel, (pair, pair, shaped((tensor, 1, wide), F32), shaped((tensor, 1, width), F32)), [VMEM] * 4,
    )(*mix_parts)
    near_x, near_y = swap_halves(places, mix_a, mix_b)
    mix_ax, mix_by = stacked((mix_a, near_x), (mix_b, near_y))
    mix_buffers = gather_rest(places, mix_ax, mix_by, places.swap(mix_ax, Y), places.swap(mix_by, X))
    feed_a, feed_b = stacked(feed_parts[:2], feed_parts[2:], after=(mix_ax, mix_by))
    near_x, near_y = swap_halves(places, feed_a, feed_b)

    row = starts[0]
    base = places.z * count
    angles, docs = doc_tables(row, base, count)
    first_doc, last_doc = doc_at(row, base), doc_at(row, base + count - 1)
    links = [doc_at(row, base - (s - 1) * count - 1) == first_doc for s in range(1, tensor)]
    links += [doc_at(row, base + s * count) == last_doc for s in range(1, tensor)]
    info = jnp.stack([piece] + [link.astype(jnp.int32) for link in links] + [piece])
    spot = jnp.arange(count)
    turn = jnp.cos(angles[:, None] - angles[None, :])
    same = docs[:, None] == docs[None, :]
    mask = jnp.where(same & (spot[:, None] >= spot[None, :]), turn, 0.0)
    mask_t = jnp.where(same & (spot[:, None] <= spot[None, :]), turn, 0.0)
    lanes = jnp.arange(2 * HEAD)[None, :]
    table = jnp.where(lanes < HEAD, jnp.cos(angles)[:, None], jnp.sin(angles)[:, None])
    query_table = jnp.where((docs == first_doc)[:, None], table, 0.0)
    key_table = jnp.where((docs == last_doc)[:, None], table, 0.0)

    states = shaped((tensor, 3, STATE, 2 * HEAD), BF16)
    sems = lambda n: pltpu.SemaphoreType.DMA((n,))
    mixed, state, mix_weight = call(
        mix_kernel,
        (shaped((tensor, count, wide), BF16), states, shaped((tensor, width, width), BF16)),
        [SMEM, VMEM, VMEM, VMEM] + [ANY] * 6, [sems(32)], after=(mask, mask_t), cost=8,
    )(info, tokens, bias_qkv, key_table, *mix_buffers)
    per_head = shaped((tensor, 3, count, 2 * HEAD), F32)
    arrived = [places.onward(state, s) for s in range(1, tensor)]
    per_head = shaped((tensor, 3, count, 2 * HEAD), F32)
    near_sums = call(local_kernel, per_head, [VMEM, VMEM], cost=7)(mixed, mask)
    feed_ax, feed_by = stacked((feed_a, near_x), (feed_b, near_y), after=(near_sums,))
    feed_far = places.swap(feed_ax, Y), places.swap(feed_by, X)
    attended, carried, dens, first, normed, scale = call(
        join_kernel,
        (shaped((tensor, count, 192), BF16), states, shaped((tensor, count, 128), F32), shaped((count, width), BF16),
         shaped((count, width), F32), shaped((count, 128), F32)),
        [SMEM] + [VMEM] * 11, cost=100,
    )(info, near_sums, *arrived, mixed, query_table, tokens, mix_weight, line(b_out), line(gain_one), line(shift_one))
    feed_buffers = gather_rest(places, *later((feed_ax, feed_by, *feed_far), first))
    hidden_like = shaped((tensor, count, width), BF16)
    vectors = shaped((8, width), F32)
    grad_like = shaped((4 * rows, tensor * width), BF16)
    square = pltpu.VMEM((tensor, width, width), BF16)
    turned = pltpu.VMEM((width, count), BF16)
    total_scratch = pltpu.VMEM((count, width), F32)
    active, slope, block_out, d_second, d_r2, vectors_two, two_keep, two_send = call(
        feed_kernel,
        (hidden_like, hidden_like, shaped((count, width), BF16), shaped((count, width), BF16),
         shaped((count, width), F32), vectors, grad_like, grad_like),
        [SMEM] + [VMEM] * 6 + [ANY] * 6, [square, square, turned, total_scratch, sems(32)], cost=19,
    )(info, first, bias_in, line(b_two), line(gain_two), line(shift_two), cotangent, *feed_buffers)

    got = places.swap(two_send, CORE)
    d_hidden, d_bias_in, in_keep, in_send = call(
        feed_back_kernel, (hidden_like, shaped((tensor, 8, width), F32), grad_like, grad_like),
        [SMEM] + [VMEM] * 3 + [ANY] * 6, [square, turned, sems(16)], cost=14,
    )(info, first, d_second, slope, *feed_buffers)
    wide_halves = halves_like(2 * rows, 2 * width)
    keep0, send0, keep1, send1 = call(first_halves_kernel, wide_halves, [VMEM] * 2, after=(in_send,))(two_keep, got)
    got_two, got_in = swap_all(places, (send0, send1), (X, Y)), places.swap(in_send, CORE)
    d_r1, d_branch, vectors_one = call(
        first_back_kernel,
        (shaped((count, width), F32), shaped((count, width), BF16), vectors),
        [SMEM] + [VMEM] * 5 + [ANY] * 6, [square, total_scratch, sems(16)], after=(send0, send1), cost=11,
    )(info, d_hidden, d_r2, normed, scale, line(gain_one), *feed_buffers)
    keep0, send0, keep1, send1 = call(
        next_halves_kernel, halves_like(rows, 2 * width), [VMEM] * 4, after=(d_branch,))(keep0, keep1, *got_two)
    got_two = swap_all(places, (send0, send1), (Y, X))
    in0, in_send0, in1, in_send1 = call(
        first_halves_kernel, wide_halves, [VMEM] * 2, after=(send0, send1))(in_keep, got_in)
    got_in = swap_all(places, (in_send0, in_send1), (X, Y))
    d_sums, d_carried = call(
        heads_back_kernel, (shaped((tensor, 3, count, 2 * HEAD), BF16), states), [VMEM] * 6,
        after=(in_send0, in_send1), cost=11,
    )(d_branch, mix_weight, attended, dens, mixed, query_table)
    arrived_back = [places.onward(d_carried, -s) for s in range(1, tensor)]
    end = shaped((rows, 2 * width), BF16)
    two_ends = call(ends_kernel, (end, end), [VMEM] * 4, after=(d_carried,))(keep0, keep1, *got_two)
    in0, in_send0, in1, in_send1 = call(
        next_halves_kernel, halves_like(rows, 2 * width), [VMEM] * 4, after=two_ends)(in0, in1, *got_in)
    got_in = swap_all(places, (in_send0, in_send1), (Y, X))
    local = call(
        local_back_kernel, shaped((tensor, count, wide), F32), [VMEM] * 4, after=(in_send0, in_send1), cost=15,
    )(mixed, d_sums, mask, mask_t)
    feed_last = call(
        feed_last_kernel, (shaped((2 * rows, width), BF16),) * tensor, [VMEM] * 6, after=(local, *arrived_back),
    )(in0, in1, *got_in, *two_ends)
    feed_own = turn_back(places, feed_last)
    mix_like = shaped((4 * rows, 2 * width), BF16)
    mix_outs = (shaped((2, count, width), BF16), shaped((2, 8, width), F32), mix_like)
    mix_scratch = [turned, turned, pltpu.VMEM((2, 3, STATE, 2 * HEAD), BF16), pltpu.VMEM((16, width), F32), pltpu.VMEM((2, count, 128), F32)]
    mix_inputs = (info, mixed, local, d_sums, carried, *arrived_back, query_table, key_table, tokens, attended, d_branch)
    d_mixed_a, d_bias_a, keep_a, send_a = call(
        functools.partial(mix_back_kernel, 0), mix_outs + (mix_like,), [SMEM] + [VMEM] * 12, mix_scratch,
        after=feed_last, cost=11,
    )(*mix_inputs)
    a0, send_a0, a1, send_a1 = call(
        first_halves_kernel, halves_like(2 * rows, width), [VMEM] * 2)(keep_a, places.swap(send_a, CORE))
    got_a = swap_all(places, (send_a0, send_a1), (X, Y))
    d_mixed_b, d_bias_b, keep_b, send_b, vector_rows = call(
        functools.partial(mix_back_kernel, 2),
        mix_outs + (shaped((4 * rows + 8, 2 * width), BF16), shaped((16, width), BF16)), [SMEM] + [VMEM] * 16,
        mix_scratch, after=(send_a0, send_a1), cost=11,
    )(*mix_inputs, vectors_one, vectors_two, d_bias_in, d_bias_a)
    a0, send_a0, a1, send_a1 = call(
        next_halves_kernel, halves_like(rows, width), [VMEM] * 4, after=(d_mixed_b,))(a0, a1, *got_a)
    feed_rows = added(places, feed_own, 2 * rows, after=(d_mixed_b,))
    got_b = places.swap(later(send_b, (send_a0, feed_rows)), CORE)
    b0, send_b0, b1, send_b1, vector_rows = call(
        first_halves_rows_kernel, halves_like(2 * rows, width, 16) + (shaped((16, width), BF16),), [VMEM] * 3,
        after=(send_a0, send_a1),
    )(keep_b, got_b, vector_rows)
    got_b = swap_all(places, (send_b0, send_b1), (X, Y))
    feed_four = spread_chips(places, later(feed_rows, (send_b0, send_b1)))
    d_tokens = call(
        tokens_back_kernel, shaped((count, width), BF16), [VMEM] * 4, after=(send_b0, send_b1), cost=6,
    )(d_mixed_a, d_mixed_b, mix_weight, d_r1)
    keep0, send0, keep1, send1, vector_rows = call(
        mix_next_kernel, halves_like(2 * rows, width, 16) + (shaped((16, width), BF16),), [VMEM] * 9,
        after=(d_tokens,),
    )(a0, send_a0, a1, send_a1, b0, b1, *got_b, vector_rows)
    got = swap_all(places, (send0, send1), (Y, X))
    mix_last = call(
        mix_last_kernel, (shaped((rows + 8, width), BF16),) * tensor, [VMEM] * 5,
    )(keep0, keep1, *got, vector_rows)
    mix_own = turn_back(places, mix_last)
    feed_all = spread_cores(places, later(feed_four, (send0, send1)))

    held = pltpu.VMEM((width, width), F32)
    d_w_in, d_w_two = call(
        finish_feed_kernel, (shaped((width, width), F32),) * 2, [SMEM] + [VMEM] * 5, [held], cost=4,
    )(info, *feed_all)
    mix_rows = added(places, mix_own, rows, after=(d_w_in,))
    d_w_qkv, d_w_out = call(
        finish_mix_kernel, (shaped((wide, width), F32), shaped((192, width), F32)), [SMEM] + [VMEM] * 5, [held], cost=3,
    )(info, *spread_cores(places, spread_chips(places, mix_rows)))

    ends = jnp.stack([part[rows:] for part in mix_own])
    ends = lax.dynamic_slice_in_dim(jnp.concatenate([ends, ends]), tensor - places.z, tensor, 0)
    summed = over_groups(places, jnp.sum(ends.astype(F32), axis=0))
    d_gain_one, d_shift_one, d_b_out, d_gain_two, d_shift_two, d_b_two = (summed[k] for k in range(6))
    d_b_qkv, d_b_in = summed[6, :wide], summed[7]
    return (block_out, d_tokens, d_w_qkv.T, d_b_qkv, d_w_out, d_b_out, d_gain_one, d_shift_one, d_w_in, d_b_in,
            d_w_two, d_b_two, d_gain_two, d_shift_two)


def solution(mesh):
    sizes = dict(mesh.shape)
    rows = P(("dp", "tensor"), None)
    wide, tall, cut, whole = P(None, "tensor"), P("tensor", None), P("tensor"), P()
    in_specs = (rows, P("dp", None), wide, cut, tall, whole, whole, whole, wide, cut, tall, whole, whole, whole, rows)
    out_specs = (rows, rows, wide, cut, tall, whole, whole, whole, wide, cut, tall, whole, whole, whole)
    return jax.shard_map(
        functools.partial(on_device, sizes["dp"], sizes["tensor"]),
        mesh=mesh, in_specs=in_specs, out_specs=out_specs, check_vma=False,
    )
```

```python
import functools
import math

import jax
import jax.numpy as jnp
from jax import lax
from jax.experimental import pallas as pl
from jax.experimental.pallas import tpu as pltpu
from jax.sharding import PartitionSpec as P

HEAD = 64
ROW_LEN = 2048
DOCS = 8
F32 = jnp.float32
BF16 = jnp.bfloat16
NN = ((1,), (0,))
NT = ((1,), (1,))
TN = ((0,), (0,))
STATE = 80
COST = 0.2 * 1.15e9
VMEM = pl.BlockSpec(memory_space=pltpu.VMEM)
SMEM = pl.BlockSpec(memory_space=pltpu.SMEM)
ANY = pl.BlockSpec(memory_space=pl.ANY)


def dot(left, right, dims=NN):
    return lax.dot_general(left, right, (dims, ((), ())), preferred_element_type=F32)


def call(body, outs, specs, scratch=(), limit=6, after=(), cost=0):
    n = len(specs)

    def waiting_body(*refs):
        body(*refs[:n], *refs[n + len(after):])

    return lambda *operands: pl.pallas_call(
        waiting_body,
        out_shape=outs,
        in_specs=list(specs) + [ANY] * len(after),
        out_specs=jax.tree.map(lambda _: VMEM, outs),
        scratch_shapes=scratch,
        cost_estimate=pl.CostEstimate(flops=1 + int(cost * COST), bytes_accessed=1, transcendentals=0),
        compiler_params=pltpu.CompilerParams(vmem_limit_bytes=limit << 20),
    )(*operands, *after)


def shaped(shape, dtype):
    return jax.ShapeDtypeStruct(shape, dtype)


class Places:
    def __init__(self, dp, tensor):
        self.dp, self.tensor = dp, tensor
        self.row = lax.axis_index("dp")
        self.z = lax.axis_index("tensor")
        self.piece = self.row & 7

    def swap(self, value, mask):
        return lax.ppermute(value, "dp", [(d, d ^ mask) for d in range(self.dp)])

    def turn(self, value, step):
        size = self.tensor
        return lax.ppermute(value, "tensor", [(k, (k + step) % size) for k in range(size)])

    def onward(self, value, step):
        size = self.tensor
        pairs = [(k, k + step) for k in range(size) if 0 <= k + step < size]
        return lax.ppermute(value, "tensor", pairs)


CORE, X, Y = 1, 2, 4
BUFFERS = ((0, (0, 2)), (0, (4, 6)), (0, (1, 3)), (0, (5, 7)), (2, (0, 4)), (2, (2, 6)), (2, (1, 5)), (2, (3, 7)))


def stacked(*groups, after=()):
    sizes = [len(group) for group in groups]

    def body(*refs):
        sources, targets = list(refs[:sum(sizes)]), refs[sum(sizes):]
        for size, target in zip(sizes, targets, strict=True):
            for k in range(size):
                target[k] = sources.pop(0)[...]

    outs = tuple(shaped((len(group),) + group[0].shape, group[0].dtype) for group in groups)
    flat = [value for group in groups for value in group]
    return call(body, outs, [VMEM] * len(flat), after=after)(*flat)


def mix_pieces_kernel(first, second, third, fourth, a, b, bias_qkv, bias_in):
    rows, wide = a.shape[1], bias_qkv.shape[2]
    for j, part in enumerate((first, second, third, fourth)):
        (a, b)[j // 2][j % 2] = part[0:rows]
        extra = part[rows:].astype(F32)
        bias_qkv[j] = extra[0:1, :wide]
        bias_in[j] = extra[1:2]


def swap_halves(places, a, b):
    return places.swap(a, X), places.swap(b, Y)


def gather_rest(places, a, b, a2, b2):
    near, far = stacked((a, b)), stacked((a2, b2))
    return a, a2, b, b2, places.swap(near[0], CORE), places.swap(far[0], CORE)


def start_placing(piece, buffers, targets, sems):
    copies = []
    a, a2, b, b2, near, far = buffers
    buffers = (a, a2, near.at[0], far.at[0], b, b2, near.at[1], far.at[1])
    for buffer, (shard, pieces) in zip(buffers, BUFFERS, strict=True):
        for k, other in enumerate(pieces):
            for at, target, first_row, rows in targets:
                spot = pl.multiple_of(first_row + (piece ^ other) * rows, 8)
                copies.append(pltpu.make_async_copy(
                    buffer.at[k, :, at:at + rows, :],
                    target.at[shard:shard + 2, pl.ds(spot, rows), :],
                    sems.at[len(copies)],
                ))
    for copy in copies:
        copy.start()
    half = len(copies) // 2
    return copies[:half], copies[half:]


def wait_all(copies):
    for copy in copies:
        copy.wait()


def doubled(part):
    return jnp.concatenate([part, part], axis=1)


def with_one(value):
    lanes = lax.broadcasted_iota(jnp.int32, (value.shape[0], 2 * HEAD), 1)
    return jnp.where(lanes < HEAD, doubled(value.astype(F32)), (lanes == HEAD).astype(F32)).astype(BF16)


def head_parts(mixed_ref, shard, head):
    at = head * 3 * HEAD
    return tuple(mixed_ref[shard, :, at + t * HEAD:at + (t + 1) * HEAD] for t in range(3))


def causal_blocks(count):
    half = count // 2
    return ((0, half, 0, half), (half, count, 0, count))


def mix_kernel(info, tokens, bias, key_table, *refs):
    buffers, (mixed_out, state_out, weight), sems = refs[:6], refs[6:9], refs[9]
    wide = mixed_out.shape[2]
    tall = weight.shape[1] - wide
    halves = start_placing(
        info[0], buffers, ((0, weight, 0, wide // 8), (wide // 8, weight, wide, tall // 8)), sems)

    def shard_step(j, carry):
        mixed = dot(tokens[...], weight[j, 0:wide], NT) + bias[j]
        lanes = lax.broadcasted_iota(jnp.int32, mixed.shape, 1)
        mixed_out[j] = jnp.where(lanes % 192 >= 128, mixed, jnp.maximum(mixed, 0.0)).astype(BF16)
        for h in range(3):
            _, key, value = head_parts(mixed_out, j, h)
            feats = (doubled(key).astype(F32) * key_table[...]).astype(BF16)
            state_out[j, h] = dot(with_one(value), feats, TN)[:STATE].astype(BF16)
        return carry

    for k, half in enumerate(halves):
        wait_all(half)
        lax.fori_loop(2 * k, 2 * k + 2, shard_step, 0)


def local_kernel(mixed, mask, sums_out):
    def shard_step(j, carry):
        for h in range(3):
            query, key, value = head_parts(mixed, j, h)
            value = with_one(value)
            for r0, r1, c0, c1 in causal_blocks(mask.shape[0]):
                scores = (dot(query[r0:r1], key[c0:c1], NT) * mask[r0:r1, c0:c1]).astype(BF16)
                sums_out[j, h, r0:r1] = dot(scores, value[c0:c1])
        return carry

    lax.fori_loop(0, mixed.shape[0], shard_step, 0)


def norm_parts(rows_in):
    centred = rows_in - jnp.mean(rows_in, axis=-1, keepdims=True)
    spread = jnp.mean(centred * centred, axis=-1, keepdims=True)
    scale = lax.rsqrt(spread + 1e-05)
    return centred * scale, scale


def norm_back(grad, normed, scale, gain):
    e = grad * gain
    d_rows = scale * (
        e
        - jnp.mean(e, axis=-1, keepdims=True)
        - normed * jnp.mean(e * normed, axis=-1, keepdims=True)
    )
    return d_rows, jnp.sum(grad * normed, axis=0, keepdims=True), jnp.sum(grad, axis=0, keepdims=True)


def join_kernel(info, sums, arrived1, arrived2, arrived3, mixed, query_table, tokens, weight, b_out, gain, shift,
                attended, carried, dens, first, normed_out, scale_out):
    shards = mixed.shape[0]
    for j in range(shards):
        total = None
        for step, arrived in enumerate((arrived1, arrived2, arrived3), 1):
            linked = info[step].astype(F32) * arrived[(j - step) % shards].astype(F32)
            total = linked if total is None else total + linked
        carried[j] = total.astype(BF16)

    def shard_step(j, branch):
        lanes = lax.broadcasted_iota(jnp.int32, (tokens.shape[0], 128), 1)
        kept = jnp.zeros((tokens.shape[0], 128), F32)
        for h in range(3):
            query = head_parts(mixed, j, h)[0]
            feats = (doubled(query).astype(F32) * query_table[...]).astype(BF16)
            total = sums[j, h][:, :STATE] + dot(feats, carried[j, h], NT)
            den = total[:, HEAD:HEAD + 1]
            inverse = 1.0 / jnp.maximum(den, 1.0)
            attended[j, :, h * HEAD:(h + 1) * HEAD] = (total[:, :HEAD] * inverse).astype(BF16)
            kept = jnp.where(lanes == h, inverse, kept)
            kept = jnp.where(lanes == 8 + h, jnp.where(den > 1.0, inverse, 0.0), kept)
        dens[j] = kept
        return branch + dot(attended[j], weight[j, weight.shape[1] - 192:])

    branch = lax.fori_loop(0, shards, shard_step, jnp.zeros(tokens.shape, F32))
    normed, scale = norm_parts(tokens[...].astype(F32) + branch + b_out[...])
    normed_out[...] = normed
    scale_out[...] = jnp.broadcast_to(scale, scale_out.shape)
    first[...] = (normed * gain[...] + shift[...]).astype(BF16)


def gelu_parts(v):
    k = math.sqrt(2 / math.pi)
    square = v * v
    t = jnp.tanh(v * (k + k * 0.044715 * square))
    half = 0.5 * v
    bent = half * t
    slope = (0.5 + 0.5 * t) + (half - bent * t) * (k + 3 * k * 0.044715 * square)
    return half + bent, slope


def rows_ordered(turned, piece, order):
    rows = turned.shape[0] // 8
    return jnp.concatenate(
        [turned[pl.ds(pl.multiple_of((piece ^ other) * rows, rows), rows), :] for other in order], axis=0)


ROUTES = ((0, 4, 2, 6), (0, 2, 4, 6))


def order_rows(ordered, turned, piece):
    for route, order in enumerate(ROUTES):
        for sends in range(2):
            ordered[2 * route + sends] = rows_ordered(turned, piece, tuple(other + sends for other in order))


def columns(j, width):
    return pl.ds(pl.multiple_of(j * width, 128), width)


def feed_kernel(info, first, bias, b_two, gain, shift, cotangent, *refs):
    buffers = refs[:6]
    active, slope, block_out, d_second_out, d_r2_out, vectors, *grads = refs[6:14]
    w_in, w_two, turned, ordered, total, sems = refs[14:]
    shards, width = w_in.shape[0], w_in.shape[2]
    rows = width // 8
    halves = start_placing(info[0], buffers, ((0, w_in, 0, rows), (rows, w_two, 0, rows)), sems)
    total[...] = jnp.broadcast_to(b_two[...], total.shape)

    def forward_step(j, carry):
        act, bend = gelu_parts(dot(first[...], w_in[j]) + bias[j])
        active[j] = act.astype(BF16)
        slope[j] = bend.astype(BF16)
        total[...] += dot(active[j], w_two[j])
        return carry

    for k, half in enumerate(halves):
        wait_all(half)
        lax.fori_loop(2 * k, 2 * k + 2, forward_step, 0)
    normed, scale = norm_parts(first[...].astype(F32) + total[...])
    block_out[...] = (normed * gain[...] + shift[...]).astype(BF16)
    d_r2, d_gain, d_shift = norm_back(cotangent[...].astype(F32), normed, scale, gain[...])
    d_r2_out[...] = d_r2
    d_second = d_r2.astype(BF16)
    d_second_out[...] = d_second
    turned[...] = d_second.T
    vectors[0:1] = d_gain
    vectors[1:2] = d_shift
    vectors[2:3] = jnp.sum(d_second.astype(F32), axis=0, keepdims=True)
    vectors[3:] = jnp.zeros((5, vectors.shape[1]), F32)
    order_rows(ordered, turned, info[0])

    def grad_step(j, carry):
        for sends in range(2):
            grads[sends][:, columns(j, width)] = dot(ordered[2 * (j // 2) + sends], active[j]).astype(BF16)
        return carry

    lax.fori_loop(0, shards, grad_step, 0)


def feed_back_kernel(info, first, d_second, slope, *refs):
    buffers = refs[:6]
    d_hidden, d_bias, *grads = refs[6:10]
    w_two, turned, ordered, sems = refs[10:]
    shards, width = w_two.shape[0], w_two.shape[2]
    rows = width // 8
    halves = start_placing(info[0], buffers, ((rows, w_two, 0, rows),), sems)
    turned[...] = first[...].T
    order_rows(ordered, turned, info[0])

    def step(j, carry):
        d_active = dot(d_second[...], w_two[j], NT)
        d_h = (d_active * slope[j].astype(F32)).astype(BF16)
        d_hidden[j] = d_h
        d_bias[j] = jnp.broadcast_to(jnp.sum(d_h.astype(F32), axis=0, keepdims=True), d_bias.shape[1:])
        for sends in range(2):
            grads[sends][:, columns(j, width)] = dot(ordered[2 * (j // 2) + sends], d_hidden[j]).astype(BF16)
        return carry

    for k, half in enumerate(halves):
        wait_all(half)
        lax.fori_loop(2 * k, 2 * k + 2, step, 0)


def first_back_kernel(info, d_hidden, d_r2, normed, scale, gain, *refs):
    buffers = refs[:6]
    d_r1_out, d_branch_out, vectors = refs[6:9]
    w_in, total, sems = refs[9:]
    rows = w_in.shape[1] // 8
    halves = start_placing(info[0], buffers, ((0, w_in, 0, rows),), sems)
    total[...] = d_r2[...]

    def first_step(j, carry):
        total[...] += dot(d_hidden[j], w_in[j], NT)
        return carry

    for k, half in enumerate(halves):
        wait_all(half)
        lax.fori_loop(2 * k, 2 * k + 2, first_step, 0)
    d_r1, d_gain, d_shift = norm_back(total[...], normed[...], scale[:, 0:1], gain[...])
    d_r1_out[...] = d_r1
    d_branch = d_r1.astype(BF16)
    d_branch_out[...] = d_branch
    vectors[0:1] = d_gain
    vectors[1:2] = d_shift
    vectors[2:3] = jnp.sum(d_branch.astype(F32), axis=0, keepdims=True)
    vectors[3:] = jnp.zeros((5, vectors.shape[1]), F32)


def heads_back_kernel(d_branch, weight, attended, dens, mixed, query_table, d_sums, d_carried):
    def shard_step(j, carry):
        g_all = dot(d_branch[...], weight[j, weight.shape[1] - 192:], NT)
        lanes = lax.broadcasted_iota(jnp.int32, (d_branch.shape[0], 128), 1)
        for h in range(3):
            g = g_all[:, h * HEAD:(h + 1) * HEAD]
            o = attended[j, :, h * HEAD:(h + 1) * HEAD].astype(F32)
            inverse, inverse_if = dens[j, :, h:h + 1], dens[j, :, 8 + h:9 + h]
            d_den = -jnp.sum(g * o, axis=-1, keepdims=True) * inverse_if
            d_num = doubled(g * inverse)
            both = jnp.where(lanes < HEAD, d_num, jnp.where(lanes == HEAD, d_den, 0.0)).astype(BF16)
            d_sums[j, h] = both
            query = head_parts(mixed, j, h)[0]
            feats = (doubled(query).astype(F32) * query_table[...]).astype(BF16)
            d_carried[j, h] = dot(both, feats, TN)[:STATE].astype(BF16)
        return carry

    lax.fori_loop(0, mixed.shape[0], shard_step, 0)


def local_back_kernel(mixed, d_sums, mask, mask_t, d_mixed):
    def shard_step(j, carry):
        for h in range(3):
            query, key, value = head_parts(mixed, j, h)
            value = with_one(value)
            grad = d_sums[j, h]
            at = h * 3 * HEAD
            for r0, r1, c0, c1 in causal_blocks(mask.shape[0]):
                d_scores = (dot(grad[r0:r1], value[c0:c1], NT) * mask[r0:r1, c0:c1]).astype(BF16)
                d_mixed[j, r0:r1, at:at + HEAD] = dot(d_scores, key[c0:c1])
            half = mask.shape[0] // 2
            for c0, c1, r0 in ((0, half, 0), (half, 2 * half, half)):
                turned = mask_t[c0:c1, r0:]
                d_scores = (dot(value[c0:c1], grad[r0:], NT) * turned).astype(BF16)
                d_mixed[j, c0:c1, at + HEAD:at + 2 * HEAD] = dot(d_scores, query[r0:])
                scores = (dot(key[c0:c1], query[r0:], NT) * turned).astype(BF16)
                d_mixed[j, c0:c1, at + 2 * HEAD:at + 3 * HEAD] = dot(scores, grad[r0:])[:, :HEAD]
        return carry

    lax.fori_loop(0, mixed.shape[0], shard_step, 0)


def mix_back_kernel(base, info, mixed, local, d_sums, carried, arrived1, arrived2, arrived3, query_table, key_table,
                    tokens, attended, d_branch, *refs):
    last = base > 0
    sources, refs = (refs[:4], refs[4:]) if last else ((), refs)
    d_mixed, d_bias, *grads = refs[:4]
    turned, turned_branch, state, held, middles = refs[-5:]
    shards, wide = mixed.shape[0], mixed.shape[2]
    width = d_mixed.shape[2]
    turned[...] = tokens[...].T
    turned_branch[...] = d_branch[...].T
    for k in range(2):
        total = None
        for step, arrived in enumerate((arrived1, arrived2, arrived3), 1):
            linked = info[3 + step].astype(F32) * arrived[(base + k + step) % shards].astype(F32)
            total = linked if total is None else total + linked
        state[k] = total.astype(BF16)

    def folded(both):
        return both[:, :HEAD] + both[:, HEAD:]

    def shard_step(k, carry):
        j = base + k
        parts = []
        for h in range(3):
            query, key, value = head_parts(mixed, j, h)
            at = h * 3 * HEAD
            spans = [slice(at + t * HEAD, at + (t + 1) * HEAD) for t in range(3)]
            d_query = folded(dot(d_sums[j, h][:, :STATE], carried[j, h]) * query_table[...])
            d_query = jnp.where(query.astype(F32) > 0, local[j, :, spans[0]] + d_query, 0.0)
            d_key = folded(dot(with_one(value)[:, :STATE], state[k, h]) * key_table[...])
            d_key = jnp.where(key.astype(F32) > 0, local[j, :, spans[1]] + d_key, 0.0)
            feats = (doubled(key).astype(F32) * key_table[...]).astype(BF16)
            d_value = local[j, :, spans[2]] + dot(feats, state[k, h], NT)[:, :HEAD]
            parts += [d_query, d_key, d_value]
        whole = jnp.concatenate(parts + [attended[j].astype(F32)], axis=1).astype(BF16)
        d_mixed[k] = whole
        middles[k] = jnp.concatenate([parts[-1], attended[j][:, :HEAD].astype(F32)], axis=1)
        d_bias[k] = jnp.broadcast_to(jnp.sum(d_mixed[k].astype(F32), axis=0, keepdims=True), d_bias.shape[1:])
        return carry

    lax.fori_loop(0, 2, shard_step, 0)
    rows = grads[0].shape[0]
    low = wide // 128 * 128
    for k in range(2):
        lanes = lax.broadcasted_iota(jnp.int32, (d_mixed.shape[1], 128), 1)
        middle = middles[k]
        left_side = jnp.where(lanes < HEAD, middle, 0.0).astype(BF16)
        right_side = jnp.where(lanes < HEAD, 0.0, middle).astype(BF16)
        left_side = jnp.concatenate([d_mixed[k][:, :low], left_side], axis=1)
        right_side = jnp.concatenate([right_side, d_mixed[k][:, low + 128:]], axis=1)
        for sends in (1, 0):
            out, at = grads[sends], k * width
            order = tuple(other + sends for other in ROUTES[k])
            left = dot(rows_ordered(turned, info[0], order), left_side)
            right = dot(rows_ordered(turned_branch, info[0], order), right_side)
            out[0:rows, at:at + low] = left[:, :low].astype(BF16)
            out[0:rows, at + low:at + low + 128] = (left[:, low:] + right[:, :128]).astype(BF16)
            out[0:rows, at + low + 128:at + width] = right[:, 128:].astype(BF16)
    if last:
        one, two, bias_in, bias_first = sources
        vectors = refs[4]
        held[0:3] = one[0:3]
        held[3:6] = two[0:3]
        for j in range(shards):
            held[6 + 2 * j:7 + 2 * j] = bias_first[j, 0:1] if j < 2 else d_bias[j - 2, 0:1]
            held[7 + 2 * j:8 + 2 * j] = bias_in[j, 0:1]
        held[14:16] = jnp.zeros((2, width), F32)
        low_rows = held[...].astype(BF16)
        vectors[...] = low_rows
        grads[1][rows:, 0:width] = low_rows[0:8]
        grads[1][rows:, width:] = low_rows[8:16]


def tokens_back_kernel(d_mixed_a, d_mixed_b, weight, d_r1, d_tokens):
    wide = weight.shape[1] - 192
    total = d_r1[...]
    for j in range(weight.shape[0]):
        d_mixed = (d_mixed_a, d_mixed_b)[j // 2]
        total = total + dot(d_mixed[j % 2][:, :wide], weight[j, 0:wide])
    d_tokens[...] = total.astype(BF16)


def later(values, others):
    return lax.optimization_barrier((values, others))[0]


def halves_like(rows, width, extra=0):
    keep, send = shaped((rows, width), F32), shaped((rows, width), BF16)
    return keep, send, keep, shaped((rows + extra, width), BF16)


def first_halves_kernel(keep, got, *outs):
    half, width = outs[0].shape
    for k in range(2):
        cols = slice(k * width, (k + 1) * width)
        outs[2 * k][...] = keep[0:half, cols].astype(F32) + got[0:half, cols].astype(F32)
        send = keep[half:2 * half, cols].astype(F32) + got[half:2 * half, cols].astype(F32)
        outs[2 * k + 1][0:half] = send.astype(BF16)


def first_pairs_kernel(keep_a, got_a, keep_b, got_b, mine, *outs):
    half, width = outs[0].shape[0] // 2, outs[0].shape[1]
    for k in range(2):
        cols = slice(k * width, (k + 1) * width)
        for t, (keep, got) in enumerate(((keep_a, got_a), (keep_b, got_b))):
            spots = slice(t * half, (t + 1) * half)
            outs[2 * k][spots] = keep[0:half, cols].astype(F32) + got[0:half, cols].astype(F32)
            send = keep[half:2 * half, cols].astype(F32) + got[half:2 * half, cols].astype(F32)
            outs[2 * k + 1][spots] = send.astype(BF16)
        rows = mine[8 * k:8 * k + 8].astype(F32) + got_b[2 * half:, cols].astype(F32)
        outs[4][8 * k:8 * k + 8] = rows.astype(BF16)
        outs[3][2 * half + 8 * k:2 * half + 8 * k + 8] = rows.astype(BF16)


def next_halves_kernel(keep0, keep1, got0, got1, *outs):
    half = outs[0].shape[0]
    for k, (keep, got) in enumerate(((keep0, got0), (keep1, got1))):
        outs[2 * k][...] = keep[0:half] + got[0:half].astype(F32)
        outs[2 * k + 1][...] = (keep[half:] + got[half:].astype(F32)).astype(BF16)


def ends_kernel(keep0, keep1, got0, got1, end0, end1):
    end0[...] = (keep0[...] + got0[...].astype(F32)).astype(BF16)
    end1[...] = (keep1[...] + got1[...].astype(F32)).astype(BF16)


def feed_last_kernel(keep0, keep1, got0, got1, two0, two1, *outs):
    rows, width = outs[0].shape[0] // 2, outs[0].shape[1]
    for j, out in enumerate(outs):
        keep, got, two = (keep0, got0, two0) if j < 2 else (keep1, got1, two1)
        cols = slice(j % 2 * width, (j % 2 + 1) * width)
        out[0:rows] = (keep[:, cols] + got[:, cols].astype(F32)).astype(BF16)
        out[rows:] = two[:, cols]


def mix_next_kernel(keep0, keep1, got0, got1, mine, *outs):
    half = outs[0].shape[0] // 2
    for k, (keep, got) in enumerate(((keep0, got0), (keep1, got1))):
        for t in range(2):
            at = 2 * t * half
            spots = slice(t * half, (t + 1) * half)
            outs[2 * k][spots] = keep[at:at + half] + got[at:at + half].astype(F32)
            send = keep[at + half:at + 2 * half] + got[at + half:at + 2 * half].astype(F32)
            outs[2 * k + 1][spots] = send.astype(BF16)
    rows = (mine[...].astype(F32) + got1[4 * half:].astype(F32)).astype(BF16)
    outs[4][...] = rows
    outs[3][2 * half:] = rows


def mix_last_kernel(keep0, keep1, got0, got1, mine, *outs):
    half = keep0.shape[0] // 2
    rows = (mine[...].astype(F32) + got1[2 * half:].astype(F32)).astype(BF16)
    for j, out in enumerate(outs):
        keep, got = (keep0, got0) if j % 2 == 0 else (keep1, got1)
        spots = slice(j // 2 * half, (j // 2 + 1) * half)
        out[0:half] = (keep[spots] + got[spots].astype(F32)).astype(BF16)
        out[half:half + 6] = rows[0:6]
        out[half + 6:half + 8] = rows[6 + 2 * j:8 + 2 * j]


def swap_all(places, values, masks):
    return [places.swap(value, mask) for value, mask in zip(values, masks, strict=True)]


def turn_back(places, parts):
    return [parts[0]] + [places.turn(parts[s], -s) for s in range(1, places.tensor)]


def pair_sum(mine, other):
    return (mine.astype(F32) + other.astype(F32)).astype(BF16)


def over_groups(places, total):
    mask = 8
    while mask < places.dp:
        total = total + places.swap(total, mask)
        mask *= 2
    return total


def added(places, values, rows, after=()):
    kind = BF16 if places.dp == 8 else F32

    def body(*refs):
        total = refs[0][0:rows].astype(F32)
        for other in refs[1:-1]:
            total = total + other[0:rows].astype(F32)
        refs[-1][...] = total.astype(kind)

    total = call(body, shaped((rows, values[0].shape[1]), kind), [VMEM] * len(values), after=after)(*values)
    return over_groups(places, total).astype(BF16)


def spread_chips(places, own):
    return [own, places.swap(own, X), places.swap(own, Y), places.swap(own, X + Y)]


def spread_cores(places, four):
    return list(four) + [places.swap(stacked(four)[0], CORE)]


def place_rows(piece, pieces, targets):
    for k in range(8):
        source = pieces[k // 2] if k % 2 == 0 else pieces[4].at[k // 2]
        for t, target in enumerate(targets):
            rows = target.shape[0] // 8
            spot = pl.multiple_of((piece ^ k) * rows, rows)
            target[pl.ds(spot, rows), :] = source[t * rows:(t + 1) * rows].astype(F32)


def finish_feed_kernel(info, own, x, y, xy, core, d_in, d_two, held):
    place_rows(info[0], (own, x, y, xy, core), (d_in, held))
    d_two[...] = held[...].T


def finish_mix_kernel(info, own, x, y, xy, core, d_qkv, d_out, held):
    place_rows(info[0], (own, x, y, xy, core), (held,))
    turned = held[...].T
    d_qkv[...] = turned[0:d_qkv.shape[0]]
    d_out[...] = turned[d_qkv.shape[0]:]


def doc_tables(starts_row, base, count):
    spots = base + jnp.arange(count, dtype=jnp.int32)
    started = (spots[:, None] >= starts_row[None, :]).astype(jnp.int32)
    doc_ids = jnp.sum(started, axis=1) - 1
    onehot = (doc_ids[:, None] == jnp.arange(DOCS, dtype=jnp.int32)[None, :]).astype(jnp.int32)
    finish = jnp.concatenate([starts_row[1:], jnp.full((1,), ROW_LEN, jnp.int32)])
    own_start = jnp.sum(onehot * starts_row[None, :], axis=1)
    own_len = jnp.sum(onehot * (finish - starts_row)[None, :], axis=1)
    angles = 0.5 * math.pi * (spots - own_start).astype(F32) / own_len.astype(F32)
    return angles, doc_ids


def doc_at(starts_row, spot):
    return jnp.sum((spot >= starts_row).astype(jnp.int32)) - 1


def on_device(dp, tensor, tokens, starts, w_qkv, b_qkv, w_out, b_out, gain_one, shift_one, w_in, b_in,
              w_two, b_two, gain_two, shift_two, cotangent):
    places = Places(dp, tensor)
    count, width = tokens.shape
    piece = places.piece
    line = lambda a: a.astype(F32).reshape(1, -1)
    sems = lambda n: pltpu.SemaphoreType.DMA((n,))

    def own_rows(weight):
        rows = weight.shape[0] // 8
        return lax.dynamic_slice_in_dim(weight, piece * rows, rows, 0)

    rows = width // 8
    wide = w_qkv.shape[1]
    bias_rows = jnp.pad(b_qkv.reshape(1, wide), ((0, 7), (0, width - wide))) + jnp.pad(b_in.reshape(1, width), ((1, 6), (0, 0)))
    mix_piece = jnp.concatenate([own_rows(w_qkv.T), own_rows(w_out), bias_rows])
    feed_piece = jnp.concatenate([own_rows(w_in), own_rows(w_two)])
    mix_parts = [mix_piece] + [places.turn(mix_piece, s) for s in range(1, tensor)]
    feed_parts = [feed_piece] + [places.turn(feed_piece, s) for s in range(1, tensor - 1)]
    feed_parts.append(places.turn(later(feed_piece, mix_parts), tensor - 1))
    pair = shaped((2, rows, width), BF16)
    mix_a, mix_b, bias_qkv, bias_in = call(
        mix_pieces_kernel, (pair, pair, shaped((tensor, 1, wide), F32), shaped((tensor, 1, width), F32)), [VMEM] * 4,
    )(*mix_parts)
    near_x, near_y = swap_halves(places, mix_a, mix_b)
    mix_ax, mix_by = stacked((mix_a, near_x), (mix_b, near_y))
    mix_buffers = gather_rest(places, mix_ax, mix_by, places.swap(mix_ax, Y), places.swap(mix_by, X))
    feed_a, feed_b = stacked(feed_parts[:2], feed_parts[2:], after=(mix_ax, mix_by))
    near_x, near_y = swap_halves(places, feed_a, feed_b)

    row = starts[0]
    base = places.z * count
    angles, docs = doc_tables(row, base, count)
    first_doc, last_doc = doc_at(row, base), doc_at(row, base + count - 1)
    links = [doc_at(row, base - (s - 1) * count - 1) == first_doc for s in range(1, tensor)]
    links += [doc_at(row, base + s * count) == last_doc for s in range(1, tensor)]
    info = jnp.stack([piece] + [link.astype(jnp.int32) for link in links] + [piece])
    spot = jnp.arange(count)
    turn = jnp.cos(angles[:, None] - angles[None, :])
    same = docs[:, None] == docs[None, :]
    mask = jnp.where(same & (spot[:, None] >= spot[None, :]), turn, 0.0)
    mask_t = jnp.where(same & (spot[:, None] <= spot[None, :]), turn, 0.0)
    lanes = jnp.arange(2 * HEAD)[None, :]
    table = jnp.where(lanes < HEAD, jnp.cos(angles)[:, None], jnp.sin(angles)[:, None])
    query_table = jnp.where((docs == first_doc)[:, None], table, 0.0)
    key_table = jnp.where((docs == last_doc)[:, None], table, 0.0)

    states = shaped((tensor, 3, STATE, 2 * HEAD), BF16)
    mixed, state, mix_weight = call(
        mix_kernel,
        (shaped((tensor, count, wide), BF16), states, shaped((tensor, width, width), BF16)),
        [SMEM, VMEM, VMEM, VMEM] + [ANY] * 6, [sems(32)], after=(mask, mask_t), limit=9, cost=8,
    )(info, tokens, bias_qkv, key_table, *mix_buffers)
    per_head = shaped((tensor, 3, count, 2 * HEAD), F32)
    arrived = [places.onward(state, s) for s in range(1, tensor)]
    per_head = shaped((tensor, 3, count, 2 * HEAD), F32)
    feed_ax, feed_by = stacked((feed_a, near_x), (feed_b, near_y), after=(state,))
    near_sums = call(local_kernel, per_head, [VMEM, VMEM], after=(feed_ax, feed_by), limit=6, cost=7)(mixed, mask)
    feed_far = places.swap(feed_ax, Y), places.swap(feed_by, X)
    attended, carried, dens, first, normed, scale = call(
        join_kernel,
        (shaped((tensor, count, 192), BF16), states, shaped((tensor, count, 128), F32), shaped((count, width), BF16),
         shaped((count, width), F32), shaped((count, 128), F32)),
        [SMEM] + [VMEM] * 11, limit=18, cost=100,
    )(info, near_sums, *arrived, mixed, query_table, tokens, mix_weight, line(b_out), line(gain_one), line(shift_one))
    feed_buffers = gather_rest(places, *later((feed_ax, feed_by, *feed_far), first))
    hidden_like = shaped((tensor, count, width), BF16)
    vectors = shaped((8, width), F32)
    grad_like = shaped((4 * rows, tensor * width), BF16)
    square = pltpu.VMEM((tensor, width, width), BF16)
    turned = pltpu.VMEM((width, count), BF16)
    ordered = pltpu.VMEM((4, 4 * rows, count), BF16)
    total_scratch = pltpu.VMEM((count, width), F32)
    active, slope, block_out, d_second, d_r2, vectors_two, two_keep, two_send = call(
        feed_kernel,
        (hidden_like, hidden_like, shaped((count, width), BF16), shaped((count, width), BF16),
         shaped((count, width), F32), vectors, grad_like, grad_like),
        [SMEM] + [VMEM] * 6 + [ANY] * 6, [square, square, turned, ordered, total_scratch, sems(32)], limit=33, cost=19,
    )(info, first, bias_in, line(b_two), line(gain_two), line(shift_two), cotangent, *feed_buffers)

    got = places.swap(two_send, CORE)
    d_hidden, d_bias_in, in_keep, in_send = call(
        feed_back_kernel, (hidden_like, shaped((tensor, 8, width), F32), grad_like, grad_like),
        [SMEM] + [VMEM] * 3 + [ANY] * 6, [square, turned, ordered, sems(16)], limit=19, cost=14,
    )(info, first, d_second, slope, *feed_buffers)
    wide_halves = halves_like(2 * rows, 2 * width)
    keep0, send0, keep1, send1 = call(first_halves_kernel, wide_halves, [VMEM] * 2, after=(in_send,))(two_keep, got)
    got_two, got_in = swap_all(places, (send0, send1), (X, Y)), places.swap(in_send, CORE)
    d_r1, d_branch, vectors_one = call(
        first_back_kernel,
        (shaped((count, width), F32), shaped((count, width), BF16), vectors),
        [SMEM] + [VMEM] * 5 + [ANY] * 6, [square, total_scratch, sems(16)], after=(send0, send1), limit=17, cost=11,
    )(info, d_hidden, d_r2, normed, scale, line(gain_one), *feed_buffers)
    keep0, send0, keep1, send1 = call(
        next_halves_kernel, halves_like(rows, 2 * width), [VMEM] * 4, after=(d_branch,))(keep0, keep1, *got_two)
    got_two = swap_all(places, (send0, send1), (Y, X))
    in0, in_send0, in1, in_send1 = call(
        first_halves_kernel, wide_halves, [VMEM] * 2, after=(send0, send1))(in_keep, got_in)
    got_in = swap_all(places, (in_send0, in_send1), (X, Y))
    d_sums, d_carried = call(
        heads_back_kernel, (shaped((tensor, 3, count, 2 * HEAD), BF16), states), [VMEM] * 6,
        after=(in_send0, in_send1), limit=10, cost=11,
    )(d_branch, mix_weight, attended, dens, mixed, query_table)
    arrived_back = [places.onward(d_carried, -s) for s in range(1, tensor)]
    end = shaped((rows, 2 * width), BF16)
    two_ends = call(ends_kernel, (end, end), [VMEM] * 4, after=(d_carried,))(keep0, keep1, *got_two)
    in0, in_send0, in1, in_send1 = call(
        next_halves_kernel, halves_like(rows, 2 * width), [VMEM] * 4, after=two_ends)(in0, in1, *got_in)
    got_in = swap_all(places, (in_send0, in_send1), (Y, X))
    local = call(
        local_back_kernel, shaped((tensor, count, wide), F32), [VMEM] * 4, after=(in_send0, in_send1), limit=10, cost=15,
    )(mixed, d_sums, mask, mask_t)
    feed_last = call(
        feed_last_kernel, (shaped((2 * rows, width), BF16),) * tensor, [VMEM] * 6, after=(local, *arrived_back),
    )(in0, in1, *got_in, *two_ends)
    feed_own = turn_back(places, feed_last)
    mix_like = shaped((4 * rows, 2 * width), BF16)
    mix_outs = (shaped((2, count, width), BF16), shaped((2, 8, width), F32), mix_like)
    mix_scratch = [turned, turned, pltpu.VMEM((2, 3, STATE, 2 * HEAD), BF16), pltpu.VMEM((16, width), F32), pltpu.VMEM((2, count, 128), F32)]
    mix_inputs = (info, mixed, local, d_sums, carried, *arrived_back, query_table, key_table, tokens, attended, d_branch)
    d_mixed_a, d_bias_a, keep_a, send_a = call(
        functools.partial(mix_back_kernel, 0), mix_outs + (mix_like,), [SMEM] + [VMEM] * 12, mix_scratch,
        after=feed_last, limit=19, cost=11,
    )(*mix_inputs)
    got_a = places.swap(send_a, CORE)
    d_mixed_b, d_bias_b, keep_b, send_b, vector_rows = call(
        functools.partial(mix_back_kernel, 2),
        mix_outs + (shaped((4 * rows + 8, 2 * width), BF16), shaped((16, width), BF16)), [SMEM] + [VMEM] * 16,
        mix_scratch, limit=19, cost=11,
    )(*mix_inputs, vectors_one, vectors_two, d_bias_in, d_bias_a)
    feed_rows = added(places, feed_own, 2 * rows, after=(d_mixed_b,))
    got_a, got_b = later(got_a, feed_rows), places.swap(later(send_b, feed_rows), CORE)
    row_like = shaped((16, width), BF16)
    keep0, send0, keep1, send1, vector_rows = call(
        first_pairs_kernel, halves_like(4 * rows, width, 16) + (row_like,), [VMEM] * 5,
    )(keep_a, got_a, keep_b, got_b, vector_rows)
    got = swap_all(places, (send0, send1), (X, Y))
    feed_four = spread_chips(places, later(feed_rows, (send0, send1)))
    d_tokens = call(
        tokens_back_kernel, shaped((count, width), BF16), [VMEM] * 4, after=(send0, send1), limit=9, cost=6,
    )(d_mixed_a, d_mixed_b, mix_weight, d_r1)
    keep0, send0, keep1, send1, vector_rows = call(
        mix_next_kernel, halves_like(2 * rows, width, 16) + (row_like,), [VMEM] * 5, after=(d_tokens,),
    )(keep0, keep1, *got, vector_rows)
    got = swap_all(places, (send0, send1), (Y, X))
    mix_last = call(
        mix_last_kernel, (shaped((rows + 8, width), BF16),) * tensor, [VMEM] * 5,
    )(keep0, keep1, *got, vector_rows)
    mix_own = turn_back(places, mix_last)
    feed_all = spread_cores(places, later(feed_four, (send0, send1)))

    held = pltpu.VMEM((width, width), F32)
    d_w_in, d_w_two = call(
        finish_feed_kernel, (shaped((width, width), F32),) * 2, [SMEM] + [VMEM] * 5, [held], limit=10, cost=4,
    )(info, *feed_all)
    mix_rows = added(places, mix_own, rows, after=(d_w_in,))
    d_w_qkv, d_w_out = call(
        finish_mix_kernel, (shaped((wide, width), F32), shaped((192, width), F32)), [SMEM] + [VMEM] * 5, [held], limit=7, cost=3,
    )(info, *spread_cores(places, spread_chips(places, mix_rows)))

    ends = jnp.stack([part[rows:] for part in mix_own])
    ends = lax.dynamic_slice_in_dim(jnp.concatenate([ends, ends]), tensor - places.z, tensor, 0)
    summed = over_groups(places, jnp.sum(ends.astype(F32), axis=0))
    d_gain_one, d_shift_one, d_b_out, d_gain_two, d_shift_two, d_b_two = (summed[k] for k in range(6))
    d_b_qkv, d_b_in = summed[6, :wide], summed[7]
    return (block_out, d_tokens, d_w_qkv.T, d_b_qkv, d_w_out, d_b_out, d_gain_one, d_shift_one, d_w_in, d_b_in,
            d_w_two, d_b_two, d_gain_two, d_shift_two)


def solution(mesh):
    sizes = dict(mesh.shape)
    rows = P(("dp", "tensor"), None)
    wide, tall, cut, whole = P(None, "tensor"), P("tensor", None), P("tensor"), P()
    in_specs = (rows, P("dp", None), wide, cut, tall, whole, whole, whole, wide, cut, tall, whole, whole, whole, rows)
    out_specs = (rows, rows, wide, cut, tall, whole, whole, whole, wide, cut, tall, whole, whole, whole)
    return jax.shard_map(
        functools.partial(on_device, sizes["dp"], sizes["tensor"]),
        mesh=mesh, in_specs=in_specs, out_specs=out_specs, check_vma=False,
    )
```

```python
import functools
import math

import jax
import jax.numpy as jnp
from jax import lax
from jax.experimental import pallas as pl
from jax.experimental.pallas import tpu as pltpu
from jax.sharding import PartitionSpec as P

HEAD = 64
ROW_LEN = 2048
DOCS = 8
F32 = jnp.float32
BF16 = jnp.bfloat16
NN = ((1,), (0,))
NT = ((1,), (1,))
TN = ((0,), (0,))
STATE = 80
COST = 0.2 * 1.15e9
VMEM = pl.BlockSpec(memory_space=pltpu.VMEM)
SMEM = pl.BlockSpec(memory_space=pltpu.SMEM)
ANY = pl.BlockSpec(memory_space=pl.ANY)


def dot(left, right, dims=NN):
    return lax.dot_general(left, right, (dims, ((), ())), preferred_element_type=F32)


def call(body, outs, specs, scratch=(), limit=6, after=(), cost=0):
    n = len(specs)

    def waiting_body(*refs):
        body(*refs[:n], *refs[n + len(after):])

    return lambda *operands: pl.pallas_call(
        waiting_body,
        out_shape=outs,
        in_specs=list(specs) + [ANY] * len(after),
        out_specs=jax.tree.map(lambda _: VMEM, outs),
        scratch_shapes=scratch,
        cost_estimate=pl.CostEstimate(flops=1 + int(cost * COST), bytes_accessed=1, transcendentals=0),
        compiler_params=pltpu.CompilerParams(vmem_limit_bytes=limit << 20),
    )(*operands, *after)


def shaped(shape, dtype):
    return jax.ShapeDtypeStruct(shape, dtype)


class Places:
    def __init__(self, dp, tensor):
        self.dp, self.tensor = dp, tensor
        self.row = lax.axis_index("dp")
        self.z = lax.axis_index("tensor")
        self.piece = self.row & 7

    def swap(self, value, mask):
        return lax.ppermute(value, "dp", [(d, d ^ mask) for d in range(self.dp)])

    def turn(self, value, step):
        size = self.tensor
        return lax.ppermute(value, "tensor", [(k, (k + step) % size) for k in range(size)])

    def onward(self, value, step):
        size = self.tensor
        pairs = [(k, k + step) for k in range(size) if 0 <= k + step < size]
        return lax.ppermute(value, "tensor", pairs)


CORE, X, Y = 1, 2, 4
BUFFERS = ((0, (0, 2)), (0, (4, 6)), (0, (1, 3)), (0, (5, 7)), (2, (0, 4)), (2, (2, 6)), (2, (1, 5)), (2, (3, 7)))


def stacked(*groups, after=()):
    sizes = [len(group) for group in groups]

    def body(*refs):
        sources, targets = list(refs[:sum(sizes)]), refs[sum(sizes):]
        for size, target in zip(sizes, targets, strict=True):
            for k in range(size):
                target[k] = sources.pop(0)[...]

    outs = tuple(shaped((len(group),) + group[0].shape, group[0].dtype) for group in groups)
    flat = [value for group in groups for value in group]
    return call(body, outs, [VMEM] * len(flat), after=after)(*flat)


def mix_pieces_kernel(first, second, third, fourth, a, b, bias_qkv, bias_in):
    rows, wide = a.shape[1], bias_qkv.shape[2]
    for j, part in enumerate((first, second, third, fourth)):
        (a, b)[j // 2][j % 2] = part[0:rows]
        extra = part[rows:].astype(F32)
        bias_qkv[j] = extra[0:1, :wide]
        bias_in[j] = extra[1:2]


def swap_halves(places, a, b):
    return places.swap(a, X), places.swap(b, Y)


def gather_rest(places, a, b, a2, b2):
    near, far = stacked((a, b)), stacked((a2, b2))
    return a, a2, b, b2, places.swap(near[0], CORE), places.swap(far[0], CORE)


def start_placing(piece, buffers, targets, sems):
    copies = []
    a, a2, b, b2, near, far = buffers
    buffers = (a, a2, near.at[0], far.at[0], b, b2, near.at[1], far.at[1])
    for buffer, (shard, pieces) in zip(buffers, BUFFERS, strict=True):
        for k, other in enumerate(pieces):
            for at, target, first_row, rows in targets:
                spot = pl.multiple_of(first_row + (piece ^ other) * rows, 8)
                copies.append(pltpu.make_async_copy(
                    buffer.at[k, :, at:at + rows, :],
                    target.at[shard:shard + 2, pl.ds(spot, rows), :],
                    sems.at[len(copies)],
                ))
    for copy in copies:
        copy.start()
    half = len(copies) // 2
    return copies[:half], copies[half:]


def wait_all(copies):
    for copy in copies:
        copy.wait()


def doubled(part):
    return jnp.concatenate([part, part], axis=1)


def with_one(value):
    lanes = lax.broadcasted_iota(jnp.int32, (value.shape[0], 2 * HEAD), 1)
    return jnp.where(lanes < HEAD, doubled(value.astype(F32)), (lanes == HEAD).astype(F32)).astype(BF16)


def head_parts(mixed_ref, shard, head):
    at = head * 3 * HEAD
    return tuple(mixed_ref[shard, :, at + t * HEAD:at + (t + 1) * HEAD] for t in range(3))


def causal_blocks(count):
    half = count // 2
    return ((0, half, 0, half), (half, count, 0, count))


def mix_kernel(info, tokens, bias, key_table, *refs):
    buffers, (mixed_out, state_out, weight), sems = refs[:6], refs[6:9], refs[9]
    wide = mixed_out.shape[2]
    tall = weight.shape[1] - wide
    halves = start_placing(
        info[0], buffers, ((0, weight, 0, wide // 8), (wide // 8, weight, wide, tall // 8)), sems)

    def shard_step(j, carry):
        mixed = dot(tokens[...], weight[j, 0:wide], NT) + bias[j]
        lanes = lax.broadcasted_iota(jnp.int32, mixed.shape, 1)
        mixed_out[j] = jnp.where(lanes % 192 >= 128, mixed, jnp.maximum(mixed, 0.0)).astype(BF16)
        for h in range(3):
            _, key, value = head_parts(mixed_out, j, h)
            feats = (doubled(key).astype(F32) * key_table[...]).astype(BF16)
            state_out[j, h] = dot(with_one(value), feats, TN)[:STATE].astype(BF16)
        return carry

    for k, half in enumerate(halves):
        wait_all(half)
        lax.fori_loop(2 * k, 2 * k + 2, shard_step, 0)


def local_kernel(mixed, mask, sums_out):
    def shard_step(j, carry):
        for h in range(3):
            query, key, value = head_parts(mixed, j, h)
            value = with_one(value)
            for r0, r1, c0, c1 in causal_blocks(mask.shape[0]):
                scores = (dot(query[r0:r1], key[c0:c1], NT) * mask[r0:r1, c0:c1]).astype(BF16)
                sums_out[j, h, r0:r1] = dot(scores, value[c0:c1])
        return carry

    lax.fori_loop(0, mixed.shape[0], shard_step, 0)


def norm_parts(rows_in):
    centred = rows_in - jnp.mean(rows_in, axis=-1, keepdims=True)
    spread = jnp.mean(centred * centred, axis=-1, keepdims=True)
    scale = lax.rsqrt(spread + 1e-05)
    return centred * scale, scale


def norm_back(grad, normed, scale, gain):
    e = grad * gain
    d_rows = scale * (
        e
        - jnp.mean(e, axis=-1, keepdims=True)
        - normed * jnp.mean(e * normed, axis=-1, keepdims=True)
    )
    return d_rows, jnp.sum(grad * normed, axis=0, keepdims=True), jnp.sum(grad, axis=0, keepdims=True)


def join_kernel(info, sums, arrived1, arrived2, arrived3, mixed, query_table, tokens, weight, b_out, gain, shift,
                attended, carried, dens, first, normed_out, scale_out):
    shards = mixed.shape[0]
    for j in range(shards):
        total = None
        for step, arrived in enumerate((arrived1, arrived2, arrived3), 1):
            linked = info[step].astype(F32) * arrived[(j - step) % shards].astype(F32)
            total = linked if total is None else total + linked
        carried[j] = total.astype(BF16)

    def shard_step(j, branch):
        lanes = lax.broadcasted_iota(jnp.int32, (tokens.shape[0], 128), 1)
        kept = jnp.zeros((tokens.shape[0], 128), F32)
        for h in range(3):
            query = head_parts(mixed, j, h)[0]
            feats = (doubled(query).astype(F32) * query_table[...]).astype(BF16)
            total = sums[j, h][:, :STATE] + dot(feats, carried[j, h], NT)
            den = total[:, HEAD:HEAD + 1]
            inverse = 1.0 / jnp.maximum(den, 1.0)
            attended[j, :, h * HEAD:(h + 1) * HEAD] = (total[:, :HEAD] * inverse).astype(BF16)
            kept = jnp.where(lanes == h, inverse, kept)
            kept = jnp.where(lanes == 8 + h, jnp.where(den > 1.0, inverse, 0.0), kept)
        dens[j] = kept
        return branch + dot(attended[j], weight[j, weight.shape[1] - 192:])

    branch = lax.fori_loop(0, shards, shard_step, jnp.zeros(tokens.shape, F32))
    normed, scale = norm_parts(tokens[...].astype(F32) + branch + b_out[...])
    normed_out[...] = normed
    scale_out[...] = jnp.broadcast_to(scale, scale_out.shape)
    first[...] = (normed * gain[...] + shift[...]).astype(BF16)


def gelu_parts(v):
    k = math.sqrt(2 / math.pi)
    square = v * v
    t = jnp.tanh(v * (k + k * 0.044715 * square))
    half = 0.5 * v
    bent = half * t
    slope = (0.5 + 0.5 * t) + (half - bent * t) * (k + 3 * k * 0.044715 * square)
    return half + bent, slope


def rows_ordered(turned, piece, order):
    rows = turned.shape[0] // 8
    return jnp.concatenate(
        [turned[pl.ds(pl.multiple_of((piece ^ other) * rows, rows), rows), :] for other in order], axis=0)


ROUTES = ((0, 4, 2, 6), (0, 2, 4, 6))


def order_rows(ordered, turned, piece):
    for route, order in enumerate(ROUTES):
        for sends in range(2):
            ordered[2 * route + sends] = rows_ordered(turned, piece, tuple(other + sends for other in order))


def columns(j, width):
    return pl.ds(pl.multiple_of(j * width, 128), width)


def feed_kernel(info, first, bias, b_two, gain, shift, cotangent, *refs):
    buffers = refs[:6]
    slope, block_out, d_second_out, d_r2_out, vectors, *grads = refs[6:13]
    w_in, w_two, active, turned, ordered, total, sems = refs[13:]
    shards, width = w_in.shape[0], w_in.shape[2]
    rows = width // 8
    halves = start_placing(info[0], buffers, ((0, w_in, 0, rows), (rows, w_two, 0, rows)), sems)
    total[...] = jnp.broadcast_to(b_two[...], total.shape)

    def forward_step(j, carry):
        half = first.shape[0] // 2
        spans = slice(0, half), slice(half, 2 * half)
        hidden = [dot(first[span], w_in[j]) + bias[j] for span in spans]
        for span, part in zip(spans, hidden, strict=True):
            act, bend = gelu_parts(part)
            act = act.astype(BF16)
            active[j, span] = act
            slope[j, span] = bend.astype(BF16)
            total[span] += dot(act, w_two[j])
        return carry

    for k, half in enumerate(halves):
        wait_all(half)
        lax.fori_loop(2 * k, 2 * k + 2, forward_step, 0)
    normed, scale = norm_parts(first[...].astype(F32) + total[...])
    block_out[...] = (normed * gain[...] + shift[...]).astype(BF16)
    d_r2, d_gain, d_shift = norm_back(cotangent[...].astype(F32), normed, scale, gain[...])
    d_r2_out[...] = d_r2
    d_second = d_r2.astype(BF16)
    d_second_out[...] = d_second
    turned[...] = d_second.T
    vectors[0:1] = d_gain
    vectors[1:2] = d_shift
    vectors[2:3] = jnp.sum(d_second.astype(F32), axis=0, keepdims=True)
    vectors[3:] = jnp.zeros((5, vectors.shape[1]), F32)
    order_rows(ordered, turned, info[0])

    def grad_step(j, carry):
        for sends in range(2):
            grads[sends][:, columns(j, width)] = dot(ordered[2 * (j // 2) + sends], active[j]).astype(BF16)
        return carry

    lax.fori_loop(0, shards, grad_step, 0)


def feed_back_kernel(info, first, d_second, slope, *refs):
    buffers = refs[:6]
    d_hidden, d_bias, *grads = refs[6:10]
    w_two, turned, ordered, sems = refs[10:]
    shards, width = w_two.shape[0], w_two.shape[2]
    rows = width // 8
    halves = start_placing(info[0], buffers, ((rows, w_two, 0, rows),), sems)
    turned[...] = first[...].T
    order_rows(ordered, turned, info[0])

    def step(j, carry):
        d_active = dot(d_second[...], w_two[j], NT)
        d_h = (d_active * slope[j].astype(F32)).astype(BF16)
        d_hidden[j] = d_h
        d_bias[j] = jnp.broadcast_to(jnp.sum(d_h.astype(F32), axis=0, keepdims=True), d_bias.shape[1:])
        for sends in range(2):
            grads[sends][:, columns(j, width)] = dot(ordered[2 * (j // 2) + sends], d_hidden[j]).astype(BF16)
        return carry

    for k, half in enumerate(halves):
        wait_all(half)
        lax.fori_loop(2 * k, 2 * k + 2, step, 0)


def first_back_kernel(info, d_hidden, d_r2, normed, scale, gain, *refs):
    buffers = refs[:6]
    d_r1_out, d_branch_out, vectors = refs[6:9]
    w_in, total, sems = refs[9:]
    rows = w_in.shape[1] // 8
    halves = start_placing(info[0], buffers, ((0, w_in, 0, rows),), sems)
    total[...] = d_r2[...]

    def first_step(j, carry):
        total[...] += dot(d_hidden[j], w_in[j], NT)
        return carry

    for k, half in enumerate(halves):
        wait_all(half)
        lax.fori_loop(2 * k, 2 * k + 2, first_step, 0)
    d_r1, d_gain, d_shift = norm_back(total[...], normed[...], scale[:, 0:1], gain[...])
    d_r1_out[...] = d_r1
    d_branch = d_r1.astype(BF16)
    d_branch_out[...] = d_branch
    vectors[0:1] = d_gain
    vectors[1:2] = d_shift
    vectors[2:3] = jnp.sum(d_branch.astype(F32), axis=0, keepdims=True)
    vectors[3:] = jnp.zeros((5, vectors.shape[1]), F32)


def heads_back_kernel(d_branch, weight, attended, dens, mixed, query_table, d_sums, d_carried):
    def shard_step(j, carry):
        g_all = dot(d_branch[...], weight[j, weight.shape[1] - 192:], NT)
        lanes = lax.broadcasted_iota(jnp.int32, (d_branch.shape[0], 128), 1)
        for h in range(3):
            g = g_all[:, h * HEAD:(h + 1) * HEAD]
            o = attended[j, :, h * HEAD:(h + 1) * HEAD].astype(F32)
            inverse, inverse_if = dens[j, :, h:h + 1], dens[j, :, 8 + h:9 + h]
            d_den = -jnp.sum(g * o, axis=-1, keepdims=True) * inverse_if
            d_num = doubled(g * inverse)
            both = jnp.where(lanes < HEAD, d_num, jnp.where(lanes == HEAD, d_den, 0.0)).astype(BF16)
            d_sums[j, h] = both
            query = head_parts(mixed, j, h)[0]
            feats = (doubled(query).astype(F32) * query_table[...]).astype(BF16)
            d_carried[j, h] = dot(both, feats, TN)[:STATE].astype(BF16)
        return carry

    lax.fori_loop(0, mixed.shape[0], shard_step, 0)


def local_back_kernel(mixed, d_sums, mask, mask_t, d_mixed):
    def shard_step(j, carry):
        for h in range(3):
            query, key, value = head_parts(mixed, j, h)
            value = with_one(value)
            grad = d_sums[j, h]
            at = h * 3 * HEAD
            for r0, r1, c0, c1 in causal_blocks(mask.shape[0]):
                d_scores = (dot(grad[r0:r1], value[c0:c1], NT) * mask[r0:r1, c0:c1]).astype(BF16)
                d_mixed[j, r0:r1, at:at + HEAD] = dot(d_scores, key[c0:c1])
            half = mask.shape[0] // 2
            for c0, c1, r0 in ((0, half, 0), (half, 2 * half, half)):
                turned = mask_t[c0:c1, r0:]
                d_scores = (dot(value[c0:c1], grad[r0:], NT) * turned).astype(BF16)
                d_mixed[j, c0:c1, at + HEAD:at + 2 * HEAD] = dot(d_scores, query[r0:])
                scores = (dot(key[c0:c1], query[r0:], NT) * turned).astype(BF16)
                d_mixed[j, c0:c1, at + 2 * HEAD:at + 3 * HEAD] = dot(scores, grad[r0:])[:, :HEAD]
        return carry

    lax.fori_loop(0, mixed.shape[0], shard_step, 0)


def mix_back_kernel(base, info, mixed, local, d_sums, carried, arrived1, arrived2, arrived3, query_table, key_table,
                    tokens, attended, d_branch, *refs):
    last = base > 0
    sources, refs = (refs[:4], refs[4:]) if last else ((), refs)
    d_mixed, d_bias, *grads = refs[:4]
    turned, turned_branch, state, held, middles = refs[-5:]
    shards, wide = mixed.shape[0], mixed.shape[2]
    width = d_mixed.shape[2]
    turned[...] = tokens[...].T
    turned_branch[...] = d_branch[...].T
    for k in range(2):
        total = None
        for step, arrived in enumerate((arrived1, arrived2, arrived3), 1):
            linked = info[3 + step].astype(F32) * arrived[(base + k + step) % shards].astype(F32)
            total = linked if total is None else total + linked
        state[k] = total.astype(BF16)

    def folded(both):
        return both[:, :HEAD] + both[:, HEAD:]

    def shard_step(k, carry):
        j = base + k
        parts = []
        for h in range(3):
            query, key, value = head_parts(mixed, j, h)
            at = h * 3 * HEAD
            spans = [slice(at + t * HEAD, at + (t + 1) * HEAD) for t in range(3)]
            d_query = folded(dot(d_sums[j, h][:, :STATE], carried[j, h]) * query_table[...])
            d_query = jnp.where(query.astype(F32) > 0, local[j, :, spans[0]] + d_query, 0.0)
            d_key = folded(dot(with_one(value)[:, :STATE], state[k, h]) * key_table[...])
            d_key = jnp.where(key.astype(F32) > 0, local[j, :, spans[1]] + d_key, 0.0)
            feats = (doubled(key).astype(F32) * key_table[...]).astype(BF16)
            d_value = local[j, :, spans[2]] + dot(feats, state[k, h], NT)[:, :HEAD]
            parts += [d_query, d_key, d_value]
        whole = jnp.concatenate(parts + [attended[j].astype(F32)], axis=1).astype(BF16)
        d_mixed[k] = whole
        middles[k] = jnp.concatenate([parts[-1], attended[j][:, :HEAD].astype(F32)], axis=1)
        d_bias[k] = jnp.broadcast_to(jnp.sum(d_mixed[k].astype(F32), axis=0, keepdims=True), d_bias.shape[1:])
        return carry

    lax.fori_loop(0, 2, shard_step, 0)
    rows = grads[0].shape[0]
    low = wide // 128 * 128
    for k in range(2):
        lanes = lax.broadcasted_iota(jnp.int32, (d_mixed.shape[1], 128), 1)
        middle = middles[k]
        left_side = jnp.where(lanes < HEAD, middle, 0.0).astype(BF16)
        right_side = jnp.where(lanes < HEAD, 0.0, middle).astype(BF16)
        left_side = jnp.concatenate([d_mixed[k][:, :low], left_side], axis=1)
        right_side = jnp.concatenate([right_side, d_mixed[k][:, low + 128:]], axis=1)
        for sends in (1, 0):
            out, at = grads[sends], k * width
            order = tuple(other + sends for other in ROUTES[k])
            left = dot(rows_ordered(turned, info[0], order), left_side)
            right = dot(rows_ordered(turned_branch, info[0], order), right_side)
            out[0:rows, at:at + low] = left[:, :low].astype(BF16)
            out[0:rows, at + low:at + low + 128] = (left[:, low:] + right[:, :128]).astype(BF16)
            out[0:rows, at + low + 128:at + width] = right[:, 128:].astype(BF16)
    if last:
        one, two, bias_in, bias_first = sources
        vectors = refs[4]
        held[0:3] = one[0:3]
        held[3:6] = two[0:3]
        for j in range(shards):
            held[6 + 2 * j:7 + 2 * j] = bias_first[j, 0:1] if j < 2 else d_bias[j - 2, 0:1]
            held[7 + 2 * j:8 + 2 * j] = bias_in[j, 0:1]
        held[14:16] = jnp.zeros((2, width), F32)
        low_rows = held[...].astype(BF16)
        vectors[...] = low_rows
        grads[1][rows:, 0:width] = low_rows[0:8]
        grads[1][rows:, width:] = low_rows[8:16]


def tokens_back_kernel(d_mixed_a, d_mixed_b, weight, d_r1, d_tokens):
    wide = weight.shape[1] - 192
    total = d_r1[...]
    for j in range(weight.shape[0]):
        d_mixed = (d_mixed_a, d_mixed_b)[j // 2]
        total = total + dot(d_mixed[j % 2][:, :wide], weight[j, 0:wide])
    d_tokens[...] = total.astype(BF16)


def later(values, others):
    return lax.optimization_barrier((values, others))[0]


def halves_like(rows, width, extra=0):
    keep, send = shaped((rows, width), F32), shaped((rows, width), BF16)
    return keep, send, keep, shaped((rows + extra, width), BF16)


def first_halves_kernel(keep, got, *outs):
    half, width = outs[0].shape
    for k in range(2):
        cols = slice(k * width, (k + 1) * width)
        outs[2 * k][...] = keep[0:half, cols].astype(F32) + got[0:half, cols].astype(F32)
        send = keep[half:2 * half, cols].astype(F32) + got[half:2 * half, cols].astype(F32)
        outs[2 * k + 1][0:half] = send.astype(BF16)


def first_pairs_kernel(keep_a, got_a, keep_b, got_b, mine, *outs):
    half, width = outs[0].shape[0] // 2, outs[0].shape[1]
    for k in range(2):
        cols = slice(k * width, (k + 1) * width)
        for t, (keep, got) in enumerate(((keep_a, got_a), (keep_b, got_b))):
            spots = slice(t * half, (t + 1) * half)
            outs[2 * k][spots] = keep[0:half, cols].astype(F32) + got[0:half, cols].astype(F32)
            send = keep[half:2 * half, cols].astype(F32) + got[half:2 * half, cols].astype(F32)
            outs[2 * k + 1][spots] = send.astype(BF16)
        rows = mine[8 * k:8 * k + 8].astype(F32) + got_b[2 * half:, cols].astype(F32)
        outs[4][8 * k:8 * k + 8] = rows.astype(BF16)
        outs[3][2 * half + 8 * k:2 * half + 8 * k + 8] = rows.astype(BF16)


def next_halves_kernel(keep0, keep1, got0, got1, *outs):
    half = outs[0].shape[0]
    for k, (keep, got) in enumerate(((keep0, got0), (keep1, got1))):
        outs[2 * k][...] = keep[0:half] + got[0:half].astype(F32)
        outs[2 * k + 1][...] = (keep[half:] + got[half:].astype(F32)).astype(BF16)


def ends_kernel(keep0, keep1, got0, got1, end0, end1):
    end0[...] = (keep0[...] + got0[...].astype(F32)).astype(BF16)
    end1[...] = (keep1[...] + got1[...].astype(F32)).astype(BF16)


def feed_last_kernel(keep0, keep1, got0, got1, two0, two1, *outs):
    rows, width = outs[0].shape[0] // 2, outs[0].shape[1]
    for j, out in enumerate(outs):
        keep, got, two = (keep0, got0, two0) if j < 2 else (keep1, got1, two1)
        cols = slice(j % 2 * width, (j % 2 + 1) * width)
        out[0:rows] = (keep[:, cols] + got[:, cols].astype(F32)).astype(BF16)
        out[rows:] = two[:, cols]


def mix_next_kernel(keep0, keep1, got0, got1, mine, *outs):
    half = outs[0].shape[0] // 2
    for k, (keep, got) in enumerate(((keep0, got0), (keep1, got1))):
        for t in range(2):
            at = 2 * t * half
            spots = slice(t * half, (t + 1) * half)
            outs[2 * k][spots] = keep[at:at + half] + got[at:at + half].astype(F32)
            send = keep[at + half:at + 2 * half] + got[at + half:at + 2 * half].astype(F32)
            outs[2 * k + 1][spots] = send.astype(BF16)
    rows = (mine[...].astype(F32) + got1[4 * half:].astype(F32)).astype(BF16)
    outs[4][...] = rows
    outs[3][2 * half:] = rows


def mix_last_kernel(keep0, keep1, got0, got1, mine, *outs):
    half = keep0.shape[0] // 2
    rows = (mine[...].astype(F32) + got1[2 * half:].astype(F32)).astype(BF16)
    for j, out in enumerate(outs):
        keep, got = (keep0, got0) if j % 2 == 0 else (keep1, got1)
        spots = slice(j // 2 * half, (j // 2 + 1) * half)
        out[0:half] = (keep[spots] + got[spots].astype(F32)).astype(BF16)
        out[half:half + 6] = rows[0:6]
        out[half + 6:half + 8] = rows[6 + 2 * j:8 + 2 * j]


def swap_all(places, values, masks):
    return [places.swap(value, mask) for value, mask in zip(values, masks, strict=True)]


def turn_back(places, parts):
    return [parts[0]] + [places.turn(parts[s], -s) for s in range(1, places.tensor)]


def pair_sum(mine, other):
    return (mine.astype(F32) + other.astype(F32)).astype(BF16)


def over_groups(places, total):
    mask = 8
    while mask < places.dp:
        total = total + places.swap(total, mask)
        mask *= 2
    return total


def added(places, values, rows, after=()):
    kind = BF16 if places.dp == 8 else F32

    def body(*refs):
        total = refs[0][0:rows].astype(F32)
        for other in refs[1:-1]:
            total = total + other[0:rows].astype(F32)
        refs[-1][...] = total.astype(kind)

    total = call(body, shaped((rows, values[0].shape[1]), kind), [VMEM] * len(values), after=after)(*values)
    return over_groups(places, total).astype(BF16)


def spread_chips(places, own):
    return [own, places.swap(own, X), places.swap(own, Y), places.swap(own, X + Y)]


def spread_cores(places, four):
    return list(four) + [places.swap(stacked(four)[0], CORE)]


def place_rows(piece, pieces, targets):
    for k in range(8):
        source = pieces[k // 2] if k % 2 == 0 else pieces[4].at[k // 2]
        for t, target in enumerate(targets):
            rows = target.shape[0] // 8
            spot = pl.multiple_of((piece ^ k) * rows, rows)
            target[pl.ds(spot, rows), :] = source[t * rows:(t + 1) * rows].astype(F32)


def finish_feed_kernel(info, own, x, y, xy, core, d_in, d_two, held):
    place_rows(info[0], (own, x, y, xy, core), (d_in, held))
    d_two[...] = held[...].T


def finish_mix_kernel(info, own, x, y, xy, core, d_qkv, d_out, held):
    place_rows(info[0], (own, x, y, xy, core), (held,))
    turned = held[...].T
    d_qkv[...] = turned[0:d_qkv.shape[0]]
    d_out[...] = turned[d_qkv.shape[0]:]


def doc_tables(starts_row, base, count):
    spots = base + jnp.arange(count, dtype=jnp.int32)
    started = (spots[:, None] >= starts_row[None, :]).astype(jnp.int32)
    doc_ids = jnp.sum(started, axis=1) - 1
    onehot = (doc_ids[:, None] == jnp.arange(DOCS, dtype=jnp.int32)[None, :]).astype(jnp.int32)
    finish = jnp.concatenate([starts_row[1:], jnp.full((1,), ROW_LEN, jnp.int32)])
    own_start = jnp.sum(onehot * starts_row[None, :], axis=1)
    own_len = jnp.sum(onehot * (finish - starts_row)[None, :], axis=1)
    angles = 0.5 * math.pi * (spots - own_start).astype(F32) / own_len.astype(F32)
    return angles, doc_ids


def doc_at(starts_row, spot):
    return jnp.sum((spot >= starts_row).astype(jnp.int32)) - 1


def on_device(dp, tensor, tokens, starts, w_qkv, b_qkv, w_out, b_out, gain_one, shift_one, w_in, b_in,
              w_two, b_two, gain_two, shift_two, cotangent):
    places = Places(dp, tensor)
    count, width = tokens.shape
    piece = places.piece
    line = lambda a: a.astype(F32).reshape(1, -1)
    sems = lambda n: pltpu.SemaphoreType.DMA((n,))

    def own_rows(weight):
        rows = weight.shape[0] // 8
        return lax.dynamic_slice_in_dim(weight, piece * rows, rows, 0)

    rows = width // 8
    wide = w_qkv.shape[1]
    bias_rows = jnp.pad(b_qkv.reshape(1, wide), ((0, 7), (0, width - wide))) + jnp.pad(b_in.reshape(1, width), ((1, 6), (0, 0)))
    mix_piece = jnp.concatenate([own_rows(w_qkv.T), own_rows(w_out), bias_rows])
    feed_piece = jnp.concatenate([own_rows(w_in), own_rows(w_two)])
    mix_parts = [mix_piece] + [places.turn(mix_piece, s) for s in range(1, tensor)]
    feed_parts = [feed_piece] + [places.turn(feed_piece, s) for s in range(1, tensor - 1)]
    feed_parts.append(places.turn(later(feed_piece, mix_parts), tensor - 1))
    pair = shaped((2, rows, width), BF16)
    mix_a, mix_b, bias_qkv, bias_in = call(
        mix_pieces_kernel, (pair, pair, shaped((tensor, 1, wide), F32), shaped((tensor, 1, width), F32)), [VMEM] * 4,
    )(*mix_parts)
    near_x, near_y = swap_halves(places, mix_a, mix_b)
    mix_ax, mix_by = stacked((mix_a, near_x), (mix_b, near_y))
    mix_buffers = gather_rest(places, mix_ax, mix_by, places.swap(mix_ax, Y), places.swap(mix_by, X))
    feed_a, feed_b = stacked(feed_parts[:2], feed_parts[2:], after=(mix_ax, mix_by))
    near_x, near_y = swap_halves(places, feed_a, feed_b)

    row = starts[0]
    base = places.z * count
    angles, docs = doc_tables(row, base, count)
    first_doc, last_doc = doc_at(row, base), doc_at(row, base + count - 1)
    links = [doc_at(row, base - (s - 1) * count - 1) == first_doc for s in range(1, tensor)]
    links += [doc_at(row, base + s * count) == last_doc for s in range(1, tensor)]
    info = jnp.stack([piece] + [link.astype(jnp.int32) for link in links] + [piece])
    spot = jnp.arange(count)
    cosine, sines = jnp.cos(angles), jnp.sin(angles)
    turn = cosine[:, None] * cosine[None, :] + sines[:, None] * sines[None, :]
    same = docs[:, None] == docs[None, :]
    mask = jnp.where(same & (spot[:, None] >= spot[None, :]), turn, 0.0)
    mask_t = jnp.where(same & (spot[:, None] <= spot[None, :]), turn, 0.0)
    lanes = jnp.arange(2 * HEAD)[None, :]
    table = jnp.where(lanes < HEAD, cosine[:, None], sines[:, None])
    query_table = jnp.where((docs == first_doc)[:, None], table, 0.0)
    key_table = jnp.where((docs == last_doc)[:, None], table, 0.0)

    states = shaped((tensor, 3, STATE, 2 * HEAD), BF16)
    mixed, state, mix_weight = call(
        mix_kernel,
        (shaped((tensor, count, wide), BF16), states, shaped((tensor, width, width), BF16)),
        [SMEM, VMEM, VMEM, VMEM] + [ANY] * 6, [sems(32)], after=(mask, mask_t), limit=9, cost=8,
    )(info, tokens, bias_qkv, key_table, *mix_buffers)
    per_head = shaped((tensor, 3, count, 2 * HEAD), F32)
    arrived = [places.onward(state, s) for s in range(1, tensor)]
    per_head = shaped((tensor, 3, count, 2 * HEAD), F32)
    feed_ax, feed_by = stacked((feed_a, near_x), (feed_b, near_y), after=(state,))
    near_sums = call(local_kernel, per_head, [VMEM, VMEM], after=(feed_ax, feed_by), limit=6, cost=7)(mixed, mask)
    feed_far = places.swap(feed_ax, Y), places.swap(feed_by, X)
    attended, carried, dens, first, normed, scale = call(
        join_kernel,
        (shaped((tensor, count, 192), BF16), states, shaped((tensor, count, 128), F32), shaped((count, width), BF16),
         shaped((count, width), F32), shaped((count, 128), F32)),
        [SMEM] + [VMEM] * 11, limit=18, cost=100,
    )(info, near_sums, *arrived, mixed, query_table, tokens, mix_weight, line(b_out), line(gain_one), line(shift_one))
    feed_buffers = gather_rest(places, *later((feed_ax, feed_by, *feed_far), first))
    hidden_like = shaped((tensor, count, width), BF16)
    vectors = shaped((8, width), F32)
    grad_like = shaped((4 * rows, tensor * width), BF16)
    square = pltpu.VMEM((tensor, width, width), BF16)
    turned = pltpu.VMEM((width, count), BF16)
    ordered = pltpu.VMEM((4, 4 * rows, count), BF16)
    total_scratch = pltpu.VMEM((count, width), F32)
    slope, block_out, d_second, d_r2, vectors_two, two_keep, two_send = call(
        feed_kernel,
        (hidden_like, shaped((count, width), BF16), shaped((count, width), BF16),
         shaped((count, width), F32), vectors, grad_like, grad_like),
        [SMEM] + [VMEM] * 6 + [ANY] * 6, [square, square, pltpu.VMEM(hidden_like.shape, BF16), turned, ordered, total_scratch, sems(32)], limit=33, cost=19,
    )(info, first, bias_in, line(b_two), line(gain_two), line(shift_two), cotangent, *feed_buffers)

    got = places.swap(two_send, CORE)
    d_hidden, d_bias_in, in_keep, in_send = call(
        feed_back_kernel, (hidden_like, shaped((tensor, 8, width), F32), grad_like, grad_like),
        [SMEM] + [VMEM] * 3 + [ANY] * 6, [square, turned, ordered, sems(16)], limit=19, cost=14,
    )(info, first, d_second, slope, *feed_buffers)
    wide_halves = halves_like(2 * rows, 2 * width)
    keep0, send0, keep1, send1 = call(first_halves_kernel, wide_halves, [VMEM] * 2, after=(in_send,))(two_keep, got)
    got_two, got_in = swap_all(places, (send0, send1), (X, Y)), places.swap(in_send, CORE)
    d_r1, d_branch, vectors_one = call(
        first_back_kernel,
        (shaped((count, width), F32), shaped((count, width), BF16), vectors),
        [SMEM] + [VMEM] * 5 + [ANY] * 6, [square, total_scratch, sems(16)], after=(send0, send1), limit=17, cost=11,
    )(info, d_hidden, d_r2, normed, scale, line(gain_one), *feed_buffers)
    keep0, send0, keep1, send1 = call(
        next_halves_kernel, halves_like(rows, 2 * width), [VMEM] * 4, after=(d_branch,))(keep0, keep1, *got_two)
    got_two = swap_all(places, (send0, send1), (Y, X))
    in0, in_send0, in1, in_send1 = call(
        first_halves_kernel, wide_halves, [VMEM] * 2, after=(send0, send1))(in_keep, got_in)
    got_in = swap_all(places, (in_send0, in_send1), (X, Y))
    d_sums, d_carried = call(
        heads_back_kernel, (shaped((tensor, 3, count, 2 * HEAD), BF16), states), [VMEM] * 6,
        after=(in_send0, in_send1), limit=10, cost=11,
    )(d_branch, mix_weight, attended, dens, mixed, query_table)
    arrived_back = [places.onward(d_carried, -s) for s in range(1, tensor)]
    end = shaped((rows, 2 * width), BF16)
    two_ends = call(ends_kernel, (end, end), [VMEM] * 4, after=(d_carried,))(keep0, keep1, *got_two)
    in0, in_send0, in1, in_send1 = call(
        next_halves_kernel, halves_like(rows, 2 * width), [VMEM] * 4, after=two_ends)(in0, in1, *got_in)
    got_in = swap_all(places, (in_send0, in_send1), (Y, X))
    local = call(
        local_back_kernel, shaped((tensor, count, wide), F32), [VMEM] * 4, after=(in_send0, in_send1), limit=10, cost=15,
    )(mixed, d_sums, mask, mask_t)
    feed_last = call(
        feed_last_kernel, (shaped((2 * rows, width), BF16),) * tensor, [VMEM] * 6, after=(local, *arrived_back),
    )(in0, in1, *got_in, *two_ends)
    feed_own = turn_back(places, feed_last)
    mix_like = shaped((4 * rows, 2 * width), BF16)
    mix_outs = (shaped((2, count, width), BF16), shaped((2, 8, width), F32), mix_like)
    mix_scratch = [turned, turned, pltpu.VMEM((2, 3, STATE, 2 * HEAD), BF16), pltpu.VMEM((16, width), F32), pltpu.VMEM((2, count, 128), F32)]
    mix_inputs = (info, mixed, local, d_sums, carried, *arrived_back, query_table, key_table, tokens, attended, d_branch)
    d_mixed_a, d_bias_a, keep_a, send_a = call(
        functools.partial(mix_back_kernel, 0), mix_outs + (mix_like,), [SMEM] + [VMEM] * 12, mix_scratch,
        after=feed_last, limit=19, cost=11,
    )(*mix_inputs)
    got_a = places.swap(send_a, CORE)
    d_mixed_b, d_bias_b, keep_b, send_b, vector_rows = call(
        functools.partial(mix_back_kernel, 2),
        mix_outs + (shaped((4 * rows + 8, 2 * width), BF16), shaped((16, width), BF16)), [SMEM] + [VMEM] * 16,
        mix_scratch, limit=19, cost=11,
    )(*mix_inputs, vectors_one, vectors_two, d_bias_in, d_bias_a)
    feed_rows = added(places, feed_own, 2 * rows, after=(d_mixed_b,))
    got_a, got_b = later(got_a, feed_rows), places.swap(later(send_b, feed_rows), CORE)
    row_like = shaped((16, width), BF16)
    keep0, send0, keep1, send1, vector_rows = call(
        first_pairs_kernel, halves_like(4 * rows, width, 16) + (row_like,), [VMEM] * 5,
    )(keep_a, got_a, keep_b, got_b, vector_rows)
    got = swap_all(places, (send0, send1), (X, Y))
    d_tokens = call(
        tokens_back_kernel, shaped((count, width), BF16), [VMEM] * 4, after=(send0, send1), limit=9, cost=6,
    )(d_mixed_a, d_mixed_b, mix_weight, d_r1)
    keep0, send0, keep1, send1, vector_rows = call(
        mix_next_kernel, halves_like(2 * rows, width, 16) + (row_like,), [VMEM] * 5, after=(d_tokens,),
    )(keep0, keep1, *got, vector_rows)
    got = swap_all(places, (send0, send1), (Y, X))
    feed_low = later(feed_rows, (send0, send1))
    feed_x, feed_y = swap_all(places, (feed_low, feed_low), (X, Y))
    mix_last = call(
        mix_last_kernel, (shaped((rows + 8, width), BF16),) * tensor, [VMEM] * 5,
    )(keep0, keep1, *got, vector_rows)
    mix_own = turn_back(places, mix_last)
    feed_x, feed_y = later((feed_x, feed_y), mix_last)
    feed_xy = later(places.swap(feed_x, Y), mix_own[1])
    feed_all = spread_cores(places, [feed_low, feed_x, feed_y, feed_xy])

    held = pltpu.VMEM((width, width), F32)
    d_w_in, d_w_two = call(
        finish_feed_kernel, (shaped((width, width), F32),) * 2, [SMEM] + [VMEM] * 5, [held], limit=10, cost=4,
    )(info, *feed_all)
    mix_own = later(mix_own, d_w_in)
    mix_rows = added(places, mix_own, rows)
    d_w_qkv, d_w_out = call(
        finish_mix_kernel, (shaped((wide, width), F32), shaped((192, width), F32)), [SMEM] + [VMEM] * 5, [held], limit=7, cost=3,
    )(info, *spread_cores(places, spread_chips(places, mix_rows)))

    ends = jnp.stack([part[rows:] for part in mix_own])
    ends = lax.dynamic_slice_in_dim(jnp.concatenate([ends, ends]), tensor - places.z, tensor, 0)
    summed = over_groups(places, jnp.sum(ends.astype(F32), axis=0))
    d_gain_one, d_shift_one, d_b_out, d_gain_two, d_shift_two, d_b_two = (summed[k] for k in range(6))
    d_b_qkv, d_b_in = summed[6, :wide], summed[7]
    return (block_out, d_tokens, d_w_qkv.T, d_b_qkv, d_w_out, d_b_out, d_gain_one, d_shift_one, d_w_in, d_b_in,
            d_w_two, d_b_two, d_gain_two, d_shift_two)


def solution(mesh):
    sizes = dict(mesh.shape)
    rows = P(("dp", "tensor"), None)
    wide, tall, cut, whole = P(None, "tensor"), P("tensor", None), P("tensor"), P()
    in_specs = (rows, P("dp", None), wide, cut, tall, whole, whole, whole, wide, cut, tall, whole, whole, whole, rows)
    out_specs = (rows, rows, wide, cut, tall, whole, whole, whole, wide, cut, tall, whole, whole, whole)
    return jax.shard_map(
        functools.partial(on_device, sizes["dp"], sizes["tensor"]),
        mesh=mesh, in_specs=in_specs, out_specs=out_specs, check_vma=False,
    )
```

```python
import functools
import math

import jax
import jax.numpy as jnp
from jax import lax
from jax.experimental import pallas as pl
from jax.experimental.pallas import tpu as pltpu
from jax.sharding import PartitionSpec as P

HEAD = 64
ROW_LEN = 2048
DOCS = 8
F32 = jnp.float32
BF16 = jnp.bfloat16
NN = ((1,), (0,))
NT = ((1,), (1,))
TN = ((0,), (0,))
STATE = 80
COST = 0.2 * 1.15e9
VMEM = pl.BlockSpec(memory_space=pltpu.VMEM)
SMEM = pl.BlockSpec(memory_space=pltpu.SMEM)
ANY = pl.BlockSpec(memory_space=pl.ANY)


def dot(left, right, dims=NN):
    return lax.dot_general(left, right, (dims, ((), ())), preferred_element_type=F32)


def call(body, outs, specs, scratch=(), limit=6, after=(), cost=0):
    n = len(specs)

    def waiting_body(*refs):
        body(*refs[:n], *refs[n + len(after):])

    return lambda *operands: pl.pallas_call(
        waiting_body,
        out_shape=outs,
        in_specs=list(specs) + [ANY] * len(after),
        out_specs=jax.tree.map(lambda _: VMEM, outs),
        scratch_shapes=scratch,
        cost_estimate=pl.CostEstimate(flops=1 + int(cost * COST), bytes_accessed=1, transcendentals=0),
        compiler_params=pltpu.CompilerParams(vmem_limit_bytes=limit << 20),
    )(*operands, *after)


def shaped(shape, dtype):
    return jax.ShapeDtypeStruct(shape, dtype)


class Places:
    def __init__(self, dp, tensor):
        self.dp, self.tensor = dp, tensor
        self.row = lax.axis_index("dp")
        self.z = lax.axis_index("tensor")
        self.piece = self.row & 7

    def swap(self, value, mask):
        return lax.ppermute(value, "dp", [(d, d ^ mask) for d in range(self.dp)])

    def turn(self, value, step):
        size = self.tensor
        return lax.ppermute(value, "tensor", [(k, (k + step) % size) for k in range(size)])

    def onward(self, value, step):
        size = self.tensor
        pairs = [(k, k + step) for k in range(size) if 0 <= k + step < size]
        return lax.ppermute(value, "tensor", pairs)


CORE, X, Y = 1, 2, 4
BUFFERS = ((0, (0, 2)), (0, (4, 6)), (0, (1, 3)), (0, (5, 7)), (2, (0, 4)), (2, (2, 6)), (2, (1, 5)), (2, (3, 7)))


def stacked(*groups, after=()):
    sizes = [len(group) for group in groups]

    def body(*refs):
        sources, targets = list(refs[:sum(sizes)]), refs[sum(sizes):]
        for size, target in zip(sizes, targets, strict=True):
            for k in range(size):
                target[k] = sources.pop(0)[...]

    outs = tuple(shaped((len(group),) + group[0].shape, group[0].dtype) for group in groups)
    flat = [value for group in groups for value in group]
    return call(body, outs, [VMEM] * len(flat), after=after)(*flat)


def mix_pieces_kernel(first, second, third, fourth, a, b, bias_qkv, bias_in):
    rows, wide = a.shape[1], bias_qkv.shape[2]
    for j, part in enumerate((first, second, third, fourth)):
        (a, b)[j // 2][j % 2] = part[0:rows]
        extra = part[rows:].astype(F32)
        bias_qkv[j] = extra[0:1, :wide]
        bias_in[j] = extra[1:2]


def swap_halves(places, a, b):
    return places.swap(a, X), places.swap(b, Y)


def gather_rest(places, a, b, a2, b2):
    near, far = stacked((a, b)), stacked((a2, b2))
    return a, a2, b, b2, places.swap(near[0], CORE), places.swap(far[0], CORE)


def start_placing(piece, buffers, targets, sems):
    copies = []
    a, a2, b, b2, near, far = buffers
    buffers = (a, a2, near.at[0], far.at[0], b, b2, near.at[1], far.at[1])
    for buffer, (shard, pieces) in zip(buffers, BUFFERS, strict=True):
        for k, other in enumerate(pieces):
            for at, target, first_row, rows in targets:
                spot = pl.multiple_of(first_row + (piece ^ other) * rows, 8)
                copies.append(pltpu.make_async_copy(
                    buffer.at[k, :, at:at + rows, :],
                    target.at[shard:shard + 2, pl.ds(spot, rows), :],
                    sems.at[len(copies)],
                ))
    for copy in copies:
        copy.start()
    half = len(copies) // 2
    return copies[:half], copies[half:]


def wait_all(copies):
    for copy in copies:
        copy.wait()


def doubled(part):
    return jnp.concatenate([part, part], axis=1)


def with_one(value):
    lanes = lax.broadcasted_iota(jnp.int32, (value.shape[0], 2 * HEAD), 1)
    return jnp.where(lanes < HEAD, doubled(value.astype(F32)), (lanes == HEAD).astype(F32)).astype(BF16)


def head_parts(mixed_ref, shard, head):
    at = head * 3 * HEAD
    return tuple(mixed_ref[shard, :, at + t * HEAD:at + (t + 1) * HEAD] for t in range(3))


def causal_blocks(count):
    half = count // 2
    return ((0, half, 0, half), (half, count, 0, count))


def mix_kernel(info, tokens, bias, key_table, *refs):
    buffers, (mixed_out, state_out, weight), sems = refs[:6], refs[6:9], refs[9]
    wide = mixed_out.shape[2]
    tall = weight.shape[1] - wide
    halves = start_placing(
        info[0], buffers, ((0, weight, 0, wide // 8), (wide // 8, weight, wide, tall // 8)), sems)

    def shard_step(j, carry):
        mixed = dot(tokens[...], weight[j, 0:wide], NT) + bias[j]
        lanes = lax.broadcasted_iota(jnp.int32, mixed.shape, 1)
        mixed_out[j] = jnp.where(lanes % 192 >= 128, mixed, jnp.maximum(mixed, 0.0)).astype(BF16)
        for h in range(3):
            _, key, value = head_parts(mixed_out, j, h)
            feats = (doubled(key).astype(F32) * key_table[...]).astype(BF16)
            state_out[j, h] = dot(with_one(value), feats, TN)[:STATE].astype(BF16)
        return carry

    for k, half in enumerate(halves):
        wait_all(half)
        lax.fori_loop(2 * k, 2 * k + 2, shard_step, 0)


def local_kernel(mixed, mask, sums_out):
    def shard_step(j, carry):
        for h in range(3):
            query, key, value = head_parts(mixed, j, h)
            value = with_one(value)
            for r0, r1, c0, c1 in causal_blocks(mask.shape[0]):
                scores = (dot(query[r0:r1], key[c0:c1], NT) * mask[r0:r1, c0:c1]).astype(BF16)
                sums_out[j, h, r0:r1] = dot(scores, value[c0:c1])
        return carry

    lax.fori_loop(0, mixed.shape[0], shard_step, 0)


def norm_parts(rows_in):
    centred = rows_in - jnp.mean(rows_in, axis=-1, keepdims=True)
    spread = jnp.mean(centred * centred, axis=-1, keepdims=True)
    scale = lax.rsqrt(spread + 1e-05)
    return centred * scale, scale


def norm_back(grad, normed, scale, gain):
    e = grad * gain
    d_rows = scale * (
        e
        - jnp.mean(e, axis=-1, keepdims=True)
        - normed * jnp.mean(e * normed, axis=-1, keepdims=True)
    )
    return d_rows, jnp.sum(grad * normed, axis=0, keepdims=True), jnp.sum(grad, axis=0, keepdims=True)


def join_kernel(info, sums, arrived1, arrived2, arrived3, mixed, query_table, tokens, weight, b_out, gain, shift,
                attended, carried, dens, first, normed_out, scale_out):
    shards = mixed.shape[0]
    for j in range(shards):
        total = None
        for step, arrived in enumerate((arrived1, arrived2, arrived3), 1):
            linked = info[step].astype(F32) * arrived[(j - step) % shards].astype(F32)
            total = linked if total is None else total + linked
        carried[j] = total.astype(BF16)

    def shard_step(j, branch):
        lanes = lax.broadcasted_iota(jnp.int32, (tokens.shape[0], 128), 1)
        kept = jnp.zeros((tokens.shape[0], 128), F32)
        for h in range(3):
            query = head_parts(mixed, j, h)[0]
            feats = (doubled(query).astype(F32) * query_table[...]).astype(BF16)
            total = sums[j, h][:, :STATE] + dot(feats, carried[j, h], NT)
            den = total[:, HEAD:HEAD + 1]
            inverse = 1.0 / jnp.maximum(den, 1.0)
            attended[j, :, h * HEAD:(h + 1) * HEAD] = (total[:, :HEAD] * inverse).astype(BF16)
            kept = jnp.where(lanes == h, inverse, kept)
            kept = jnp.where(lanes == 8 + h, jnp.where(den > 1.0, inverse, 0.0), kept)
        dens[j] = kept
        return branch + dot(attended[j], weight[j, weight.shape[1] - 192:])

    branch = lax.fori_loop(0, shards, shard_step, jnp.zeros(tokens.shape, F32))
    normed, scale = norm_parts(tokens[...].astype(F32) + branch + b_out[...])
    normed_out[...] = normed
    scale_out[...] = jnp.broadcast_to(scale, scale_out.shape)
    first[...] = (normed * gain[...] + shift[...]).astype(BF16)


def gelu_parts(v):
    k = math.sqrt(2 / math.pi)
    square = v * v
    t = jnp.tanh(v * (k + k * 0.044715 * square))
    half = 0.5 * v
    bent = half * t
    slope = (0.5 + 0.5 * t) + (half - bent * t) * (k + 3 * k * 0.044715 * square)
    return half + bent, slope


def rows_ordered(turned, piece, order):
    rows = turned.shape[0] // 8
    return jnp.concatenate(
        [turned[pl.ds(pl.multiple_of((piece ^ other) * rows, rows), rows), :] for other in order], axis=0)


ROUTES = ((0, 4, 2, 6), (0, 2, 4, 6))


def order_rows(ordered, turned, piece):
    for route, order in enumerate(ROUTES):
        for sends in range(2):
            ordered[2 * route + sends] = rows_ordered(turned, piece, tuple(other + sends for other in order))


def columns(j, width):
    return pl.ds(pl.multiple_of(j * width, 128), width)


def feed_kernel(info, first, bias, b_two, gain, shift, cotangent, *refs):
    buffers = refs[:6]
    slope, block_out, d_second_out, d_r2_out, vectors, *grads = refs[6:13]
    w_in, w_two, active, turned, ordered, total, sems = refs[13:]
    shards, width = w_in.shape[0], w_in.shape[2]
    rows = width // 8
    halves = start_placing(info[0], buffers, ((0, w_in, 0, rows), (rows, w_two, 0, rows)), sems)
    total[...] = jnp.broadcast_to(b_two[...], total.shape)

    def forward_step(j, carry):
        half = first.shape[0] // 2
        spans = slice(0, half), slice(half, 2 * half)
        hidden = [dot(first[span], w_in[j]) + bias[j] for span in spans]
        for span, part in zip(spans, hidden, strict=True):
            act, bend = gelu_parts(part)
            act = act.astype(BF16)
            active[j, span] = act
            slope[j, span] = bend.astype(BF16)
            total[span] += dot(act, w_two[j])
        return carry

    for k, half in enumerate(halves):
        wait_all(half)
        lax.fori_loop(2 * k, 2 * k + 2, forward_step, 0)
    normed, scale = norm_parts(first[...].astype(F32) + total[...])
    block_out[...] = (normed * gain[...] + shift[...]).astype(BF16)
    d_r2, d_gain, d_shift = norm_back(cotangent[...].astype(F32), normed, scale, gain[...])
    d_r2_out[...] = d_r2
    d_second = d_r2.astype(BF16)
    d_second_out[...] = d_second
    turned[...] = d_second.T
    vectors[0:1] = d_gain
    vectors[1:2] = d_shift
    vectors[2:3] = jnp.sum(d_second.astype(F32), axis=0, keepdims=True)
    vectors[3:] = jnp.zeros((5, vectors.shape[1]), F32)
    order_rows(ordered, turned, info[0])

    def grad_step(j, carry):
        for sends in range(2):
            grads[sends][:, columns(j, width)] = dot(ordered[2 * (j // 2) + sends], active[j]).astype(BF16)
        return carry

    lax.fori_loop(0, shards, grad_step, 0)


def feed_back_kernel(info, first, d_second, slope, *refs):
    buffers = refs[:6]
    d_hidden, d_bias, *grads = refs[6:10]
    w_two, turned, ordered, sems = refs[10:]
    shards, width = w_two.shape[0], w_two.shape[2]
    rows = width // 8
    halves = start_placing(info[0], buffers, ((rows, w_two, 0, rows),), sems)
    turned[...] = first[...].T
    order_rows(ordered, turned, info[0])

    def step(j, carry):
        d_active = dot(d_second[...], w_two[j], NT)
        d_h = (d_active * slope[j].astype(F32)).astype(BF16)
        d_hidden[j] = d_h
        d_bias[j] = jnp.broadcast_to(jnp.sum(d_h.astype(F32), axis=0, keepdims=True), d_bias.shape[1:])
        for sends in range(2):
            grads[sends][:, columns(j, width)] = dot(ordered[2 * (j // 2) + sends], d_hidden[j]).astype(BF16)
        return carry

    for k, half in enumerate(halves):
        wait_all(half)
        lax.fori_loop(2 * k, 2 * k + 2, step, 0)


def first_back_kernel(info, d_hidden, d_r2, normed, scale, gain, *refs):
    buffers = refs[:6]
    d_r1_out, d_branch_out, vectors = refs[6:9]
    w_in, total, sems = refs[9:]
    rows = w_in.shape[1] // 8
    halves = start_placing(info[0], buffers, ((0, w_in, 0, rows),), sems)
    total[...] = d_r2[...]

    def first_step(j, carry):
        total[...] += dot(d_hidden[j], w_in[j], NT)
        return carry

    for k, half in enumerate(halves):
        wait_all(half)
        lax.fori_loop(2 * k, 2 * k + 2, first_step, 0)
    d_r1, d_gain, d_shift = norm_back(total[...], normed[...], scale[:, 0:1], gain[...])
    d_r1_out[...] = d_r1
    d_branch = d_r1.astype(BF16)
    d_branch_out[...] = d_branch
    vectors[0:1] = d_gain
    vectors[1:2] = d_shift
    vectors[2:3] = jnp.sum(d_branch.astype(F32), axis=0, keepdims=True)
    vectors[3:] = jnp.zeros((5, vectors.shape[1]), F32)


def heads_back_kernel(d_branch, weight, attended, dens, mixed, query_table, d_sums, d_carried):
    def shard_step(j, carry):
        g_all = dot(d_branch[...], weight[j, weight.shape[1] - 192:], NT)
        lanes = lax.broadcasted_iota(jnp.int32, (d_branch.shape[0], 128), 1)
        for h in range(3):
            g = g_all[:, h * HEAD:(h + 1) * HEAD]
            o = attended[j, :, h * HEAD:(h + 1) * HEAD].astype(F32)
            inverse, inverse_if = dens[j, :, h:h + 1], dens[j, :, 8 + h:9 + h]
            d_den = -jnp.sum(g * o, axis=-1, keepdims=True) * inverse_if
            d_num = doubled(g * inverse)
            both = jnp.where(lanes < HEAD, d_num, jnp.where(lanes == HEAD, d_den, 0.0)).astype(BF16)
            d_sums[j, h] = both
            query = head_parts(mixed, j, h)[0]
            feats = (doubled(query).astype(F32) * query_table[...]).astype(BF16)
            d_carried[j, h] = dot(both, feats, TN)[:STATE].astype(BF16)
        return carry

    lax.fori_loop(0, mixed.shape[0], shard_step, 0)


def local_back_kernel(mixed, d_sums, mask, mask_t, d_mixed):
    def shard_step(j, carry):
        for h in range(3):
            query, key, value = head_parts(mixed, j, h)
            value = with_one(value)
            grad = d_sums[j, h]
            at = h * 3 * HEAD
            for r0, r1, c0, c1 in causal_blocks(mask.shape[0]):
                d_scores = (dot(grad[r0:r1], value[c0:c1], NT) * mask[r0:r1, c0:c1]).astype(BF16)
                d_mixed[j, r0:r1, at:at + HEAD] = dot(d_scores, key[c0:c1])
            half = mask.shape[0] // 2
            for c0, c1, r0 in ((0, half, 0), (half, 2 * half, half)):
                turned = mask_t[c0:c1, r0:]
                d_scores = (dot(value[c0:c1], grad[r0:], NT) * turned).astype(BF16)
                d_mixed[j, c0:c1, at + HEAD:at + 2 * HEAD] = dot(d_scores, query[r0:])
                scores = (dot(key[c0:c1], query[r0:], NT) * turned).astype(BF16)
                d_mixed[j, c0:c1, at + 2 * HEAD:at + 3 * HEAD] = dot(scores, grad[r0:])[:, :HEAD]
        return carry

    lax.fori_loop(0, mixed.shape[0], shard_step, 0)


def mix_back_kernel(base, info, mixed, local, d_sums, carried, arrived1, arrived2, arrived3, query_table, key_table,
                    tokens, attended, d_branch, *refs):
    last = base > 0
    sources, refs = (refs[:4], refs[4:]) if last else ((), refs)
    d_mixed, d_bias, *grads = refs[:4]
    turned, turned_branch, state, held, middles = refs[-5:]
    shards, wide = mixed.shape[0], mixed.shape[2]
    width = d_mixed.shape[2]
    turned[...] = tokens[...].T
    turned_branch[...] = d_branch[...].T
    for k in range(2):
        total = None
        for step, arrived in enumerate((arrived1, arrived2, arrived3), 1):
            linked = info[3 + step].astype(F32) * arrived[(base + k + step) % shards].astype(F32)
            total = linked if total is None else total + linked
        state[k] = total.astype(BF16)

    def folded(both):
        return both[:, :HEAD] + both[:, HEAD:]

    def shard_step(k, carry):
        j = base + k
        parts = []
        for h in range(3):
            query, key, value = head_parts(mixed, j, h)
            at = h * 3 * HEAD
            spans = [slice(at + t * HEAD, at + (t + 1) * HEAD) for t in range(3)]
            d_query = folded(dot(d_sums[j, h][:, :STATE], carried[j, h]) * query_table[...])
            d_query = jnp.where(query.astype(F32) > 0, local[j, :, spans[0]] + d_query, 0.0)
            d_key = folded(dot(with_one(value)[:, :STATE], state[k, h]) * key_table[...])
            d_key = jnp.where(key.astype(F32) > 0, local[j, :, spans[1]] + d_key, 0.0)
            feats = (doubled(key).astype(F32) * key_table[...]).astype(BF16)
            d_value = local[j, :, spans[2]] + dot(feats, state[k, h], NT)[:, :HEAD]
            parts += [d_query, d_key, d_value]
        whole = jnp.concatenate(parts + [attended[j].astype(F32)], axis=1).astype(BF16)
        d_mixed[k] = whole
        middles[k] = jnp.concatenate([parts[-1], attended[j][:, :HEAD].astype(F32)], axis=1)
        d_bias[k] = jnp.broadcast_to(jnp.sum(d_mixed[k].astype(F32), axis=0, keepdims=True), d_bias.shape[1:])
        return carry

    lax.fori_loop(0, 2, shard_step, 0)
    rows = grads[0].shape[0]
    low = wide // 128 * 128
    for k in range(2):
        lanes = lax.broadcasted_iota(jnp.int32, (d_mixed.shape[1], 128), 1)
        middle = middles[k]
        left_side = jnp.where(lanes < HEAD, middle, 0.0).astype(BF16)
        right_side = jnp.where(lanes < HEAD, 0.0, middle).astype(BF16)
        left_side = jnp.concatenate([d_mixed[k][:, :low], left_side], axis=1)
        right_side = jnp.concatenate([right_side, d_mixed[k][:, low + 128:]], axis=1)
        for sends in (1, 0):
            out, at = grads[sends], k * width
            order = tuple(other + sends for other in ROUTES[k])
            left = dot(rows_ordered(turned, info[0], order), left_side)
            right = dot(rows_ordered(turned_branch, info[0], order), right_side)
            out[0:rows, at:at + low] = left[:, :low].astype(BF16)
            out[0:rows, at + low:at + low + 128] = (left[:, low:] + right[:, :128]).astype(BF16)
            out[0:rows, at + low + 128:at + width] = right[:, 128:].astype(BF16)
    if last:
        one, two, bias_in, bias_first = sources
        vectors = refs[4]
        held[0:3] = one[0:3]
        held[3:6] = two[0:3]
        for j in range(shards):
            held[6 + 2 * j:7 + 2 * j] = bias_first[j, 0:1] if j < 2 else d_bias[j - 2, 0:1]
            held[7 + 2 * j:8 + 2 * j] = bias_in[j, 0:1]
        held[14:16] = jnp.zeros((2, width), F32)
        low_rows = held[...].astype(BF16)
        vectors[...] = low_rows
        grads[1][rows:, 0:width] = low_rows[0:8]
        grads[1][rows:, width:] = low_rows[8:16]


def tokens_back_kernel(d_mixed_a, d_mixed_b, weight, d_r1, d_tokens):
    wide = weight.shape[1] - 192
    total = d_r1[...]
    for j in range(weight.shape[0]):
        d_mixed = (d_mixed_a, d_mixed_b)[j // 2]
        total = total + dot(d_mixed[j % 2][:, :wide], weight[j, 0:wide])
    d_tokens[...] = total.astype(BF16)


def later(values, others):
    return lax.optimization_barrier((values, others))[0]


def halves_like(rows, width, extra=0):
    keep, send = shaped((rows, width), F32), shaped((rows, width), BF16)
    return keep, send, keep, shaped((rows + extra, width), BF16)


def first_halves_kernel(keep, got, *outs):
    half, width = outs[0].shape
    for k in range(2):
        cols = slice(k * width, (k + 1) * width)
        outs[2 * k][...] = keep[0:half, cols].astype(F32) + got[0:half, cols].astype(F32)
        send = keep[half:2 * half, cols].astype(F32) + got[half:2 * half, cols].astype(F32)
        outs[2 * k + 1][0:half] = send.astype(BF16)


def first_pairs_kernel(keep_a, got_a, keep_b, got_b, mine, *outs):
    half, width = outs[0].shape[0] // 2, outs[0].shape[1]
    for k in range(2):
        cols = slice(k * width, (k + 1) * width)
        for t, (keep, got) in enumerate(((keep_a, got_a), (keep_b, got_b))):
            spots = slice(t * half, (t + 1) * half)
            outs[2 * k][spots] = keep[0:half, cols].astype(F32) + got[0:half, cols].astype(F32)
            send = keep[half:2 * half, cols].astype(F32) + got[half:2 * half, cols].astype(F32)
            outs[2 * k + 1][spots] = send.astype(BF16)
        rows = mine[8 * k:8 * k + 8].astype(F32) + got_b[2 * half:, cols].astype(F32)
        outs[4][8 * k:8 * k + 8] = rows.astype(BF16)
        outs[3][2 * half + 8 * k:2 * half + 8 * k + 8] = rows.astype(BF16)


def next_halves_kernel(keep0, keep1, got0, got1, *outs):
    half = outs[0].shape[0]
    for k, (keep, got) in enumerate(((keep0, got0), (keep1, got1))):
        outs[2 * k][...] = keep[0:half] + got[0:half].astype(F32)
        outs[2 * k + 1][...] = (keep[half:] + got[half:].astype(F32)).astype(BF16)


def ends_kernel(keep0, keep1, got0, got1, end0, end1):
    end0[...] = (keep0[...] + got0[...].astype(F32)).astype(BF16)
    end1[...] = (keep1[...] + got1[...].astype(F32)).astype(BF16)


def feed_last_kernel(keep0, keep1, got0, got1, two0, two1, *outs):
    rows, width = outs[0].shape[0] // 2, outs[0].shape[1]
    for j, out in enumerate(outs):
        keep, got, two = (keep0, got0, two0) if j < 2 else (keep1, got1, two1)
        cols = slice(j % 2 * width, (j % 2 + 1) * width)
        out[0:rows] = (keep[:, cols] + got[:, cols].astype(F32)).astype(BF16)
        out[rows:] = two[:, cols]


def mix_next_kernel(keep0, keep1, got0, got1, mine, *outs):
    half = outs[0].shape[0] // 2
    for k, (keep, got) in enumerate(((keep0, got0), (keep1, got1))):
        for t in range(2):
            at = 2 * t * half
            spots = slice(t * half, (t + 1) * half)
            outs[2 * k][spots] = keep[at:at + half] + got[at:at + half].astype(F32)
            send = keep[at + half:at + 2 * half] + got[at + half:at + 2 * half].astype(F32)
            outs[2 * k + 1][spots] = send.astype(BF16)
    rows = (mine[...].astype(F32) + got1[4 * half:].astype(F32)).astype(BF16)
    outs[4][...] = rows
    outs[3][2 * half:] = rows


def mix_last_kernel(keep0, keep1, got0, got1, mine, *outs):
    half = keep0.shape[0] // 2
    rows = (mine[...].astype(F32) + got1[2 * half:].astype(F32)).astype(BF16)
    for j, out in enumerate(outs):
        keep, got = (keep0, got0) if j % 2 == 0 else (keep1, got1)
        spots = slice(j // 2 * half, (j // 2 + 1) * half)
        out[0:half] = (keep[spots] + got[spots].astype(F32)).astype(BF16)
        out[half:half + 6] = rows[0:6]
        out[half + 6:half + 8] = rows[6 + 2 * j:8 + 2 * j]


def swap_all(places, values, masks):
    return [places.swap(value, mask) for value, mask in zip(values, masks, strict=True)]


def turn_back(places, parts):
    return [parts[0]] + [places.turn(parts[s], -s) for s in range(1, places.tensor)]


def pair_sum(mine, other):
    return (mine.astype(F32) + other.astype(F32)).astype(BF16)


def over_groups(places, total):
    mask = 8
    while mask < places.dp:
        total = total + places.swap(total, mask)
        mask *= 2
    return total


def added(places, values, rows, after=()):
    kind = BF16 if places.dp == 8 else F32

    def body(*refs):
        total = refs[0][0:rows].astype(F32)
        for other in refs[1:-1]:
            total = total + other[0:rows].astype(F32)
        refs[-1][...] = total.astype(kind)

    total = call(body, shaped((rows, values[0].shape[1]), kind), [VMEM] * len(values), after=after)(*values)
    return over_groups(places, total).astype(BF16)


def spread_chips(places, own):
    return [own, places.swap(own, X), places.swap(own, Y), places.swap(own, X + Y)]


def spread_cores(places, four):
    return list(four) + [places.swap(stacked(four)[0], CORE)]


def place_rows(piece, pieces, targets):
    for k in range(8):
        source = pieces[k // 2] if k % 2 == 0 else pieces[4].at[k // 2]
        for t, target in enumerate(targets):
            rows = target.shape[0] // 8
            spot = pl.multiple_of((piece ^ k) * rows, rows)
            target[pl.ds(spot, rows), :] = source[t * rows:(t + 1) * rows].astype(F32)


def finish_feed_kernel(info, own, x, y, xy, core, d_in, d_two, held):
    place_rows(info[0], (own, x, y, xy, core), (d_in, held))
    d_two[...] = held[...].T


def finish_mix_kernel(info, own, x, y, xy, core, d_qkv, d_out, held):
    place_rows(info[0], (own, x, y, xy, core), (held,))
    turned = held[...].T
    d_qkv[...] = turned[0:d_qkv.shape[0]]
    d_out[...] = turned[d_qkv.shape[0]:]


def doc_tables(starts_row, base, count):
    spots = base + jnp.arange(count, dtype=jnp.int32)
    started = (spots[:, None] >= starts_row[None, :]).astype(jnp.int32)
    doc_ids = jnp.sum(started, axis=1) - 1
    onehot = (doc_ids[:, None] == jnp.arange(DOCS, dtype=jnp.int32)[None, :]).astype(jnp.int32)
    finish = jnp.concatenate([starts_row[1:], jnp.full((1,), ROW_LEN, jnp.int32)])
    own_start = jnp.sum(onehot * starts_row[None, :], axis=1)
    own_len = jnp.sum(onehot * (finish - starts_row)[None, :], axis=1)
    angles = 0.5 * math.pi * (spots - own_start).astype(F32) / own_len.astype(F32)
    return angles, doc_ids


def doc_at(starts_row, spot):
    return jnp.sum((spot >= starts_row).astype(jnp.int32)) - 1


def on_device(dp, tensor, tokens, starts, w_qkv, b_qkv, w_out, b_out, gain_one, shift_one, w_in, b_in,
              w_two, b_two, gain_two, shift_two, cotangent):
    places = Places(dp, tensor)
    count, width = tokens.shape
    piece = places.piece
    line = lambda a: a.astype(F32).reshape(1, -1)
    sems = lambda n: pltpu.SemaphoreType.DMA((n,))

    def own_rows(weight):
        rows = weight.shape[0] // 8
        return lax.dynamic_slice_in_dim(weight, piece * rows, rows, 0)

    rows = width // 8
    wide = w_qkv.shape[1]
    bias_rows = jnp.pad(b_qkv.reshape(1, wide), ((0, 7), (0, width - wide))) + jnp.pad(b_in.reshape(1, width), ((1, 6), (0, 0)))
    mix_piece = jnp.concatenate([own_rows(w_qkv.T), own_rows(w_out), bias_rows])
    feed_piece = jnp.concatenate([own_rows(w_in), own_rows(w_two)])
    mix_parts = [mix_piece] + [places.turn(mix_piece, s) for s in range(1, tensor)]
    feed_parts = [feed_piece] + [places.turn(feed_piece, s) for s in range(1, tensor - 1)]
    feed_parts.append(places.turn(later(feed_piece, mix_parts), tensor - 1))
    pair = shaped((2, rows, width), BF16)
    mix_a, mix_b, bias_qkv, bias_in = call(
        mix_pieces_kernel, (pair, pair, shaped((tensor, 1, wide), F32), shaped((tensor, 1, width), F32)), [VMEM] * 4,
    )(*mix_parts)
    near_x, near_y = swap_halves(places, mix_a, mix_b)
    mix_ax, mix_by = stacked((mix_a, near_x), (mix_b, near_y))
    mix_buffers = gather_rest(places, mix_ax, mix_by, places.swap(mix_ax, Y), places.swap(mix_by, X))
    feed_a, feed_b = stacked(feed_parts[:2], feed_parts[2:], after=(mix_ax, mix_by))
    near_x, near_y = swap_halves(places, feed_a, feed_b)

    row = starts[0]
    base = places.z * count
    angles, docs = doc_tables(row, base, count)
    first_doc, last_doc = doc_at(row, base), doc_at(row, base + count - 1)
    links = [doc_at(row, base - (s - 1) * count - 1) == first_doc for s in range(1, tensor)]
    links += [doc_at(row, base + s * count) == last_doc for s in range(1, tensor)]
    info = jnp.stack([piece] + [link.astype(jnp.int32) for link in links] + [piece])
    spot = jnp.arange(count)
    cosine, sines = jnp.cos(angles), jnp.sin(angles)
    turn = cosine[:, None] * cosine[None, :] + sines[:, None] * sines[None, :]
    same = docs[:, None] == docs[None, :]
    mask = jnp.where(same & (spot[:, None] >= spot[None, :]), turn, 0.0)
    mask_t = jnp.where(same & (spot[:, None] <= spot[None, :]), turn, 0.0)
    lanes = jnp.arange(2 * HEAD)[None, :]
    table = jnp.where(lanes < HEAD, cosine[:, None], sines[:, None])
    query_table = jnp.where((docs == first_doc)[:, None], table, 0.0)
    key_table = jnp.where((docs == last_doc)[:, None], table, 0.0)

    states = shaped((tensor, 3, STATE, 2 * HEAD), BF16)
    mixed, state, mix_weight = call(
        mix_kernel,
        (shaped((tensor, count, wide), BF16), states, shaped((tensor, width, width), BF16)),
        [SMEM, VMEM, VMEM, VMEM] + [ANY] * 6, [sems(32)], limit=9, cost=8,
    )(info, tokens, bias_qkv, key_table, *mix_buffers)
    per_head = shaped((tensor, 3, count, 2 * HEAD), F32)
    arrived = [places.onward(state, s) for s in range(1, tensor)]
    per_head = shaped((tensor, 3, count, 2 * HEAD), F32)
    feed_ax, feed_by = stacked((feed_a, near_x), (feed_b, near_y), after=(state,))
    near_sums = call(local_kernel, per_head, [VMEM, VMEM], after=(feed_ax, feed_by), limit=6, cost=7)(mixed, mask)
    feed_far = places.swap(feed_ax, Y), places.swap(feed_by, X)
    attended, carried, dens, first, normed, scale = call(
        join_kernel,
        (shaped((tensor, count, 192), BF16), states, shaped((tensor, count, 128), F32), shaped((count, width), BF16),
         shaped((count, width), F32), shaped((count, 128), F32)),
        [SMEM] + [VMEM] * 11, limit=18, cost=100,
    )(info, near_sums, *arrived, mixed, query_table, tokens, mix_weight, line(b_out), line(gain_one), line(shift_one))
    feed_buffers = gather_rest(places, *later((feed_ax, feed_by, *feed_far), first))
    hidden_like = shaped((tensor, count, width), BF16)
    vectors = shaped((8, width), F32)
    grad_like = shaped((4 * rows, tensor * width), BF16)
    square = pltpu.VMEM((tensor, width, width), BF16)
    turned = pltpu.VMEM((width, count), BF16)
    ordered = pltpu.VMEM((4, 4 * rows, count), BF16)
    total_scratch = pltpu.VMEM((count, width), F32)
    slope, block_out, d_second, d_r2, vectors_two, two_keep, two_send = call(
        feed_kernel,
        (hidden_like, shaped((count, width), BF16), shaped((count, width), BF16),
         shaped((count, width), F32), vectors, grad_like, grad_like),
        [SMEM] + [VMEM] * 6 + [ANY] * 6, [square, square, pltpu.VMEM(hidden_like.shape, BF16), turned, ordered, total_scratch, sems(32)], limit=33, cost=19,
    )(info, first, bias_in, line(b_two), line(gain_two), line(shift_two), cotangent, *feed_buffers)

    got = places.swap(two_send, CORE)
    d_hidden, d_bias_in, in_keep, in_send = call(
        feed_back_kernel, (hidden_like, shaped((tensor, 8, width), F32), grad_like, grad_like),
        [SMEM] + [VMEM] * 3 + [ANY] * 6, [square, turned, ordered, sems(16)], limit=19, cost=14,
    )(info, first, d_second, slope, *feed_buffers)
    wide_halves = halves_like(2 * rows, 2 * width)
    keep0, send0, keep1, send1 = call(first_halves_kernel, wide_halves, [VMEM] * 2, after=(in_send,))(two_keep, got)
    got_two, got_in = swap_all(places, (send0, send1), (X, Y)), places.swap(in_send, CORE)
    d_r1, d_branch, vectors_one = call(
        first_back_kernel,
        (shaped((count, width), F32), shaped((count, width), BF16), vectors),
        [SMEM] + [VMEM] * 5 + [ANY] * 6, [square, total_scratch, sems(16)], after=(send0, send1), limit=17, cost=11,
    )(info, d_hidden, d_r2, normed, scale, line(gain_one), *feed_buffers)
    keep0, send0, keep1, send1 = call(
        next_halves_kernel, halves_like(rows, 2 * width), [VMEM] * 4, after=(d_branch,))(keep0, keep1, *got_two)
    got_two = swap_all(places, (send0, send1), (Y, X))
    in0, in_send0, in1, in_send1 = call(
        first_halves_kernel, wide_halves, [VMEM] * 2, after=(send0, send1))(in_keep, got_in)
    got_in = swap_all(places, (in_send0, in_send1), (X, Y))
    d_sums, d_carried = call(
        heads_back_kernel, (shaped((tensor, 3, count, 2 * HEAD), BF16), states), [VMEM] * 6,
        after=(in_send0, in_send1), limit=10, cost=11,
    )(d_branch, mix_weight, attended, dens, mixed, query_table)
    arrived_back = [places.onward(d_carried, -s) for s in range(1, tensor)]
    end = shaped((rows, 2 * width), BF16)
    two_ends = call(ends_kernel, (end, end), [VMEM] * 4, after=(d_carried,))(keep0, keep1, *got_two)
    in0, in_send0, in1, in_send1 = call(
        next_halves_kernel, halves_like(rows, 2 * width), [VMEM] * 4, after=two_ends)(in0, in1, *got_in)
    got_in = swap_all(places, (in_send0, in_send1), (Y, X))
    local = call(
        local_back_kernel, shaped((tensor, count, wide), F32), [VMEM] * 4, after=(in_send0, in_send1), limit=10, cost=15,
    )(mixed, d_sums, mask, mask_t)
    feed_last = call(
        feed_last_kernel, (shaped((2 * rows, width), BF16),) * tensor, [VMEM] * 6, after=(local, *arrived_back),
    )(in0, in1, *got_in, *two_ends)
    feed_own = turn_back(places, feed_last)
    mix_like = shaped((4 * rows, 2 * width), BF16)
    mix_outs = (shaped((2, count, width), BF16), shaped((2, 8, width), F32), mix_like)
    mix_scratch = [turned, turned, pltpu.VMEM((2, 3, STATE, 2 * HEAD), BF16), pltpu.VMEM((16, width), F32), pltpu.VMEM((2, count, 128), F32)]
    mix_inputs = (info, mixed, local, d_sums, carried, *arrived_back, query_table, key_table, tokens, attended, d_branch)
    d_mixed_a, d_bias_a, keep_a, send_a = call(
        functools.partial(mix_back_kernel, 0), mix_outs + (mix_like,), [SMEM] + [VMEM] * 12, mix_scratch,
        after=feed_last, limit=19, cost=11,
    )(*mix_inputs)
    got_a = places.swap(send_a, CORE)
    d_mixed_b, d_bias_b, keep_b, send_b, vector_rows = call(
        functools.partial(mix_back_kernel, 2),
        mix_outs + (shaped((4 * rows + 8, 2 * width), BF16), shaped((16, width), BF16)), [SMEM] + [VMEM] * 16,
        mix_scratch, limit=19, cost=11,
    )(*mix_inputs, vectors_one, vectors_two, d_bias_in, d_bias_a)
    feed_rows = added(places, feed_own, 2 * rows, after=(d_mixed_b,))
    got_a, got_b = later(got_a, feed_rows), places.swap(later(send_b, feed_rows), CORE)
    row_like = shaped((16, width), BF16)
    keep0, send0, keep1, send1, vector_rows = call(
        first_pairs_kernel, halves_like(4 * rows, width, 16) + (row_like,), [VMEM] * 5,
    )(keep_a, got_a, keep_b, got_b, vector_rows)
    got = swap_all(places, (send0, send1), (X, Y))
    d_tokens = call(
        tokens_back_kernel, shaped((count, width), BF16), [VMEM] * 4, after=(send0, send1), limit=9, cost=6,
    )(d_mixed_a, d_mixed_b, mix_weight, d_r1)
    keep0, send0, keep1, send1, vector_rows = call(
        mix_next_kernel, halves_like(2 * rows, width, 16) + (row_like,), [VMEM] * 5, after=(d_tokens,),
    )(keep0, keep1, *got, vector_rows)
    got = swap_all(places, (send0, send1), (Y, X))
    feed_low = later(feed_rows, (send0, send1))
    feed_x, feed_y = swap_all(places, (feed_low, feed_low), (X, Y))
    mix_last = call(
        mix_last_kernel, (shaped((rows + 8, width), BF16),) * tensor, [VMEM] * 5,
    )(keep0, keep1, *got, vector_rows)
    mix_own = turn_back(places, mix_last)
    feed_x, feed_y = later((feed_x, feed_y), mix_own[1])
    feed_all = spread_cores(places, [feed_low, feed_x, feed_y, places.swap(feed_x, Y)])

    held = pltpu.VMEM((width, width), F32)
    d_w_in, d_w_two = call(
        finish_feed_kernel, (shaped((width, width), F32),) * 2, [SMEM] + [VMEM] * 5, [held], limit=10, cost=4,
    )(info, *feed_all)
    mix_rows = added(places, mix_own, rows)
    mix_four = later(spread_chips(places, mix_rows), d_w_in)
    d_w_qkv, d_w_out = call(
        finish_mix_kernel, (shaped((wide, width), F32), shaped((192, width), F32)), [SMEM] + [VMEM] * 5, [held], limit=7, cost=3,
    )(info, *spread_cores(places, mix_four))

    ends = jnp.stack([part[rows:] for part in mix_own])
    ends = lax.dynamic_slice_in_dim(jnp.concatenate([ends, ends]), tensor - places.z, tensor, 0)
    summed = over_groups(places, jnp.sum(ends.astype(F32), axis=0))
    d_gain_one, d_shift_one, d_b_out, d_gain_two, d_shift_two, d_b_two = (summed[k] for k in range(6))
    d_b_qkv, d_b_in = summed[6, :wide], summed[7]
    return (block_out, d_tokens, d_w_qkv.T, d_b_qkv, d_w_out, d_b_out, d_gain_one, d_shift_one, d_w_in, d_b_in,
            d_w_two, d_b_two, d_gain_two, d_shift_two)


def solution(mesh):
    sizes = dict(mesh.shape)
    rows = P(("dp", "tensor"), None)
    wide, tall, cut, whole = P(None, "tensor"), P("tensor", None), P("tensor"), P()
    in_specs = (rows, P("dp", None), wide, cut, tall, whole, whole, whole, wide, cut, tall, whole, whole, whole, rows)
    out_specs = (rows, rows, wide, cut, tall, whole, whole, whole, wide, cut, tall, whole, whole, whole)
    return jax.shard_map(
        functools.partial(on_device, sizes["dp"], sizes["tensor"]),
        mesh=mesh, in_specs=in_specs, out_specs=out_specs, check_vma=False,
    )
```

```python
import functools
import math

import jax
import jax.numpy as jnp
from jax import lax
from jax.experimental import pallas as pl
from jax.experimental.pallas import tpu as pltpu
from jax.sharding import PartitionSpec as P

HEAD = 64
ROW_LEN = 2048
DOCS = 8
F32 = jnp.float32
BF16 = jnp.bfloat16
NN = ((1,), (0,))
NT = ((1,), (1,))
TN = ((0,), (0,))
STATE = 80
COST = 0.2 * 1.15e9
VMEM = pl.BlockSpec(memory_space=pltpu.VMEM)
SMEM = pl.BlockSpec(memory_space=pltpu.SMEM)
ANY = pl.BlockSpec(memory_space=pl.ANY)


def dot(left, right, dims=NN):
    return lax.dot_general(left, right, (dims, ((), ())), preferred_element_type=F32)


def call(body, outs, specs, scratch=(), limit=6, after=(), cost=0):
    n = len(specs)

    def waiting_body(*refs):
        body(*refs[:n], *refs[n + len(after):])

    return lambda *operands: pl.pallas_call(
        waiting_body,
        out_shape=outs,
        in_specs=list(specs) + [ANY] * len(after),
        out_specs=jax.tree.map(lambda _: VMEM, outs),
        scratch_shapes=scratch,
        cost_estimate=pl.CostEstimate(flops=1 + int(cost * COST), bytes_accessed=1, transcendentals=0),
        compiler_params=pltpu.CompilerParams(vmem_limit_bytes=limit << 20),
    )(*operands, *after)


def shaped(shape, dtype):
    return jax.ShapeDtypeStruct(shape, dtype)


class Places:
    def __init__(self, dp, tensor):
        self.dp, self.tensor = dp, tensor
        self.row = lax.axis_index("dp")
        self.z = lax.axis_index("tensor")
        self.piece = self.row & 7

    def swap(self, value, mask):
        return lax.ppermute(value, "dp", [(d, d ^ mask) for d in range(self.dp)])

    def turn(self, value, step):
        size = self.tensor
        return lax.ppermute(value, "tensor", [(k, (k + step) % size) for k in range(size)])

    def onward(self, value, step):
        size = self.tensor
        pairs = [(k, k + step) for k in range(size) if 0 <= k + step < size]
        return lax.ppermute(value, "tensor", pairs)


CORE, X, Y = 1, 2, 4
BUFFERS = ((0, (0, 2)), (0, (4, 6)), (0, (1, 3)), (0, (5, 7)), (2, (0, 4)), (2, (2, 6)), (2, (1, 5)), (2, (3, 7)))


def stacked(*groups, after=()):
    sizes = [len(group) for group in groups]

    def body(*refs):
        sources, targets = list(refs[:sum(sizes)]), refs[sum(sizes):]
        for size, target in zip(sizes, targets, strict=True):
            for k in range(size):
                target[k] = sources.pop(0)[...]

    outs = tuple(shaped((len(group),) + group[0].shape, group[0].dtype) for group in groups)
    flat = [value for group in groups for value in group]
    return call(body, outs, [VMEM] * len(flat), after=after)(*flat)


def mix_pieces_kernel(first, second, third, fourth, a, b, bias_qkv, bias_in):
    rows, wide = a.shape[1], bias_qkv.shape[2]
    for j, part in enumerate((first, second, third, fourth)):
        (a, b)[j // 2][j % 2] = part[0:rows]
        extra = part[rows:].astype(F32)
        bias_qkv[j] = extra[0:1, :wide]
        bias_in[j] = extra[1:2]


def swap_halves(places, a, b):
    return places.swap(a, X), places.swap(b, Y)


def gather_rest(places, a, b, a2, b2):
    near, far = stacked((a, b)), stacked((a2, b2))
    return a, a2, b, b2, places.swap(near[0], CORE), places.swap(far[0], CORE)


def start_placing(piece, buffers, targets, sems):
    copies = []
    a, a2, b, b2, near, far = buffers
    buffers = (a, a2, near.at[0], far.at[0], b, b2, near.at[1], far.at[1])
    for buffer, (shard, pieces) in zip(buffers, BUFFERS, strict=True):
        for k, other in enumerate(pieces):
            for at, target, first_row, rows in targets:
                spot = pl.multiple_of(first_row + (piece ^ other) * rows, 8)
                copies.append(pltpu.make_async_copy(
                    buffer.at[k, :, at:at + rows, :],
                    target.at[shard:shard + 2, pl.ds(spot, rows), :],
                    sems.at[len(copies)],
                ))
    for copy in copies:
        copy.start()
    half = len(copies) // 2
    return copies[:half], copies[half:]


def wait_all(copies):
    for copy in copies:
        copy.wait()


def doubled(part):
    return jnp.concatenate([part, part], axis=1)


def with_one(value):
    lanes = lax.broadcasted_iota(jnp.int32, (value.shape[0], 2 * HEAD), 1)
    return jnp.where(lanes < HEAD, doubled(value.astype(F32)), (lanes == HEAD).astype(F32)).astype(BF16)


def head_parts(mixed_ref, shard, head):
    at = head * 3 * HEAD
    return tuple(mixed_ref[shard, :, at + t * HEAD:at + (t + 1) * HEAD] for t in range(3))


def causal_blocks(count):
    half = count // 2
    return ((0, half, 0, half), (half, count, 0, count))


def mix_kernel(info, tokens, bias, key_table, *refs):
    buffers, (mixed_out, state_out, weight), sems = refs[:6], refs[6:9], refs[9]
    wide = mixed_out.shape[2]
    tall = weight.shape[1] - wide
    halves = start_placing(
        info[0], buffers, ((0, weight, 0, wide // 8), (wide // 8, weight, wide, tall // 8)), sems)

    def shard_step(j, carry):
        mixed = dot(tokens[...], weight[j, 0:wide], NT) + bias[j]
        lanes = lax.broadcasted_iota(jnp.int32, mixed.shape, 1)
        mixed_out[j] = jnp.where(lanes % 192 >= 128, mixed, jnp.maximum(mixed, 0.0)).astype(BF16)
        for h in range(3):
            _, key, value = head_parts(mixed_out, j, h)
            feats = (doubled(key).astype(F32) * key_table[...]).astype(BF16)
            state_out[j, h] = dot(with_one(value), feats, TN)[:STATE].astype(BF16)
        return carry

    for k, half in enumerate(halves):
        wait_all(half)
        lax.fori_loop(2 * k, 2 * k + 2, shard_step, 0)


def local_kernel(mixed, mask, sums_out):
    def shard_step(j, carry):
        for h in range(3):
            query, key, value = head_parts(mixed, j, h)
            value = with_one(value)
            for r0, r1, c0, c1 in causal_blocks(mask.shape[0]):
                scores = (dot(query[r0:r1], key[c0:c1], NT) * mask[r0:r1, c0:c1]).astype(BF16)
                sums_out[j, h, r0:r1] = dot(scores, value[c0:c1])
        return carry

    lax.fori_loop(0, mixed.shape[0], shard_step, 0)


def norm_parts(rows_in):
    centred = rows_in - jnp.mean(rows_in, axis=-1, keepdims=True)
    spread = jnp.mean(centred * centred, axis=-1, keepdims=True)
    scale = lax.rsqrt(spread + 1e-05)
    return centred * scale, scale


def norm_back(grad, normed, scale, gain):
    e = grad * gain
    d_rows = scale * (
        e
        - jnp.mean(e, axis=-1, keepdims=True)
        - normed * jnp.mean(e * normed, axis=-1, keepdims=True)
    )
    return d_rows, jnp.sum(grad * normed, axis=0, keepdims=True), jnp.sum(grad, axis=0, keepdims=True)


def join_kernel(info, sums, arrived1, arrived2, arrived3, mixed, query_table, tokens, weight, b_out, gain, shift,
                attended, carried, dens, first, normed_out, scale_out):
    shards = mixed.shape[0]
    for j in range(shards):
        total = None
        for step, arrived in enumerate((arrived1, arrived2, arrived3), 1):
            linked = info[step].astype(F32) * arrived[(j - step) % shards].astype(F32)
            total = linked if total is None else total + linked
        carried[j] = total.astype(BF16)

    def shard_step(j, branch):
        lanes = lax.broadcasted_iota(jnp.int32, (tokens.shape[0], 128), 1)
        kept = jnp.zeros((tokens.shape[0], 128), F32)
        for h in range(3):
            query = head_parts(mixed, j, h)[0]
            feats = (doubled(query).astype(F32) * query_table[...]).astype(BF16)
            total = sums[j, h][:, :STATE] + dot(feats, carried[j, h], NT)
            den = total[:, HEAD:HEAD + 1]
            inverse = 1.0 / jnp.maximum(den, 1.0)
            attended[j, :, h * HEAD:(h + 1) * HEAD] = (total[:, :HEAD] * inverse).astype(BF16)
            kept = jnp.where(lanes == h, inverse, kept)
            kept = jnp.where(lanes == 8 + h, jnp.where(den > 1.0, inverse, 0.0), kept)
        dens[j] = kept
        return branch + dot(attended[j], weight[j, weight.shape[1] - 192:])

    branch = lax.fori_loop(0, shards, shard_step, jnp.zeros(tokens.shape, F32))
    normed, scale = norm_parts(tokens[...].astype(F32) + branch + b_out[...])
    normed_out[...] = normed
    scale_out[...] = jnp.broadcast_to(scale, scale_out.shape)
    first[...] = (normed * gain[...] + shift[...]).astype(BF16)


def gelu_parts(v):
    k = math.sqrt(2 / math.pi)
    square = v * v
    t = jnp.tanh(v * (k + k * 0.044715 * square))
    half = 0.5 * v
    bent = half * t
    slope = (0.5 + 0.5 * t) + (half - bent * t) * (k + 3 * k * 0.044715 * square)
    return half + bent, slope


def rows_ordered(turned, piece, order):
    rows = turned.shape[0] // 8
    return jnp.concatenate(
        [turned[pl.ds(pl.multiple_of((piece ^ other) * rows, rows), rows), :] for other in order], axis=0)


ROUTES = ((0, 4, 2, 6), (0, 2, 4, 6))


def order_rows(ordered, turned, piece):
    for route, order in enumerate(ROUTES):
        for sends in range(2):
            ordered[2 * route + sends] = rows_ordered(turned, piece, tuple(other + sends for other in order))


def columns(j, width):
    return pl.ds(pl.multiple_of(j * width, 128), width)


def feed_kernel(info, first, bias, b_two, gain, shift, cotangent, *refs):
    buffers = refs[:6]
    slope, block_out, d_second_out, d_r2_out, vectors, *grads = refs[6:13]
    w_in, w_two, active, turned, ordered, total, sems = refs[13:]
    shards, width = w_in.shape[0], w_in.shape[2]
    rows = width // 8
    halves = start_placing(info[0], buffers, ((0, w_in, 0, rows), (rows, w_two, 0, rows)), sems)
    total[...] = jnp.broadcast_to(b_two[...], total.shape)

    def forward_step(j, carry):
        half = first.shape[0] // 2
        spans = slice(0, half), slice(half, 2 * half)
        hidden = [dot(first[span], w_in[j]) + bias[j] for span in spans]
        for span, part in zip(spans, hidden, strict=True):
            act, bend = gelu_parts(part)
            act = act.astype(BF16)
            active[j, span] = act
            slope[j, span] = bend.astype(BF16)
            total[span] += dot(act, w_two[j])
        return carry

    for k, half in enumerate(halves):
        wait_all(half)
        lax.fori_loop(2 * k, 2 * k + 2, forward_step, 0)
    normed, scale = norm_parts(first[...].astype(F32) + total[...])
    block_out[...] = (normed * gain[...] + shift[...]).astype(BF16)
    d_r2, d_gain, d_shift = norm_back(cotangent[...].astype(F32), normed, scale, gain[...])
    d_r2_out[...] = d_r2
    d_second = d_r2.astype(BF16)
    d_second_out[...] = d_second
    turned[...] = d_second.T
    vectors[0:1] = d_gain
    vectors[1:2] = d_shift
    vectors[2:3] = jnp.sum(d_second.astype(F32), axis=0, keepdims=True)
    vectors[3:] = jnp.zeros((5, vectors.shape[1]), F32)
    order_rows(ordered, turned, info[0])

    def grad_step(j, carry):
        for sends in range(2):
            grads[sends][:, columns(j, width)] = dot(ordered[2 * (j // 2) + sends], active[j]).astype(BF16)
        return carry

    lax.fori_loop(0, shards, grad_step, 0)


def feed_back_kernel(info, first, d_second, slope, *refs):
    buffers = refs[:6]
    d_hidden, d_bias, *grads = refs[6:10]
    w_two, turned, ordered, sems = refs[10:]
    shards, width = w_two.shape[0], w_two.shape[2]
    rows = width // 8
    halves = start_placing(info[0], buffers, ((rows, w_two, 0, rows),), sems)
    turned[...] = first[...].T
    order_rows(ordered, turned, info[0])

    def step(j, carry):
        d_active = dot(d_second[...], w_two[j], NT)
        d_h = (d_active * slope[j].astype(F32)).astype(BF16)
        d_hidden[j] = d_h
        d_bias[j] = jnp.broadcast_to(jnp.sum(d_h.astype(F32), axis=0, keepdims=True), d_bias.shape[1:])
        for sends in range(2):
            grads[sends][:, columns(j, width)] = dot(ordered[2 * (j // 2) + sends], d_hidden[j]).astype(BF16)
        return carry

    for k, half in enumerate(halves):
        wait_all(half)
        lax.fori_loop(2 * k, 2 * k + 2, step, 0)


def first_back_kernel(info, d_hidden, d_r2, normed, scale, gain, *refs):
    buffers = refs[:6]
    d_r1_out, d_branch_out, vectors = refs[6:9]
    w_in, total, sems = refs[9:]
    rows = w_in.shape[1] // 8
    halves = start_placing(info[0], buffers, ((0, w_in, 0, rows),), sems)
    total[...] = d_r2[...]

    def first_step(j, carry):
        total[...] += dot(d_hidden[j], w_in[j], NT)
        return carry

    for k, half in enumerate(halves):
        wait_all(half)
        lax.fori_loop(2 * k, 2 * k + 2, first_step, 0)
    d_r1, d_gain, d_shift = norm_back(total[...], normed[...], scale[:, 0:1], gain[...])
    d_r1_out[...] = d_r1
    d_branch = d_r1.astype(BF16)
    d_branch_out[...] = d_branch
    vectors[0:1] = d_gain
    vectors[1:2] = d_shift
    vectors[2:3] = jnp.sum(d_branch.astype(F32), axis=0, keepdims=True)
    vectors[3:] = jnp.zeros((5, vectors.shape[1]), F32)


def heads_back_kernel(d_branch, weight, attended, dens, mixed, query_table, d_sums, d_carried):
    def shard_step(j, carry):
        g_all = dot(d_branch[...], weight[j, weight.shape[1] - 192:], NT)
        lanes = lax.broadcasted_iota(jnp.int32, (d_branch.shape[0], 128), 1)
        for h in range(3):
            g = g_all[:, h * HEAD:(h + 1) * HEAD]
            o = attended[j, :, h * HEAD:(h + 1) * HEAD].astype(F32)
            inverse, inverse_if = dens[j, :, h:h + 1], dens[j, :, 8 + h:9 + h]
            d_den = -jnp.sum(g * o, axis=-1, keepdims=True) * inverse_if
            d_num = doubled(g * inverse)
            both = jnp.where(lanes < HEAD, d_num, jnp.where(lanes == HEAD, d_den, 0.0)).astype(BF16)
            d_sums[j, h] = both
            query = head_parts(mixed, j, h)[0]
            feats = (doubled(query).astype(F32) * query_table[...]).astype(BF16)
            d_carried[j, h] = dot(both, feats, TN)[:STATE].astype(BF16)
        return carry

    lax.fori_loop(0, mixed.shape[0], shard_step, 0)


def local_back_kernel(mixed, d_sums, mask, mask_t, d_mixed):
    def shard_step(j, carry):
        for h in range(3):
            query, key, value = head_parts(mixed, j, h)
            value = with_one(value)
            grad = d_sums[j, h]
            at = h * 3 * HEAD
            for r0, r1, c0, c1 in causal_blocks(mask.shape[0]):
                d_scores = (dot(grad[r0:r1], value[c0:c1], NT) * mask[r0:r1, c0:c1]).astype(BF16)
                d_mixed[j, r0:r1, at:at + HEAD] = dot(d_scores, key[c0:c1])
            half = mask.shape[0] // 2
            for c0, c1, r0 in ((0, half, 0), (half, 2 * half, half)):
                turned = mask_t[c0:c1, r0:]
                d_scores = (dot(value[c0:c1], grad[r0:], NT) * turned).astype(BF16)
                d_mixed[j, c0:c1, at + HEAD:at + 2 * HEAD] = dot(d_scores, query[r0:])
                scores = (dot(key[c0:c1], query[r0:], NT) * turned).astype(BF16)
                d_mixed[j, c0:c1, at + 2 * HEAD:at + 3 * HEAD] = dot(scores, grad[r0:])[:, :HEAD]
        return carry

    lax.fori_loop(0, mixed.shape[0], shard_step, 0)


def mix_back_kernel(base, info, mixed, local, d_sums, carried, arrived1, arrived2, arrived3, query_table, key_table,
                    tokens, attended, d_branch, *refs):
    last = base > 0
    sources, refs = (refs[:4], refs[4:]) if last else ((), refs)
    d_mixed, d_bias, *grads = refs[:4]
    turned, turned_branch, state, held, middles = refs[-5:]
    shards, wide = mixed.shape[0], mixed.shape[2]
    width = d_mixed.shape[2]
    turned[...] = tokens[...].T
    turned_branch[...] = d_branch[...].T
    for k in range(2):
        total = None
        for step, arrived in enumerate((arrived1, arrived2, arrived3), 1):
            linked = info[3 + step].astype(F32) * arrived[(base + k + step) % shards].astype(F32)
            total = linked if total is None else total + linked
        state[k] = total.astype(BF16)

    def folded(both):
        return both[:, :HEAD] + both[:, HEAD:]

    def shard_step(k, carry):
        j = base + k
        parts = []
        for h in range(3):
            query, key, value = head_parts(mixed, j, h)
            at = h * 3 * HEAD
            spans = [slice(at + t * HEAD, at + (t + 1) * HEAD) for t in range(3)]
            d_query = folded(dot(d_sums[j, h][:, :STATE], carried[j, h]) * query_table[...])
            d_query = jnp.where(query.astype(F32) > 0, local[j, :, spans[0]] + d_query, 0.0)
            d_key = folded(dot(with_one(value)[:, :STATE], state[k, h]) * key_table[...])
            d_key = jnp.where(key.astype(F32) > 0, local[j, :, spans[1]] + d_key, 0.0)
            feats = (doubled(key).astype(F32) * key_table[...]).astype(BF16)
            d_value = local[j, :, spans[2]] + dot(feats, state[k, h], NT)[:, :HEAD]
            parts += [d_query, d_key, d_value]
        whole = jnp.concatenate(parts + [attended[j].astype(F32)], axis=1).astype(BF16)
        d_mixed[k] = whole
        middles[k] = jnp.concatenate([parts[-1], attended[j][:, :HEAD].astype(F32)], axis=1)
        d_bias[k] = jnp.broadcast_to(jnp.sum(d_mixed[k].astype(F32), axis=0, keepdims=True), d_bias.shape[1:])
        return carry

    lax.fori_loop(0, 2, shard_step, 0)
    rows = grads[0].shape[0]
    low = wide // 128 * 128
    for k in range(2):
        lanes = lax.broadcasted_iota(jnp.int32, (d_mixed.shape[1], 128), 1)
        middle = middles[k]
        left_side = jnp.where(lanes < HEAD, middle, 0.0).astype(BF16)
        right_side = jnp.where(lanes < HEAD, 0.0, middle).astype(BF16)
        left_side = jnp.concatenate([d_mixed[k][:, :low], left_side], axis=1)
        right_side = jnp.concatenate([right_side, d_mixed[k][:, low + 128:]], axis=1)
        for sends in (1, 0):
            out, at = grads[sends], k * width
            order = tuple(other + sends for other in ROUTES[k])
            left = dot(rows_ordered(turned, info[0], order), left_side)
            right = dot(rows_ordered(turned_branch, info[0], order), right_side)
            out[0:rows, at:at + low] = left[:, :low].astype(BF16)
            out[0:rows, at + low:at + low + 128] = (left[:, low:] + right[:, :128]).astype(BF16)
            out[0:rows, at + low + 128:at + width] = right[:, 128:].astype(BF16)
    if last:
        one, two, bias_in, bias_first = sources
        vectors = refs[4]
        held[0:3] = one[0:3]
        held[3:6] = two[0:3]
        for j in range(shards):
            held[6 + 2 * j:7 + 2 * j] = bias_first[j, 0:1] if j < 2 else d_bias[j - 2, 0:1]
            held[7 + 2 * j:8 + 2 * j] = bias_in[j, 0:1]
        held[14:16] = jnp.zeros((2, width), F32)
        low_rows = held[...].astype(BF16)
        vectors[...] = low_rows
        grads[1][rows:, 0:width] = low_rows[0:8]
        grads[1][rows:, width:] = low_rows[8:16]


def tokens_back_kernel(d_mixed_a, d_mixed_b, weight, d_r1, d_tokens):
    wide = weight.shape[1] - 192
    total = d_r1[...]
    for j in range(weight.shape[0]):
        d_mixed = (d_mixed_a, d_mixed_b)[j // 2]
        total = total + dot(d_mixed[j % 2][:, :wide], weight[j, 0:wide])
    d_tokens[...] = total.astype(BF16)


def later(values, others):
    return lax.optimization_barrier((values, others))[0]


def halves_like(rows, width, extra=0):
    keep, send = shaped((rows, width), F32), shaped((rows, width), BF16)
    return keep, send, keep, shaped((rows + extra, width), BF16)


def first_halves_kernel(keep, got, *outs):
    half, width = outs[0].shape
    for k in range(2):
        cols = slice(k * width, (k + 1) * width)
        outs[2 * k][...] = keep[0:half, cols].astype(F32) + got[0:half, cols].astype(F32)
        send = keep[half:2 * half, cols].astype(F32) + got[half:2 * half, cols].astype(F32)
        outs[2 * k + 1][0:half] = send.astype(BF16)


def first_pairs_kernel(keep_a, got_a, keep_b, got_b, mine, *outs):
    half, width = outs[0].shape[0] // 2, outs[0].shape[1]
    for k in range(2):
        cols = slice(k * width, (k + 1) * width)
        for t, (keep, got) in enumerate(((keep_a, got_a), (keep_b, got_b))):
            spots = slice(t * half, (t + 1) * half)
            outs[2 * k][spots] = keep[0:half, cols].astype(F32) + got[0:half, cols].astype(F32)
            send = keep[half:2 * half, cols].astype(F32) + got[half:2 * half, cols].astype(F32)
            outs[2 * k + 1][spots] = send.astype(BF16)
        rows = mine[8 * k:8 * k + 8].astype(F32) + got_b[2 * half:, cols].astype(F32)
        outs[4][8 * k:8 * k + 8] = rows.astype(BF16)
        outs[3][2 * half + 8 * k:2 * half + 8 * k + 8] = rows.astype(BF16)


def next_halves_kernel(keep0, keep1, got0, got1, *outs):
    half = outs[0].shape[0]
    for k, (keep, got) in enumerate(((keep0, got0), (keep1, got1))):
        outs[2 * k][...] = keep[0:half] + got[0:half].astype(F32)
        outs[2 * k + 1][...] = (keep[half:] + got[half:].astype(F32)).astype(BF16)


def ends_kernel(keep0, keep1, got0, got1, end0, end1):
    end0[...] = (keep0[...] + got0[...].astype(F32)).astype(BF16)
    end1[...] = (keep1[...] + got1[...].astype(F32)).astype(BF16)


def feed_last_kernel(keep0, keep1, got0, got1, two0, two1, *outs):
    rows, width = outs[0].shape[0] // 2, outs[0].shape[1]
    for j, out in enumerate(outs):
        keep, got, two = (keep0, got0, two0) if j < 2 else (keep1, got1, two1)
        cols = slice(j % 2 * width, (j % 2 + 1) * width)
        out[0:rows] = (keep[:, cols] + got[:, cols].astype(F32)).astype(BF16)
        out[rows:] = two[:, cols]


def mix_next_kernel(keep0, keep1, got0, got1, mine, *outs):
    half = outs[0].shape[0] // 2
    for k, (keep, got) in enumerate(((keep0, got0), (keep1, got1))):
        for t in range(2):
            at = 2 * t * half
            spots = slice(t * half, (t + 1) * half)
            outs[2 * k][spots] = keep[at:at + half] + got[at:at + half].astype(F32)
            send = keep[at + half:at + 2 * half] + got[at + half:at + 2 * half].astype(F32)
            outs[2 * k + 1][spots] = send.astype(BF16)
    rows = (mine[...].astype(F32) + got1[4 * half:].astype(F32)).astype(BF16)
    outs[4][...] = rows
    outs[3][2 * half:] = rows


def mix_last_kernel(keep0, keep1, got0, got1, mine, *outs):
    half = keep0.shape[0] // 2
    rows = (mine[...].astype(F32) + got1[2 * half:].astype(F32)).astype(BF16)
    for j, out in enumerate(outs):
        keep, got = (keep0, got0) if j % 2 == 0 else (keep1, got1)
        spots = slice(j // 2 * half, (j // 2 + 1) * half)
        out[0:half] = (keep[spots] + got[spots].astype(F32)).astype(BF16)
        out[half:half + 6] = rows[0:6]
        out[half + 6:half + 8] = rows[6 + 2 * j:8 + 2 * j]


def swap_all(places, values, masks):
    return [places.swap(value, mask) for value, mask in zip(values, masks, strict=True)]


def turn_back(places, parts):
    return [parts[0]] + [places.turn(parts[s], -s) for s in range(1, places.tensor)]


def pair_sum(mine, other):
    return (mine.astype(F32) + other.astype(F32)).astype(BF16)


def over_groups(places, total):
    mask = 8
    while mask < places.dp:
        total = total + places.swap(total, mask)
        mask *= 2
    return total


def added(places, values, rows, after=()):
    kind = BF16 if places.dp == 8 else F32

    def body(*refs):
        total = refs[0][0:rows].astype(F32)
        for other in refs[1:-1]:
            total = total + other[0:rows].astype(F32)
        refs[-1][...] = total.astype(kind)

    total = call(body, shaped((rows, values[0].shape[1]), kind), [VMEM] * len(values), after=after)(*values)
    return over_groups(places, total).astype(BF16)


def spread_chips(places, own):
    return [own, places.swap(own, X), places.swap(own, Y), places.swap(own, X + Y)]


def spread_cores(places, four):
    return list(four) + [places.swap(stacked(four)[0], CORE)]


def place_rows(piece, pieces, targets):
    for k in range(8):
        source = pieces[k // 2] if k % 2 == 0 else pieces[4].at[k // 2]
        for t, target in enumerate(targets):
            rows = target.shape[0] // 8
            spot = pl.multiple_of((piece ^ k) * rows, rows)
            target[pl.ds(spot, rows), :] = source[t * rows:(t + 1) * rows].astype(F32)


def finish_feed_kernel(info, own, x, y, xy, core, d_in, d_two, held):
    place_rows(info[0], (own, x, y, xy, core), (d_in, held))
    d_two[...] = held[...].T


def finish_mix_kernel(info, own, x, y, xy, core, d_qkv, d_out, held):
    place_rows(info[0], (own, x, y, xy, core), (held,))
    turned = held[...].T
    d_qkv[...] = turned[0:d_qkv.shape[0]]
    d_out[...] = turned[d_qkv.shape[0]:]


def doc_tables(starts_row, base, count):
    spots = base + jnp.arange(count, dtype=jnp.int32)
    started = (spots[:, None] >= starts_row[None, :]).astype(jnp.int32)
    doc_ids = jnp.sum(started, axis=1) - 1
    onehot = (doc_ids[:, None] == jnp.arange(DOCS, dtype=jnp.int32)[None, :]).astype(jnp.int32)
    finish = jnp.concatenate([starts_row[1:], jnp.full((1,), ROW_LEN, jnp.int32)])
    own_start = jnp.sum(onehot * starts_row[None, :], axis=1)
    own_len = jnp.sum(onehot * (finish - starts_row)[None, :], axis=1)
    angles = 0.5 * math.pi * (spots - own_start).astype(F32) / own_len.astype(F32)
    return angles, doc_ids


def doc_at(starts_row, spot):
    return jnp.sum((spot >= starts_row).astype(jnp.int32)) - 1


def on_device(dp, tensor, tokens, starts, w_qkv, b_qkv, w_out, b_out, gain_one, shift_one, w_in, b_in,
              w_two, b_two, gain_two, shift_two, cotangent):
    places = Places(dp, tensor)
    count, width = tokens.shape
    piece = places.piece
    line = lambda a: a.astype(F32).reshape(1, -1)
    sems = lambda n: pltpu.SemaphoreType.DMA((n,))

    def own_rows(weight):
        rows = weight.shape[0] // 8
        return lax.dynamic_slice_in_dim(weight, piece * rows, rows, 0)

    rows = width // 8
    wide = w_qkv.shape[1]
    bias_rows = jnp.pad(b_qkv.reshape(1, wide), ((0, 7), (0, width - wide))) + jnp.pad(b_in.reshape(1, width), ((1, 6), (0, 0)))
    mix_piece = jnp.concatenate([own_rows(w_qkv.T), own_rows(w_out), bias_rows])
    feed_piece = jnp.concatenate([own_rows(w_in), own_rows(w_two)])
    mix_parts = [mix_piece] + [places.turn(mix_piece, s) for s in range(1, tensor)]
    feed_parts = [feed_piece] + [places.turn(feed_piece, s) for s in range(1, tensor - 1)]
    feed_parts.append(places.turn(later(feed_piece, mix_parts), tensor - 1))
    pair = shaped((2, rows, width), BF16)
    mix_a, mix_b, bias_qkv, bias_in = call(
        mix_pieces_kernel, (pair, pair, shaped((tensor, 1, wide), F32), shaped((tensor, 1, width), F32)), [VMEM] * 4,
    )(*mix_parts)
    near_x, near_y = swap_halves(places, mix_a, mix_b)
    mix_ax, mix_by = stacked((mix_a, near_x), (mix_b, near_y))
    mix_buffers = gather_rest(places, mix_ax, mix_by, places.swap(mix_ax, Y), places.swap(mix_by, X))
    feed_a, feed_b = stacked(feed_parts[:2], feed_parts[2:], after=(mix_ax, mix_by))
    near_x, near_y = swap_halves(places, feed_a, feed_b)

    row = starts[0]
    base = places.z * count
    angles, docs = doc_tables(row, base, count)
    first_doc, last_doc = doc_at(row, base), doc_at(row, base + count - 1)
    links = [doc_at(row, base - (s - 1) * count - 1) == first_doc for s in range(1, tensor)]
    links += [doc_at(row, base + s * count) == last_doc for s in range(1, tensor)]
    info = jnp.stack([piece] + [link.astype(jnp.int32) for link in links] + [piece])
    spot = jnp.arange(count)
    cosine, sines = jnp.cos(angles), jnp.sin(angles)
    turn = cosine[:, None] * cosine[None, :] + sines[:, None] * sines[None, :]
    same = docs[:, None] == docs[None, :]
    mask = jnp.where(same & (spot[:, None] >= spot[None, :]), turn, 0.0)
    mask_t = jnp.where(same & (spot[:, None] <= spot[None, :]), turn, 0.0)
    lanes = jnp.arange(2 * HEAD)[None, :]
    table = jnp.where(lanes < HEAD, cosine[:, None], sines[:, None])
    query_table = jnp.where((docs == first_doc)[:, None], table, 0.0)
    key_table = jnp.where((docs == last_doc)[:, None], table, 0.0)

    states = shaped((tensor, 3, STATE, 2 * HEAD), BF16)
    mixed, state, mix_weight = call(
        mix_kernel,
        (shaped((tensor, count, wide), BF16), states, shaped((tensor, width, width), BF16)),
        [SMEM, VMEM, VMEM, VMEM] + [ANY] * 6, [sems(32)], limit=9, cost=8,
    )(info, tokens, bias_qkv, key_table, *mix_buffers)
    per_head = shaped((tensor, 3, count, 2 * HEAD), F32)
    arrived = [places.onward(state, s) for s in range(1, tensor)]
    per_head = shaped((tensor, 3, count, 2 * HEAD), F32)
    feed_ax, feed_by = stacked((feed_a, near_x), (feed_b, near_y), after=(state,))
    near_sums = call(local_kernel, per_head, [VMEM, VMEM], after=(feed_ax, feed_by), limit=6, cost=7)(mixed, mask)
    feed_far = places.swap(feed_ax, Y), places.swap(feed_by, X)
    attended, carried, dens, first, normed, scale = call(
        join_kernel,
        (shaped((tensor, count, 192), BF16), states, shaped((tensor, count, 128), F32), shaped((count, width), BF16),
         shaped((count, width), F32), shaped((count, 128), F32)),
        [SMEM] + [VMEM] * 11, limit=18, cost=100,
    )(info, near_sums, *arrived, mixed, query_table, tokens, mix_weight, line(b_out), line(gain_one), line(shift_one))
    feed_buffers = gather_rest(places, *later((feed_ax, feed_by, *feed_far), first))
    hidden_like = shaped((tensor, count, width), BF16)
    vectors = shaped((8, width), F32)
    grad_like = shaped((4 * rows, tensor * width), BF16)
    square = pltpu.VMEM((tensor, width, width), BF16)
    turned = pltpu.VMEM((width, count), BF16)
    ordered = pltpu.VMEM((4, 4 * rows, count), BF16)
    total_scratch = pltpu.VMEM((count, width), F32)
    slope, block_out, d_second, d_r2, vectors_two, two_keep, two_send = call(
        feed_kernel,
        (hidden_like, shaped((count, width), BF16), shaped((count, width), BF16),
         shaped((count, width), F32), vectors, grad_like, grad_like),
        [SMEM] + [VMEM] * 6 + [ANY] * 6, [square, square, pltpu.VMEM(hidden_like.shape, BF16), turned, ordered, total_scratch, sems(32)], limit=31, cost=19,
    )(info, first, bias_in, line(b_two), line(gain_two), line(shift_two), cotangent, *feed_buffers)

    got = places.swap(two_send, CORE)
    d_hidden, d_bias_in, in_keep, in_send = call(
        feed_back_kernel, (hidden_like, shaped((tensor, 8, width), F32), grad_like, grad_like),
        [SMEM] + [VMEM] * 3 + [ANY] * 6, [square, turned, ordered, sems(16)], limit=18, cost=14,
    )(info, first, d_second, slope, *feed_buffers)
    wide_halves = halves_like(2 * rows, 2 * width)
    keep0, send0, keep1, send1 = call(first_halves_kernel, wide_halves, [VMEM] * 2, after=(in_send,))(two_keep, got)
    got_two, got_in = swap_all(places, (send0, send1), (X, Y)), places.swap(in_send, CORE)
    d_r1, d_branch, vectors_one = call(
        first_back_kernel,
        (shaped((count, width), F32), shaped((count, width), BF16), vectors),
        [SMEM] + [VMEM] * 5 + [ANY] * 6, [square, total_scratch, sems(16)], after=(send0, send1), limit=17, cost=11,
    )(info, d_hidden, d_r2, normed, scale, line(gain_one), *feed_buffers)
    keep0, send0, keep1, send1 = call(
        next_halves_kernel, halves_like(rows, 2 * width), [VMEM] * 4, after=(d_branch,))(keep0, keep1, *got_two)
    got_two = swap_all(places, (send0, send1), (Y, X))
    in0, in_send0, in1, in_send1 = call(
        first_halves_kernel, wide_halves, [VMEM] * 2, after=(send0, send1))(in_keep, got_in)
    got_in = swap_all(places, (in_send0, in_send1), (X, Y))
    d_sums, d_carried = call(
        heads_back_kernel, (shaped((tensor, 3, count, 2 * HEAD), BF16), states), [VMEM] * 6,
        after=(in_send0, in_send1), limit=9, cost=11,
    )(d_branch, mix_weight, attended, dens, mixed, query_table)
    arrived_back = [places.onward(d_carried, -s) for s in range(1, tensor)]
    end = shaped((rows, 2 * width), BF16)
    two_ends = call(ends_kernel, (end, end), [VMEM] * 4, after=(d_carried,))(keep0, keep1, *got_two)
    in0, in_send0, in1, in_send1 = call(
        next_halves_kernel, halves_like(rows, 2 * width), [VMEM] * 4, after=two_ends)(in0, in1, *got_in)
    got_in = swap_all(places, (in_send0, in_send1), (Y, X))
    local = call(
        local_back_kernel, shaped((tensor, count, wide), F32), [VMEM] * 4, after=(in_send0, in_send1), limit=9, cost=15,
    )(mixed, d_sums, mask, mask_t)
    feed_last = call(
        feed_last_kernel, (shaped((2 * rows, width), BF16),) * tensor, [VMEM] * 6, after=(local, *arrived_back),
    )(in0, in1, *got_in, *two_ends)
    feed_own = turn_back(places, feed_last)
    mix_like = shaped((4 * rows, 2 * width), BF16)
    mix_outs = (shaped((2, count, width), BF16), shaped((2, 8, width), F32), mix_like)
    mix_scratch = [turned, turned, pltpu.VMEM((2, 3, STATE, 2 * HEAD), BF16), pltpu.VMEM((16, width), F32), pltpu.VMEM((2, count, 128), F32)]
    mix_inputs = (info, mixed, local, d_sums, carried, *arrived_back, query_table, key_table, tokens, attended, d_branch)
    d_mixed_a, d_bias_a, keep_a, send_a = call(
        functools.partial(mix_back_kernel, 0), mix_outs + (mix_like,), [SMEM] + [VMEM] * 12, mix_scratch,
        after=feed_last, limit=17, cost=11,
    )(*mix_inputs)
    got_a = places.swap(send_a, CORE)
    d_mixed_b, d_bias_b, keep_b, send_b, vector_rows = call(
        functools.partial(mix_back_kernel, 2),
        mix_outs + (shaped((4 * rows + 8, 2 * width), BF16), shaped((16, width), BF16)), [SMEM] + [VMEM] * 16,
        mix_scratch, limit=17, cost=11,
    )(*mix_inputs, vectors_one, vectors_two, d_bias_in, d_bias_a)
    feed_rows = added(places, feed_own, 2 * rows, after=(d_mixed_b,))
    got_a, got_b = later(got_a, feed_rows), places.swap(later(send_b, feed_rows), CORE)
    row_like = shaped((16, width), BF16)
    keep0, send0, keep1, send1, vector_rows = call(
        first_pairs_kernel, halves_like(4 * rows, width, 16) + (row_like,), [VMEM] * 5,
    )(keep_a, got_a, keep_b, got_b, vector_rows)
    got = swap_all(places, (send0, send1), (X, Y))
    d_tokens = call(
        tokens_back_kernel, shaped((count, width), BF16), [VMEM] * 4, after=(send0, send1), limit=9, cost=6,
    )(d_mixed_a, d_mixed_b, mix_weight, d_r1)
    keep0, send0, keep1, send1, vector_rows = call(
        mix_next_kernel, halves_like(2 * rows, width, 16) + (row_like,), [VMEM] * 5, after=(d_tokens,),
    )(keep0, keep1, *got, vector_rows)
    got = swap_all(places, (send0, send1), (Y, X))
    feed_low = later(feed_rows, (send0, send1))
    feed_x, feed_y = swap_all(places, (feed_low, feed_low), (X, Y))
    mix_last = call(
        mix_last_kernel, (shaped((rows + 8, width), BF16),) * tensor, [VMEM] * 5,
    )(keep0, keep1, *got, vector_rows)
    mix_own = turn_back(places, mix_last)
    feed_x, feed_y = later((feed_x, feed_y), mix_own[1])
    feed_all = spread_cores(places, [feed_low, feed_x, feed_y, places.swap(feed_x, Y)])

    held = pltpu.VMEM((width, width), F32)
    d_w_in, d_w_two = call(
        finish_feed_kernel, (shaped((width, width), F32),) * 2, [SMEM] + [VMEM] * 5, [held], limit=10, cost=4,
    )(info, *feed_all)
    mix_rows = added(places, mix_own, rows)
    mix_four = later(spread_chips(places, mix_rows), d_w_in)
    d_w_qkv, d_w_out = call(
        finish_mix_kernel, (shaped((wide, width), F32), shaped((192, width), F32)), [SMEM] + [VMEM] * 5, [held], limit=7, cost=3,
    )(info, *spread_cores(places, mix_four))

    ends = jnp.stack([part[rows:] for part in mix_own])
    ends = lax.dynamic_slice_in_dim(jnp.concatenate([ends, ends]), tensor - places.z, tensor, 0)
    summed = over_groups(places, jnp.sum(ends.astype(F32), axis=0))
    d_gain_one, d_shift_one, d_b_out, d_gain_two, d_shift_two, d_b_two = (summed[k] for k in range(6))
    d_b_qkv, d_b_in = summed[6, :wide], summed[7]
    return (block_out, d_tokens, d_w_qkv.T, d_b_qkv, d_w_out, d_b_out, d_gain_one, d_shift_one, d_w_in, d_b_in,
            d_w_two, d_b_two, d_gain_two, d_shift_two)


def solution(mesh):
    sizes = dict(mesh.shape)
    rows = P(("dp", "tensor"), None)
    wide, tall, cut, whole = P(None, "tensor"), P("tensor", None), P("tensor"), P()
    in_specs = (rows, P("dp", None), wide, cut, tall, whole, whole, whole, wide, cut, tall, whole, whole, whole, rows)
    out_specs = (rows, rows, wide, cut, tall, whole, whole, whole, wide, cut, tall, whole, whole, whole)
    return jax.shard_map(
        functools.partial(on_device, sizes["dp"], sizes["tensor"]),
        mesh=mesh, in_specs=in_specs, out_specs=out_specs, check_vma=False,
    )
```
